128 devices in a mesh: node: 4 (over z), band: 32 (over x, y, core).
Axes of the slice: x: 4, y: 4, z: 4, core: 2. Of those that a mesh axis runs over, the one named last changes fastest.
Arguments:
- state0: float32 [2, 1024, 4, 3, 512], P(None, 'band'), may hold values from -36 to 36
- iterate: float32 [4, 2, 1024, 4, 3, 512], P('node', None, 'band'), may hold values from -37.2 to 37.2
- legendre: bfloat16 [1024, 512, 512], P('band'), may hold values from -0.25 to 0.25
- lat_weight: float32 [512], replicated, may hold values from 0.25 to 1
- coriolis: float32 [2, 512], replicated, may hold values from -1.5 to 1.5
- damping: float32 [1024, 3, 512], P('band'), may hold values from 0.1 to 10
- quadrature: float32 [4, 4], replicated, may hold values from 0.02 to 0.25
Outputs:
- updated: float32 [4, 2, 1024, 4, 3, 512], P('node', None, 'band')
- sweep_change: float32 [3], replicated
The draws below stay inside these ranges and needn't reach their ends.
All inputs are finite; a program needn't handle non-finite values.
Results may differ from the reference program's by a relative error of at most 0.0017.
Values may be sent and summed in bfloat16 or wider, within the bound.
No kernel may reach another device: no remote copies, remote signals or barrier semaphores. Data moves between devices by JAX's collectives and lax.ppermute only.
A program may use at most 256 MiB of HBM per device.

```python
import math
import jax
import jax.numpy as jnp
from jax import lax

M = 1024
J = 512
NH = 512
ENS = 4
NLON = 2048
NODES = 4


def base_field(key):
    noise_key, row_key, col_key = jax.random.split(key, 3)
    shape = (2, M, ENS, 3, J)
    noise = jnp.clip(jax.random.normal(noise_key, shape, jnp.float32), -4.0, 4.0)
    low = math.log(0.3)
    high = math.log(3.0)
    rows = jnp.exp(jax.random.uniform(row_key, (1, M, 1, 3, 1), jnp.float32, low, high))
    cols = jnp.exp(jax.random.uniform(col_key, (1, 1, 1, 1, J), jnp.float32, low, high))
    return noise * rows * cols


def draw_state0(key, part):
    return base_field(jax.random.fold_in(key, 11)).astype(jnp.float32)


def draw_iterate(key, part):
    start = base_field(jax.random.fold_in(key, 11))
    noise = jnp.clip(jax.random.normal(jax.random.fold_in(key, 12), (NODES,) + start.shape, jnp.float32), -4.0, 4.0)
    return (start[None] + 0.3 * noise).astype(jnp.float32)


def levels(key, extent, cuts, smallest, high):
    loudness = 1.0
    for position, blocks in cuts:
        heights = jax.random.uniform(jax.random.fold_in(jax.random.fold_in(key, 6), position), (blocks,), jnp.float32, smallest / len(cuts), high / len(cuts))
        loudness = loudness * jnp.repeat(jnp.exp(heights), extent[position] // blocks).reshape((-1,) + (1,) * (len(extent) - 1 - position))
    return loudness


def gaussian(key, extent, spread, limit, cuts=(), kind=jnp.bfloat16):
    gain = levels(key, extent, cuts, -0.22, 0.18) if cuts else 1.0
    drawn = jax.random.normal(key, extent, jnp.float32) * spread * gain
    return jnp.minimum(jnp.maximum(drawn, -limit), limit).astype(kind)


def setup_inputs(seed: int = 0) -> dict:
    keys = jax.random.split(jax.random.key(seed), 8)
    return {
        "state0": draw_state0(jax.random.fold_in(keys[7], 71), 0),
        "iterate": draw_iterate(jax.random.fold_in(keys[7], 71), 0),
        "legendre": gaussian(keys[2], (M, NH, J), J ** -0.5, 0.25, ((0, 32),)),
        "lat_weight": jnp.clip(jax.random.uniform(keys[3], (NH,), jnp.float32, 0.25, 1.0), 0.25, 1.0),
        "coriolis": jnp.clip(jax.random.uniform(keys[4], (2, NH), jnp.float32, -1.5, 1.5), -1.5, 1.5),
        "damping": jnp.clip(jnp.exp(math.log(10.0) - 4.6051702 * jax.random.uniform(keys[5], (M, 3, J), jnp.float32) ** levels(keys[5], (M, 3, J), ((0, 32),), -0.2, 0.2)), 0.1, 10.0),
        "quadrature": jnp.clip(jax.random.uniform(keys[6], (NODES, NODES), jnp.float32, 0.02, 0.25), 0.02, 0.25),
    }


def to_grid(coeffs):
    first = (2.0 * jnp.real(coeffs[..., :1])).astype(coeffs.dtype)
    tail = jnp.zeros(coeffs.shape[:-1] + (NLON // 2 + 1 - M,), coeffs.dtype)
    padded = jnp.concatenate([first, coeffs[..., 1:], tail], axis=-1)
    return math.sqrt(M) * jnp.fft.irfft(padded, n=NLON, axis=-1)

def node_force(spec, legendre, lat_weight, coriolis, damping):
    half = J // 2
    table = legendre.astype(jnp.float32)
    coeff = spec.astype(jnp.bfloat16).astype(jnp.float32)
    even = jnp.einsum('cmefj,mlj->cmefl', coeff[..., :half], table[:, :, :half])
    odd = jnp.einsum('cmefj,mlj->cmefl', coeff[..., half:], table[:, :, half:])
    four = jnp.stack([even + odd, even - odd], axis=4)
    four = jnp.transpose(four, (0, 2, 3, 4, 5, 1))
    comp = four[0] + 1j * four[1]
    wave = jnp.arange(M, dtype=jnp.float32) / M
    values = to_grid(comp)
    slopes = to_grid(1j * wave * comp)
    u_wind, v_wind, height = (values[:, 0], values[:, 1], values[:, 2])
    u_slope, v_slope, h_slope = (slopes[:, 0], slopes[:, 1], slopes[:, 2])
    cor = coriolis[:, :, None]
    tend_u = -u_wind * u_slope + cor * v_wind - h_slope
    tend_v = -u_wind * v_slope - cor * u_wind
    tend_h = -u_wind * h_slope - (1.0 + height) * u_slope
    tend = jnp.stack([tend_u, tend_v, tend_h], axis=1)
    spectrum = jnp.fft.rfft(tend, axis=-1)[..., :M] / math.sqrt(M)
    weight = lat_weight[:, None]
    sym = weight * (spectrum[:, :, 0] + spectrum[:, :, 1])
    anti = weight * (spectrum[:, :, 0] - spectrum[:, :, 1])

    def to_real(z):
        parts = jnp.stack([jnp.real(z), jnp.imag(z)], axis=0)
        parts = jnp.transpose(parts, (0, 4, 1, 2, 3))
        return parts.astype(jnp.bfloat16).astype(jnp.float32)
    sym_r = to_real(sym)
    anti_r = to_real(anti)
    spec_even = jnp.einsum('cmefl,mlj->cmefj', sym_r, table[:, :, :half])
    spec_odd = jnp.einsum('cmefl,mlj->cmefj', anti_r, table[:, :, half:])
    nonlinear = jnp.concatenate([spec_even, spec_odd], axis=-1)
    return nonlinear - damping[None, :, None] * spec

def reference(state0, iterate, legendre, lat_weight, coriolis, damping, quadrature):
    force = lax.map(lambda spec: node_force(spec, legendre, lat_weight, coriolis, damping), iterate)
    mixed = jnp.tensordot(quadrature, force, axes=1, precision=lax.Precision.HIGHEST)
    diag = jnp.diagonal(quadrature)[:, None, None, None, None, None]
    rate = damping[None, None, :, None, :, :]
    updated = (state0[None] + mixed + diag * rate * iterate) / (1.0 + diag * rate)
    change = lax.optimization_barrier(jnp.sum((updated - iterate) ** 2, axis=(0, 1, 2, 3, 5)))
    base = lax.optimization_barrier(jnp.sum(state0 ** 2, axis=(0, 1, 2, 4)))
    sweep_change = jnp.sqrt(change / (NODES * base + 1e-06))
    return (updated, sweep_change)
```

```python
import functools
import math

import jax
import jax.numpy as jnp
import numpy as np
from jax import lax
from jax.experimental import pallas as pl
from jax.experimental.pallas import tpu as pltpu
from jax.sharding import Mesh
from jax.sharding import PartitionSpec as P

BAND = ("band_0", "band_1", "band_2")
MODES = 1024
POINTS = 2 * MODES
HALF = MODES // 2
QUARTER = POINTS // 4
ROWS = QUARTER + 16
LATS = 512
DEGREES = 512
NBAND = 32
PAIRS = 16
COLS = 24
LANES = 384
MB = 4
MIB = 1 << 20

NT = (((1,), (1,)), ((), ()))


def mm(a, b):
    return jnp.dot(a, b, preferred_element_type=jnp.float32)


def swap_groups(arrays, lane):
    for step in range(3):
        width = 16 << step
        low = (lane & width) == 0
        out = list(arrays)
        for i in range(8):
            if not i & (1 << step):
                j = i | (1 << step)
                a, b = arrays[i], arrays[j]
                out[i] = jnp.where(low, a, pltpu.roll(b, width, 1))
                out[j] = jnp.where(low, pltpu.roll(a, 128 - width, 1), b)
        arrays = out
    return arrays


def synthesis_kernel(it_ref, leg_ref, out_ref, coef_ref, wide_ref):
    step = pl.program_id(0)
    for k in range(MB):
        for c in range(2):
            for e in range(4):
                coef_ref[k, pl.ds((c * 4 + e) * 3, 3), :] = it_ref[c, k, e]
        coeff = coef_ref[k].astype(jnp.bfloat16)
        table = leg_ref[k]
        even = lax.dot_general(
            coeff[:, :256], table[:, :256], NT, preferred_element_type=jnp.float32
        )
        odd = lax.dot_general(
            coeff[:, 256:], table[:, 256:], NT, preferred_element_type=jnp.float32
        )
        at = step * MB + k
        for t in range(4):
            cut = slice(128 * t, 128 * (t + 1))
            wide_ref[0, t, pl.ds(at, COLS, stride=PAIRS), :] = (even + odd)[:, cut]
            wide_ref[1, t, pl.ds(at, COLS, stride=PAIRS), :] = (even - odd)[:, cut]

    @pl.when(step == pl.num_programs(0) - 1)
    def _():
        lane = lax.broadcasted_iota(jnp.int32, (PAIRS, 128), 1)
        for c in range(2):
            for f in range(3):
                for t in range(4):
                    parts = [
                        wide_ref[h, t, pl.ds(((c * 4 + e) * 3 + f) * PAIRS, PAIRS), :]
                        for h in range(2)
                        for e in range(4)
                    ]
                    for g, part in enumerate(swap_groups(parts, lane)):
                        out_ref[
                            8 * t + g, pl.ds(c * PAIRS, PAIRS), pl.ds(128 * f, 128)
                        ] = part.astype(jnp.bfloat16)


def synthesis(it6, leg4, par):
    return pl.pallas_call(
        synthesis_kernel,
        grid=(PAIRS // MB,),
        in_specs=[
            pl.BlockSpec((2, MB, None, 4, 3, DEGREES), lambda i: (0, i, par, 0, 0, 0)),
            pl.BlockSpec((MB, None, LATS, DEGREES), lambda i: (i, par, 0, 0)),
        ],
        out_specs=pl.BlockSpec((NBAND, 2 * PAIRS, LANES), lambda i: (0, 0, 0)),
        out_shape=jax.ShapeDtypeStruct((NBAND, 2 * PAIRS, LANES), jnp.bfloat16),
        scratch_shapes=[
            pltpu.VMEM((MB, COLS, DEGREES), jnp.float32),
            pltpu.VMEM((2, 4, COLS * PAIRS, 128), jnp.float32),
        ],
        compiler_params=pltpu.CompilerParams(vmem_limit_bytes=24 * MIB),
        cost_estimate=pl.CostEstimate(
            flops=2 * PAIRS * COLS * LATS * DEGREES, bytes_accessed=11 * MIB, transcendentals=0
        ),
        name="synthesis",
    )(it6, leg4)


def split(x):
    high = x.astype(jnp.bfloat16)
    return high, (x - high.astype(jnp.float32)).astype(jnp.bfloat16)


def table_kernel(row1_ref, row2_ref, col1_ref, col2_ref, tab_ref, back_ref):
    for par in range(2):
        wave = (
            2 * lax.broadcasted_iota(jnp.int32, (1, HALF), 1) + par
        ).astype(jnp.float32) * (1.0 / MODES)

        def rows(j, _, par=par, wave=wave):
            lead_c = row1_ref[par, 0, pl.ds(j, 1), :]
            lead_s = row1_ref[par, 1, pl.ds(j, 1), :]
            cosine = lead_c * row2_ref[par, 0] - lead_s * row2_ref[par, 1]
            sine = lead_s * row2_ref[par, 0] + lead_c * row2_ref[par, 1]
            at = pl.ds(pl.multiple_of(16 * j, 16), 16)
            for t, value in enumerate((cosine, sine, -wave * cosine, wave * sine)):
                high, low = split(value)
                tab_ref[4 * par + t, 0, at, :] = high
                tab_ref[4 * par + t, 1, at, :] = low
            return 0

        lax.fori_loop(0, ROWS // 16, rows, 0)
        for block in range(4):
            lead_c = col1_ref[par, 0, :, pl.ds(block, 1)]
            lead_s = col1_ref[par, 1, :, pl.ds(block, 1)]
            cosine = lead_c * col2_ref[par, 0] - lead_s * col2_ref[par, 1]
            sine = lead_s * col2_ref[par, 0] + lead_c * col2_ref[par, 1]
            if block == 0:
                first = lax.broadcasted_iota(jnp.int32, (1, 128), 1) == 0
                halve = jnp.where(first, 0.5, 1.0)
                cosine, sine = cosine * halve, sine * halve
            for t, value in enumerate((cosine, -sine)):
                high, low = split(value)
                back_ref[2 * par + t, 0, :, pl.ds(128 * block, 128)] = high
                back_ref[2 * par + t, 1, :, pl.ds(128 * block, 128)] = low


def small_tables():
    scale = 1.0 / math.sqrt(MODES)
    step = 2.0 * math.pi / POINTS
    rows1, rows2, cols1, cols2 = [], [], [], []
    for par in range(2):
        m = 2 * np.arange(HALF) + par

        def pair(k, factor):
            angle = ((k[:, None] * m[None, :]) % POINTS) * step
            return np.stack([np.cos(angle), np.sin(angle)]) * factor

        rows1.append(pair(16 * np.arange(ROWS // 16), 1.0))
        rows2.append(pair(np.arange(16), scale))
        cols1.append(pair(128 * np.arange(4), 1.0).transpose(0, 2, 1))
        cols2.append(pair(np.arange(128), scale).transpose(0, 2, 1))
    return [np.stack(x).astype(np.float32) for x in (rows1, rows2, cols1, cols2)]


def tables(parts):
    return pl.pallas_call(
        table_kernel,
        out_shape=(
            jax.ShapeDtypeStruct((8, 2, ROWS, HALF), jnp.bfloat16),
            jax.ShapeDtypeStruct((4, 2, HALF, QUARTER), jnp.bfloat16),
        ),
        compiler_params=pltpu.CompilerParams(vmem_limit_bytes=24 * MIB),
        cost_estimate=pl.CostEstimate(
            flops=16 * ROWS * HALF, bytes_accessed=15 * MIB, transcendentals=0
        ),
        name="tables",
    )(*parts)


def grid_kernel(
    xe_ref, xo_ref, tab_ref, back_ref, cor_ref, weight_ref,
    ye_ref, yo_ref,
    x_ref, wave_ref, high_ref, low_ref, edge_ref,
):
    for par, ref in enumerate((xe_ref, xo_ref)):
        for c in range(2):
            x_ref[2 * par + c] = ref[:, c * PAIRS : (c + 1) * PAIRS, :].reshape(HALF, LANES)
    which = (0, 1, 1, 0)
    for t in range(8):
        x = x_ref[4 * (t // 4) // 2 + which[t % 4]]
        wave_ref[t] = mm(tab_ref[t, 0], x) + mm(tab_ref[t, 1], x)
    cor = cor_ref[...]

    def quads(base, at, lanes):
        ce, se = wave_ref[base, at, lanes], wave_ref[base + 1, at, lanes]
        co, so = wave_ref[base + 4, at, lanes], wave_ref[base + 5, at, lanes]
        a, b, s, d = ce + co, ce - co, se + so, se - so
        return a - s, b + d, b - d, a + s

    def tendency(at):
        cuts = [pl.ds(128 * f, 128) for f in range(3)]
        values = [quads(0, at, cut) for cut in cuts]
        slopes = [quads(2, at, cut) for cut in cuts]
        out = [[], [], []]
        for q in range(4):
            u, v, h = (values[f][q] for f in range(3))
            us, vs, hs = (slopes[f][q] for f in range(3))
            out[0].append(cor * v - u * us - hs)
            out[1].append(-u * vs - cor * u)
            out[2].append(-u * hs - (1.0 + h) * us)
        folded = []
        for t1, t2, t3, t4 in out:
            a, b, c, d = t1 + t4, t2 + t3, t1 - t4, t3 - t2
            folded.append((a + b, c + d, a - b, c - d))
        return folded

    def block(j, _):
        at = pl.ds(pl.multiple_of(16 * j, 16), 16)
        for f, folded in enumerate(tendency(at)):
            for i, value in enumerate(folded):
                high, low = split(value)
                high_ref[i, at, pl.ds(128 * f, 128)] = high
                low_ref[i, at, pl.ds(128 * f, 128)] = low
        return 0

    lax.fori_loop(0, QUARTER // 16, block, 0)
    for f, folded in enumerate(tendency(pl.ds(QUARTER, 16))):
        edge_ref[0, :, pl.ds(128 * f, 128)] = folded[0]
        edge_ref[1, :, pl.ds(128 * f, 128)] = folded[3]

    odd_row = (lax.broadcasted_iota(jnp.int32, (HALF, 1), 0) & 1) == 1
    half_scale = 0.5 / math.sqrt(MODES)
    sign = jnp.where(odd_row, -half_scale, half_scale)
    lane = lax.broadcasted_iota(jnp.int32, (1, 128), 1)
    weight = weight_ref[...]
    signed = jnp.where(lane < 64, weight, -weight)
    for i in range(4):
        out = mm(back_ref[i, 0], high_ref[i]) + mm(back_ref[i, 1], high_ref[i])
        out = out + mm(back_ref[i, 0], low_ref[i])
        if i == 0:
            out = out + sign * edge_ref[0, 0:1, :]
        if i == 3:
            out = out - sign * edge_ref[1, 0:1, :]
        ref, c = (ye_ref, yo_ref)[i // 2], i % 2
        for f in range(3):
            part = out[:, 128 * f : 128 * (f + 1)]
            both = pltpu.roll(part, 64, 1) * weight + part * signed
            ref[:, c * PAIRS : (c + 1) * PAIRS, 128 * f : 128 * (f + 1)] = both.astype(
                jnp.bfloat16
            ).reshape(NBAND, PAIRS, 128)


def grid_stage(xe, xo, tab, back, cor, weight):
    shape = jax.ShapeDtypeStruct((NBAND, 2 * PAIRS, LANES), jnp.bfloat16)
    return pl.pallas_call(
        grid_kernel,
        out_shape=(shape, shape),
        scratch_shapes=[
            pltpu.VMEM((4, HALF, LANES), jnp.bfloat16),
            pltpu.VMEM((8, ROWS, LANES), jnp.float32),
            pltpu.VMEM((4, QUARTER, LANES), jnp.bfloat16),
            pltpu.VMEM((4, QUARTER, LANES), jnp.bfloat16),
            pltpu.VMEM((2, 16, LANES), jnp.float32),
        ],
        compiler_params=pltpu.CompilerParams(vmem_limit_bytes=48 * MIB),
        cost_estimate=pl.CostEstimate(
            flops=2 * 28 * ROWS * HALF * LANES, bytes_accessed=17 * MIB, transcendentals=0
        ),
        name="grid",
    )(xe, xo, tab, back, cor, weight)


def analysis_kernel(y_ref, leg_ref, it_ref, st_ref, damp_ref, out_ref, wide_ref, lin_ref, pair_ref):
    step = pl.program_id(0)

    @pl.when(step == 0)
    def _():
        lane = lax.broadcasted_iota(jnp.int32, (PAIRS, 128), 1)
        for c in range(2):
            for f in range(3):
                for t in range(4):
                    parts = [
                        y_ref[
                            8 * t + g, pl.ds(c * PAIRS, PAIRS), pl.ds(128 * f, 128)
                        ].astype(jnp.float32)
                        for g in range(8)
                    ]
                    for i, part in enumerate(swap_groups(parts, lane)):
                        row = ((c * 4 + i % 4) * 3 + f) * PAIRS
                        wide_ref[i // 4, t, pl.ds(row, PAIRS), :] = part

    for k in range(MB):
        rate = damp_ref[k]
        for c in range(2):
            for e in range(4):
                lin_ref[k, pl.ds((c * 4 + e) * 3, 3), :] = rate * (it_ref[c, k, e] - st_ref[c, k, e])
        at = step * MB + k
        for h in range(2):
            spec = jnp.concatenate(
                [wide_ref[h, t, pl.ds(at, COLS, stride=PAIRS), :] for t in range(4)], axis=1
            ).astype(jnp.bfloat16)
            cut = slice(256 * h, 256 * (h + 1))
            pair_ref[pl.ds(COLS * k, COLS), cut] = (
                mm(spec, leg_ref[k, :, cut]) - lin_ref[k, :, cut]
            )
    out_ref[...] = pair_ref[...].astype(jnp.bfloat16)


def analysis(y, leg4, it6, st6, damp4, par):
    state = pl.BlockSpec((2, MB, None, 4, 3, DEGREES), lambda i: (0, i, par, 0, 0, 0))
    return pl.pallas_call(
        analysis_kernel,
        grid=(PAIRS // MB,),
        in_specs=[
            pl.BlockSpec((NBAND, 2 * PAIRS, LANES), lambda i: (0, 0, 0)),
            pl.BlockSpec((MB, None, LATS, DEGREES), lambda i: (i, par, 0, 0)),
            state,
            state,
            pl.BlockSpec((MB, None, 3, DEGREES), lambda i: (i, par, 0, 0)),
        ],
        out_specs=pl.BlockSpec((MB * COLS, DEGREES), lambda i: (i, 0)),
        out_shape=jax.ShapeDtypeStruct((PAIRS * COLS, DEGREES), jnp.bfloat16),
        scratch_shapes=[
            pltpu.VMEM((2, 4, COLS * PAIRS, 128), jnp.float32),
            pltpu.VMEM((MB, COLS, DEGREES), jnp.float32),
            pltpu.VMEM((MB * COLS, DEGREES), jnp.float32),
        ],
        compiler_params=pltpu.CompilerParams(vmem_limit_bytes=24 * MIB),
        cost_estimate=pl.CostEstimate(
            flops=2 * PAIRS * COLS * LATS * DEGREES, bytes_accessed=13 * MIB, transcendentals=0
        ),
        name="analysis",
    )(y, leg4, it6, st6, damp4)


def update_kernel(
    quad_ref, own0, own1, up0, up1, dn0, dn1, fa0, fa1, fb0, fb1,
    st_ref, it_ref, damp_ref, out_ref, sums_ref, mix_ref, acc_ref,
):
    step = pl.program_id(0)
    w_own, w_up, w_dn, w_far = quad_ref[0], quad_ref[1], quad_ref[2], quad_ref[3]
    total, diag = quad_ref[4], quad_ref[5]
    rows = own0.shape[0]

    @pl.when(step == 0)
    def _():
        acc_ref[...] = jnp.zeros_like(acc_ref)

    for par, (own, up, dn, fa, fb) in enumerate(
        ((own0, up0, dn0, fa0, fb0), (own1, up1, dn1, fa1, fb1))
    ):
        near = (
            w_own * own[...].astype(jnp.float32)
            + w_up * up[...].astype(jnp.float32)
            + w_dn * dn[...].astype(jnp.float32)
        )
        far = jnp.where(step < pl.num_programs(0) // 2, fa[...].astype(jnp.float32), fb[...].astype(jnp.float32))
        mix_ref[par] = near + w_far * far

    for k in range(rows // COLS):
        for par in range(2):
            rate = damp_ref[k, par]
            keep = 1.0 - rate * total
            mine = diag * rate
            inverse = 1.0 / (1.0 + mine)
            for c in range(2):
                for e in range(4):
                    start = st_ref[c, k, par, e]
                    old = it_ref[c, k, par, e]
                    mixed = mix_ref[par, pl.ds(COLS * k + (c * 4 + e) * 3, 3), :]
                    new = (start * keep + mixed + mine * old) * inverse
                    out_ref[c, k, par, e] = new
                    acc_ref[0] += (new - old) * (new - old)
                    acc_ref[1] += start * start
    sums_ref[...] = acc_ref[...]


def update(quad, own, up, dn, fa, fb, st6, it6, damp4):
    steps = 4
    mb = PAIRS // steps
    dense = pl.BlockSpec((mb * COLS, DEGREES), lambda i: (i, 0))
    first = pl.BlockSpec((mb * COLS, DEGREES), lambda i: (jnp.minimum(i, steps // 2 - 1), 0))
    second = pl.BlockSpec((mb * COLS, DEGREES), lambda i: (jnp.maximum(i - steps // 2, 0), 0))
    state = pl.BlockSpec((2, mb, 2, 4, 3, DEGREES), lambda i: (0, i, 0, 0, 0, 0))
    return pl.pallas_call(
        update_kernel,
        grid=(steps,),
        in_specs=[pl.BlockSpec(memory_space=pltpu.SMEM)]
        + [dense] * 6
        + [first] * 2
        + [second] * 2
        + [state, state, pl.BlockSpec((mb, 2, 3, DEGREES), lambda i: (i, 0, 0, 0))],
        out_specs=(state, pl.BlockSpec((2, 3, DEGREES), lambda i: (0, 0, 0))),
        out_shape=(
            jax.ShapeDtypeStruct(it6.shape, jnp.float32),
            jax.ShapeDtypeStruct((2, 3, DEGREES), jnp.float32),
        ),
        scratch_shapes=[
            pltpu.VMEM((2, mb * COLS, DEGREES), jnp.float32),
            pltpu.VMEM((2, 3, DEGREES), jnp.float32),
        ],
        compiler_params=pltpu.CompilerParams(vmem_limit_bytes=32 * MIB),
        cost_estimate=pl.CostEstimate(
            flops=20 * 2 * PAIRS * COLS * DEGREES, bytes_accessed=10 * MIB, transcendentals=0
        ),
        name="update",
    )(quad, *own, *up, *dn, *fa, *fb, st6, it6, damp4)


def body(state0, iterate, legendre, lat_weight, coriolis, damping, quadrature):
    node = lax.axis_index("node")
    band = lax.axis_index(BAND)
    lat_rows = LATS // NBAND
    it6 = iterate.reshape(2, PAIRS, 2, 4, 3, DEGREES)
    st6 = state0.reshape(2, PAIRS, 2, 4, 3, DEGREES)
    leg4 = legendre.reshape(PAIRS, 2, LATS, DEGREES)
    damp4 = damping.reshape(PAIRS, 2, 3, DEGREES)

    def exchange(x):
        return lax.all_to_all(x, BAND, split_axis=0, concat_axis=0, tiled=True)

    def shift(x, by):
        return lax.ppermute(x, "node", [(i, (i + by) % 4) for i in range(4)])

    sent = [synthesis(it6, leg4, par) for par in range(2)]
    got = [exchange(x) for x in sent]
    parts = [jnp.asarray(x) for x in small_tables()]
    parts, _ = lax.optimization_barrier((parts, sent))
    tab, back = tables(parts)
    first = band * lat_rows
    cor = lax.dynamic_slice_in_dim(coriolis, first, lat_rows, 1)
    cor = jnp.broadcast_to(cor[:, None, :], (2, 4, lat_rows)).reshape(1, 128)
    weight = lax.dynamic_slice_in_dim(lat_weight, first, lat_rows, 0)
    weight = jnp.broadcast_to(weight[None, :], (8, lat_rows)).reshape(1, 128)
    back_sent = grid_stage(*got, tab, back, cor, weight)
    spectra = [exchange(y) for y in back_sent]
    own = [analysis(spectra[par], leg4, it6, st6, damp4, par) for par in range(2)]
    rows = own[0].shape[0] // 2
    up = [shift(x, 1) for x in own]
    dn = [shift(x, -1) for x in own]
    fa = [shift(x[:rows], 1) for x in up]
    fb = [shift(x[rows:], -1) for x in dn]
    row = lax.dynamic_slice_in_dim(quadrature, node, 1, 0)[0]
    weights = jnp.roll(jnp.concatenate([row, row]), 0)
    pick = lax.dynamic_slice_in_dim(weights, node, 4, 0)
    quad = jnp.stack([pick[0], pick[3], pick[1], pick[2], jnp.sum(row), pick[0]])
    out, sums = update(quad, own, up, dn, fa, fb, st6, it6, damp4)
    partial = jnp.sum(sums, axis=2)
    for axis in ("node",) + BAND:
        partial = lax.psum(partial, axis)
    change, base = partial[0], partial[1]
    ratio = jnp.sqrt(change / (base + 1e-06))
    return (out.reshape(iterate.shape), ratio)


def solution(mesh):
    torus = Mesh(
        mesh.devices.reshape(mesh.shape["node"], 4, 4, 2), ("node", "band_0", "band_1", "band_2")
    )
    return jax.shard_map(
        body,
        mesh=torus,
        in_specs=(
            P(None, BAND, None, None, None),
            P("node", None, BAND, None, None, None),
            P(BAND, None, None),
            P(),
            P(),
            P(BAND, None, None),
            P(),
        ),
        out_specs=(P("node", None, BAND, None, None, None), P()),
        check_vma=False,
    )
```

```python
import functools
import math

import jax
import jax.numpy as jnp
import numpy as np
from jax import lax
from jax.experimental import pallas as pl
from jax.experimental.pallas import tpu as pltpu
from jax.sharding import Mesh
from jax.sharding import PartitionSpec as P

BAND = ("band_0", "band_1", "band_2")
NODE_BAND = ("node",) + BAND
MODES = 1024
POINTS = 2 * MODES
HALF = MODES // 2
QUARTER = POINTS // 4
ROWS = QUARTER + 16
LATS = 512
DEGREES = 512
NBAND = 32
PAIRS = 16
COLS = 24
LANES = 384
MB = 4
MIB = 1 << 20


def mm(a, b):
    return jnp.dot(a, b, preferred_element_type=jnp.float32)


def swap_groups(arrays, lane):
    for step in range(3):
        width = 16 << step
        low = (lane & width) == 0
        out = list(arrays)
        for i in range(8):
            if not i & (1 << step):
                j = i | (1 << step)
                a, b = arrays[i], arrays[j]
                out[i] = jnp.where(low, a, pltpu.roll(b, width, 1))
                out[j] = jnp.where(low, pltpu.roll(a, 128 - width, 1), b)
        arrays = out
    return arrays


def synthesis_kernel(it_ref, leg_ref, out_ref, send_ref, coef_ref, wide_ref):
    step = pl.program_id(0)

    @pl.when(step == 0)
    def _():
        coef_ref[...] = jnp.zeros_like(coef_ref)

    for k in range(MB):
        for c in range(2):
            for f in range(3):
                row = (c * 3 + f) * 4
                coef_ref[pl.ds(32 * k + row, 4), :] = it_ref[c, k, f]
                send_ref[pl.ds(COLS * k + row, 4), :] = it_ref[c, k, f]
    turned = jnp.transpose(coef_ref[...].astype(jnp.bfloat16).astype(jnp.float32))
    owner = lax.broadcasted_iota(jnp.int32, (DEGREES, 128), 1) // 32
    total = jnp.zeros((LATS, 256), jnp.float32)
    for k in range(MB):
        mine = jnp.where(owner == k, turned, 0.0)
        north = mine.astype(jnp.bfloat16)
        south = jnp.concatenate([mine[:256], -mine[256:]], axis=0).astype(jnp.bfloat16)
        total = total + mm(leg_ref[k], jnp.concatenate([north, south], axis=1))
    par = step // 4
    at = par * PAIRS + (step % 4) * MB
    for h in range(2):
        for t in range(4):
            block = jnp.transpose(total[128 * t : 128 * (t + 1), 128 * h : 128 * (h + 1)])
            for k in range(MB):
                wide_ref[h, t, pl.ds(at + k, COLS, stride=2 * PAIRS), :] = block[
                    32 * k : 32 * k + COLS
                ]

    @pl.when(step == pl.num_programs(0) - 1)
    def _():
        lane = lax.broadcasted_iota(jnp.int32, (PAIRS, 128), 1)
        for p in range(2):
            for c in range(2):
                for f in range(3):
                    for t in range(4):
                        parts = [
                            wide_ref[
                                h, t, pl.ds((((c * 3 + f) * 4 + e) * 2 + p) * PAIRS, PAIRS), :
                            ]
                            for h in range(2)
                            for e in range(4)
                        ]
                        for g, part in enumerate(swap_groups(parts, lane)):
                            out_ref[
                                8 * t + g, pl.ds((2 * p + c) * PAIRS, PAIRS), pl.ds(128 * f, 128)
                            ] = part.astype(jnp.bfloat16)


def synthesis(it6, leg4):
    return pl.pallas_call(
        synthesis_kernel,
        grid=(8,),
        in_specs=[
            pl.BlockSpec((2, MB, None, 3, 4, DEGREES), lambda i: (0, i % 4, i // 4, 0, 0, 0)),
            pl.BlockSpec((MB, None, LATS, DEGREES), lambda i: (i % 4, i // 4, 0, 0)),
        ],
        out_specs=(
            pl.BlockSpec((NBAND, 4 * PAIRS, LANES), lambda i: (0, 0, 0)),
            pl.BlockSpec((None, MB * COLS, DEGREES), lambda i: (i // 2, i % 2, 0)),
        ),
        out_shape=(
            jax.ShapeDtypeStruct((NBAND, 4 * PAIRS, LANES), jnp.bfloat16),
            jax.ShapeDtypeStruct((4, 8 * COLS, DEGREES), jnp.float32),
        ),
        scratch_shapes=[
            pltpu.VMEM((MB * 32, DEGREES), jnp.float32),
            pltpu.VMEM((2, 4, COLS * 2 * PAIRS, 128), jnp.float32),
        ],
        compiler_params=pltpu.CompilerParams(vmem_limit_bytes=56 * MIB),
        cost_estimate=pl.CostEstimate(
            flops=4 * 32 * COLS * LATS * DEGREES, bytes_accessed=21 * MIB, transcendentals=0
        ),
        name="synthesis",
    )(it6, leg4)


def split(x):
    high = x.astype(jnp.bfloat16)
    return high, (x - high.astype(jnp.float32)).astype(jnp.bfloat16)


def table_kernel(row1_ref, row2_ref, col1_ref, col2_ref, tab_ref, back_ref):
    for par in range(2):
        wave = (
            2 * lax.broadcasted_iota(jnp.int32, (1, HALF), 1) + par
        ).astype(jnp.float32) * (1.0 / MODES)

        def rows(j, _, par=par, wave=wave):
            lead_c = row1_ref[par, 0, pl.ds(j, 1), :]
            lead_s = row1_ref[par, 1, pl.ds(j, 1), :]
            cosine = lead_c * row2_ref[par, 0] - lead_s * row2_ref[par, 1]
            sine = lead_s * row2_ref[par, 0] + lead_c * row2_ref[par, 1]
            at = pl.ds(pl.multiple_of(16 * j, 16), 16)
            for t, value in enumerate((cosine, sine, -wave * cosine, wave * sine)):
                high, low = split(value)
                tab_ref[4 * par + t, 0, at, :] = high
                tab_ref[4 * par + t, 1, at, :] = low
            return 0

        lax.fori_loop(0, ROWS // 16, rows, 0)
        for block in range(4):
            lead_c = col1_ref[par, 0, :, pl.ds(block, 1)]
            lead_s = col1_ref[par, 1, :, pl.ds(block, 1)]
            cosine = lead_c * col2_ref[par, 0] - lead_s * col2_ref[par, 1]
            sine = lead_s * col2_ref[par, 0] + lead_c * col2_ref[par, 1]
            if block == 0:
                first = lax.broadcasted_iota(jnp.int32, (1, 128), 1) == 0
                halve = jnp.where(first, 0.5, 1.0)
                cosine, sine = cosine * halve, sine * halve
            for t, value in enumerate((cosine, -sine)):
                high, low = split(value)
                back_ref[2 * par + t, 0, :, pl.ds(128 * block, 128)] = high
                back_ref[2 * par + t, 1, :, pl.ds(128 * block, 128)] = low


def small_tables():
    scale = 1.0 / math.sqrt(MODES)
    step = 2.0 * math.pi / POINTS
    rows1, rows2, cols1, cols2 = [], [], [], []
    for par in range(2):
        m = 2 * np.arange(HALF) + par

        def pair(k, factor):
            angle = ((k[:, None] * m[None, :]) % POINTS) * step
            return np.stack([np.cos(angle), np.sin(angle)]) * factor

        rows1.append(pair(16 * np.arange(ROWS // 16), 1.0))
        rows2.append(pair(np.arange(16), scale))
        cols1.append(pair(128 * np.arange(4), 1.0).transpose(0, 2, 1))
        cols2.append(pair(np.arange(128), scale).transpose(0, 2, 1))
    return [np.stack(x).astype(np.float32) for x in (rows1, rows2, cols1, cols2)]


def tables(parts):
    return pl.pallas_call(
        table_kernel,
        out_shape=(
            jax.ShapeDtypeStruct((8, 2, ROWS, HALF), jnp.bfloat16),
            jax.ShapeDtypeStruct((4, 2, HALF, QUARTER), jnp.bfloat16),
        ),
        compiler_params=pltpu.CompilerParams(vmem_limit_bytes=24 * MIB),
        cost_estimate=pl.CostEstimate(
            flops=16 * ROWS * HALF, bytes_accessed=15 * MIB, transcendentals=0
        ),
        name="tables",
    )(*parts)


def grid_kernel(
    got_ref, tab_ref, back_ref, cor_ref, weight_ref,
    out_ref,
    x_ref, wave_ref, high_ref, low_ref, edge_ref,
):
    for i in range(4):
        x_ref[i] = got_ref[:, i * PAIRS : (i + 1) * PAIRS, :].reshape(HALF, LANES)
    which = (0, 1, 1, 0, 2, 3, 3, 2)
    for t in range(8):
        x = x_ref[which[t]]
        wave_ref[t] = mm(tab_ref[t, 0], x) + mm(tab_ref[t, 1], x)
    cor = cor_ref[...]

    def quads(base, at, lanes):
        ce, se = wave_ref[base, at, lanes], wave_ref[base + 1, at, lanes]
        co, so = wave_ref[base + 4, at, lanes], wave_ref[base + 5, at, lanes]
        a, b, s, d = ce + co, ce - co, se + so, se - so
        return a - s, b + d, b - d, a + s

    def tendency(at):
        cuts = [pl.ds(128 * f, 128) for f in range(3)]
        values = [quads(0, at, cut) for cut in cuts]
        slopes = [quads(2, at, cut) for cut in cuts]
        out = [[], [], []]
        for q in range(4):
            u, v, h = (values[f][q] for f in range(3))
            us, vs, hs = (slopes[f][q] for f in range(3))
            out[0].append(cor * v - u * us - hs)
            out[1].append(-u * vs - cor * u)
            out[2].append(-u * hs - (1.0 + h) * us)
        folded = []
        for t1, t2, t3, t4 in out:
            a, b, c, d = t1 + t4, t2 + t3, t1 - t4, t3 - t2
            folded.append((a + b, c + d, a - b, c - d))
        return folded

    def block(j, _):
        at = pl.ds(pl.multiple_of(16 * j, 16), 16)
        for f, folded in enumerate(tendency(at)):
            for i, value in enumerate(folded):
                high, low = split(value)
                high_ref[i, at, pl.ds(128 * f, 128)] = high
                low_ref[i, at, pl.ds(128 * f, 128)] = low
        return 0

    lax.fori_loop(0, QUARTER // 16, block, 0)
    for f, folded in enumerate(tendency(pl.ds(QUARTER, 16))):
        edge_ref[0, :, pl.ds(128 * f, 128)] = folded[0]
        edge_ref[1, :, pl.ds(128 * f, 128)] = folded[3]

    odd_row = (lax.broadcasted_iota(jnp.int32, (HALF, 1), 0) & 1) == 1
    half_scale = 0.5 / math.sqrt(MODES)
    sign = jnp.where(odd_row, -half_scale, half_scale)
    lane = lax.broadcasted_iota(jnp.int32, (1, 128), 1)
    weight = weight_ref[...]
    signed = jnp.where(lane < 64, weight, -weight)
    for par in range(2):
        both = []
        for c in range(2):
            i = 2 * par + c
            out = mm(back_ref[i, 0], high_ref[i]) + mm(back_ref[i, 1], high_ref[i])
            out = out + mm(back_ref[i, 0], low_ref[i])
            if i == 0:
                out = out + sign * edge_ref[0, 0:1, :]
            if i == 3:
                out = out - sign * edge_ref[1, 0:1, :]
            both.append(out)
        for f in range(3):
            parts = []
            for out in both:
                part = out[:, 128 * f : 128 * (f + 1)]
                part = pltpu.roll(part, 64, 1) * weight + part * signed
                parts.append(part.reshape(NBAND, 2, 8, 128))
            joined = jnp.concatenate(parts, axis=2).astype(jnp.bfloat16)
            for h in range(2):
                z = 2 * par + h
                out_ref[z * NBAND : (z + 1) * NBAND, :, 128 * f : 128 * (f + 1)] = joined[:, h]


def grid_stage(got, tab, back, cor, weight):
    return pl.pallas_call(
        grid_kernel,
        out_shape=jax.ShapeDtypeStruct((4 * NBAND, 16, LANES), jnp.bfloat16),
        scratch_shapes=[
            pltpu.VMEM((4, HALF, LANES), jnp.bfloat16),
            pltpu.VMEM((8, ROWS, LANES), jnp.float32),
            pltpu.VMEM((4, QUARTER, LANES), jnp.bfloat16),
            pltpu.VMEM((4, QUARTER, LANES), jnp.bfloat16),
            pltpu.VMEM((2, 16, LANES), jnp.float32),
        ],
        compiler_params=pltpu.CompilerParams(vmem_limit_bytes=28 * MIB),
        cost_estimate=pl.CostEstimate(
            flops=2 * 28 * ROWS * HALF * LANES, bytes_accessed=17 * MIB, transcendentals=0
        ),
        name="grid",
    )(got, tab, back, cor, weight)


def analysis_kernel(
    id_ref, quad_ref, y_ref, leg_ref, it_ref, st_ref, damp_ref,
    out_ref, sums_ref,
    wide_ref, rate_ref, start_ref, mix_ref, acc_ref,
):
    step = pl.program_id(0)

    @pl.when(step == 0)
    def _():
        acc_ref[...] = jnp.zeros_like(acc_ref)
        lane = lax.broadcasted_iota(jnp.int32, (16, 128), 1)
        for p in range(4):
            for f in range(3):
                for t in range(4):
                    parts = [
                        y_ref[p * NBAND + 8 * t + g, :, pl.ds(128 * f, 128)].astype(jnp.float32)
                        for g in range(8)
                    ]
                    for i, part in enumerate(swap_groups(parts, lane)):
                        for c in range(2):
                            row = (((p * 2 + c) * 3 + f) * 4 + i % 4) * 8
                            wide_ref[i // 4, t, pl.ds(row, 8), :] = part[8 * c : 8 * c + 8]

    node = id_ref[0]
    for k in range(MB):
        at = step * MB + k
        mode = 2 * (8 * (node % 2) + at) + node // 2
        for c in range(2):
            for f in range(3):
                row = (c * 3 + f) * 4
                rate_ref[pl.ds(row, 4), :] = jnp.broadcast_to(
                    damp_ref[f, pl.ds(mode, 1), :], (4, DEGREES)
                )
                start_ref[pl.ds(row, 4), :] = st_ref[c, k, f]
        halves = []
        for h in range(2):
            spec = jnp.concatenate(
                [wide_ref[h, t, pl.ds(at, 4 * COLS, stride=8), :] for t in range(4)], axis=1
            ).astype(jnp.bfloat16)
            halves.append(mm(spec, leg_ref[k, :, 256 * h : 256 * (h + 1)]))
        for h in range(2):
            cut = slice(256 * h, 256 * (h + 1))
            rate, start = rate_ref[:, cut], start_ref[:, cut]
            olds = [it_ref[p, COLS * k : COLS * (k + 1), cut] for p in range(4)]
            forces = [
                halves[h][COLS * p : COLS * (p + 1)] - rate * (olds[p] - start) for p in range(4)
            ]
            change = jnp.zeros_like(start)
            for q in range(4):
                row = [quad_ref[q, p] for p in range(4)]
                mine = row[q] * rate
                inverse = 1.0 / (1.0 + mine)
                mixed = (
                    row[0] * forces[0] + row[1] * forces[1] + row[2] * forces[2] + row[3] * forces[3]
                ) * inverse
                total = row[0] + row[1] + row[2] + row[3]
                new = mixed + (start * (1.0 - rate * total) + mine * olds[q]) * inverse
                moved = new - olds[q]
                change = change + moved * moved
                mix_ref[q, COLS * k : COLS * (k + 1), cut] = mixed
            acc_ref[0, :, cut] += change
            acc_ref[1, :, cut] += start * start
    out_ref[...] = mix_ref[...].astype(jnp.bfloat16)

    @pl.when(step == pl.num_programs(0) - 1)
    def _():
        field = lax.broadcasted_iota(jnp.int32, (COLS, 1), 0) // 4 % 3
        lane = lax.broadcasted_iota(jnp.int32, (1, 128), 1)
        sums = jnp.zeros((1, 128), jnp.float32)
        for s in range(2):
            per_row = jnp.sum(acc_ref[s], axis=1, keepdims=True)
            for f in range(3):
                value = jnp.sum(jnp.where(field == f, per_row, 0.0), axis=0, keepdims=True)
                sums = sums + jnp.where(lane == 3 * s + f, value, 0.0)
        sums_ref[...] = sums


def analysis(ids, quad, y, leg4, it_all, st6, damp):
    spec = pl.BlockSpec
    return pl.pallas_call(
        analysis_kernel,
        grid_spec=pltpu.PrefetchScalarGridSpec(
            num_scalar_prefetch=1,
            grid=(2,),
            in_specs=[
                spec(memory_space=pltpu.SMEM),
                spec((4 * NBAND, 16, LANES), lambda i, s: (0, 0, 0)),
                spec(
                    (MB, None, LATS, DEGREES), lambda i, s: (s[0] % 2 * 2 + i, s[0] // 2, 0, 0)
                ),
                spec((4, MB * COLS, DEGREES), lambda i, s: (0, i, 0)),
                spec(
                    (2, MB, None, 3, 4, DEGREES),
                    lambda i, s: (0, s[0] % 2 * 2 + i, s[0] // 2, 0, 0, 0),
                ),
                spec((3, 32, DEGREES), lambda i, s: (0, 0, 0)),
            ],
            out_specs=(
                spec((4, MB * COLS, DEGREES), lambda i, s: (0, i, 0)),
                spec((1, 128), lambda i, s: (0, 0)),
            ),
            scratch_shapes=[
                pltpu.VMEM((2, 4, 4 * COLS * 8, 128), jnp.float32),
                pltpu.VMEM((COLS, DEGREES), jnp.float32),
                pltpu.VMEM((COLS, DEGREES), jnp.float32),
                pltpu.VMEM((4, MB * COLS, DEGREES), jnp.float32),
                pltpu.VMEM((2, COLS, DEGREES), jnp.float32),
            ],
        ),
        out_shape=(
            jax.ShapeDtypeStruct((4, 8 * COLS, DEGREES), jnp.bfloat16),
            jax.ShapeDtypeStruct((1, 128), jnp.float32),
        ),
        compiler_params=pltpu.CompilerParams(vmem_limit_bytes=56 * MIB),
        cost_estimate=pl.CostEstimate(
            flops=2 * 32 * COLS * LATS * DEGREES, bytes_accessed=10 * MIB, transcendentals=0
        ),
        name="analysis",
    )(ids, quad, y, leg4, it_all, st6, damp)


def update_kernel(id_ref, quad_ref, mixed_ref, st_ref, it_ref, damp_ref, out_ref, mix_ref):
    z = pl.program_id(0)
    node = id_ref[0]
    total = quad_ref[node, 0] + quad_ref[node, 1] + quad_ref[node, 2] + quad_ref[node, 3]
    diag = quad_ref[node, node]
    mix_ref[...] = mixed_ref[...].astype(jnp.float32)
    for k in range(8):
        mode = 2 * (8 * (z % 2) + k) + z // 2
        for f in range(3):
            rate = damp_ref[f, pl.ds(mode, 1), :]
            mine = diag * rate
            inverse = 1.0 / (1.0 + mine)
            keep = (1.0 - rate * total) * inverse
            mine = mine * inverse
            for c in range(2):
                mixed = mix_ref[pl.ds(COLS * k + (c * 3 + f) * 4, 4), :]
                out_ref[c, k, f] = mixed + st_ref[c, k, f] * keep + mine * it_ref[c, k, f]


def update(ids, quad, mixed, st7, it7, damp):
    spec = pl.BlockSpec
    state = spec((2, None, 8, None, 3, 4, DEGREES), lambda i, s: (0, i % 2, 0, i // 2, 0, 0, 0))
    return pl.pallas_call(
        update_kernel,
        grid_spec=pltpu.PrefetchScalarGridSpec(
            num_scalar_prefetch=1,
            grid=(4,),
            in_specs=[
                spec(memory_space=pltpu.SMEM),
                spec((None, 8 * COLS, DEGREES), lambda i, s: (i, 0, 0)),
                state,
                state,
                spec((3, 32, DEGREES), lambda i, s: (0, 0, 0)),
            ],
            out_specs=state,
            scratch_shapes=[pltpu.VMEM((8 * COLS, DEGREES), jnp.float32)],
        ),
        out_shape=jax.ShapeDtypeStruct(it7.shape, jnp.float32),
        compiler_params=pltpu.CompilerParams(vmem_limit_bytes=32 * MIB),
        cost_estimate=pl.CostEstimate(
            flops=4 * 32 * COLS * DEGREES, bytes_accessed=6 * MIB, transcendentals=0
        ),
        name="update",
    )(ids, quad, mixed, st7, it7, damp)


def exchange(x, axes):
    return lax.all_to_all(x, axes, split_axis=0, concat_axis=0, tiled=True)


def body(state0, iterate, legendre, lat_weight, coriolis, damping, quadrature):
    node = lax.axis_index("node")
    band = lax.axis_index(BAND)
    lat_rows = LATS // NBAND
    spec = iterate[0].transpose(0, 1, 3, 2, 4)
    base = state0.transpose(0, 1, 3, 2, 4)
    it6 = spec.reshape(2, PAIRS, 2, 3, 4, DEGREES)
    st6 = base.reshape(2, PAIRS, 2, 3, 4, DEGREES)
    leg4 = legendre.reshape(PAIRS, 2, LATS, DEGREES)
    damp = damping.transpose(1, 0, 2)
    ids = jnp.reshape(node, (1,)).astype(jnp.int32)

    sent, spread = synthesis(it6, leg4)
    got = exchange(sent, BAND)
    spread = exchange(spread, "node")
    parts = [jnp.asarray(x) for x in small_tables()]
    parts, _ = lax.optimization_barrier((parts, sent))
    tab, back = tables(parts)
    first = band * lat_rows
    cor = lax.dynamic_slice_in_dim(coriolis, first, lat_rows, 1)
    cor = jnp.broadcast_to(cor[:, None, :], (2, 4, lat_rows)).reshape(1, 128)
    weight = lax.dynamic_slice_in_dim(lat_weight, first, lat_rows, 0)
    weight = jnp.broadcast_to(weight[None, :], (8, lat_rows)).reshape(1, 128)
    spectra = exchange(grid_stage(got, tab, back, cor, weight), NODE_BAND)
    mixed, sums = analysis(ids, quadrature, spectra, leg4, spread, st6, damp)
    mixed = exchange(mixed, "node")
    sums = exchange(jnp.broadcast_to(sums[None], (4 * NBAND, 1, 128)), NODE_BAND)
    shape7 = (2, 2, 8, 2, 3, 4, DEGREES)
    out = update(ids, quadrature, mixed, base.reshape(shape7), spec.reshape(shape7), damp)
    total = jnp.sum(sums, axis=(0, 1))
    ratio = jnp.sqrt(total[:3] / (4.0 * total[3:6] + 1e-06))
    out = out.reshape(2, 32, 3, 4, DEGREES).transpose(0, 1, 3, 2, 4)
    return (out[None], ratio)


def solution(mesh):
    torus = Mesh(
        mesh.devices.reshape(mesh.shape["node"], 4, 4, 2), ("node", "band_0", "band_1", "band_2")
    )
    return jax.shard_map(
        body,
        mesh=torus,
        in_specs=(
            P(None, BAND, None, None, None),
            P("node", None, BAND, None, None, None),
            P(BAND, None, None),
            P(),
            P(),
            P(BAND, None, None),
            P(),
        ),
        out_specs=(P("node", None, BAND, None, None, None), P()),
        check_vma=False,
    )
```

```python
import functools
import math

import jax
import jax.numpy as jnp
import numpy as np
from jax import lax
from jax.experimental import pallas as pl
from jax.experimental.pallas import tpu as pltpu
from jax.sharding import Mesh
from jax.sharding import PartitionSpec as P

BAND = ("band_0", "band_1", "band_2")
NODE_BAND = ("node",) + BAND
MODES = 1024
POINTS = 2 * MODES
HALF = MODES // 2
QUARTER = POINTS // 4
ROWS = QUARTER + 16
LATS = 512
DEGREES = 512
NBAND = 32
PAIRS = 16
COLS = 24
LANES = 384
MB = 4
MIB = 1 << 20


NT = (((1,), (1,)), ((), ()))


def mm(a, b):
    return jnp.dot(a, b, preferred_element_type=jnp.float32)


STREAMS = 16


def synthesis_kernel(it_hbm, leg_hbm, out_ref, it_ref, leg_ref, sems, coef_ref, wide_ref):
    def stream(j):
        return pltpu.make_async_copy(
            leg_hbm.at[pl.ds(j % 8 * 2, 2), j // 8], leg_ref.at[j], sems.at[j]
        )

    coefficients = pltpu.make_async_copy(it_hbm, it_ref, sems.at[STREAMS])
    coefficients.start()
    for j in range(STREAMS):
        stream(j).start()
    coefficients.wait()
    low = lax.broadcasted_iota(jnp.int32, (COLS, 128), 1) < 64

    def pair(j, _):
        stream(j).wait()
        par = j // 8
        for k in range(2):
            i = j % 8 * 2 + k
            for c in range(2):
                for f in range(3):
                    row = (c * 3 + f) * 4
                    coef_ref[k, row : row + 4, :] = it_ref[c, i, par, f]
            coeff = coef_ref[k].astype(jnp.bfloat16)
            even = lax.dot_general(
                coeff[:, :256], leg_ref[j, k, :, :256], NT, preferred_element_type=jnp.float32
            )
            odd = lax.dot_general(
                coeff[:, 256:], leg_ref[j, k, :, 256:], NT, preferred_element_type=jnp.float32
            )
            for t in range(4):
                cut = slice(128 * t, 128 * (t + 1))
                north = even[:, cut] + odd[:, cut]
                south = pltpu.roll(even[:, cut] - odd[:, cut], 64, 1)
                rows = pl.ds(par * PAIRS + i, COLS, stride=2 * PAIRS)
                wide_ref[2 * t, rows, :] = jnp.where(low, north, south)
                wide_ref[2 * t + 1, rows, :] = jnp.where(low, south, north)
        return 0

    lax.fori_loop(0, STREAMS, pair, 0)
    for p in range(2):
        for c in range(2):
            for f in range(3):
                for e in range(4):
                    row = (((c * 3 + f) * 4 + e) * 2 + p) * PAIRS
                    out_ref[
                        8 * e : 8 * e + 8,
                        (2 * p + c) * PAIRS : (2 * p + c + 1) * PAIRS,
                        128 * f : 128 * (f + 1),
                    ] = wide_ref[:, row : row + PAIRS, :].astype(jnp.bfloat16)


def synthesis(it6, leg4):
    return pl.pallas_call(
        synthesis_kernel,
        in_specs=[pl.BlockSpec(memory_space=pl.ANY)] * 2,
        out_shape=jax.ShapeDtypeStruct((NBAND, 4 * PAIRS, LANES), jnp.bfloat16),
        scratch_shapes=[
            pltpu.VMEM(it6.shape, jnp.float32),
            pltpu.VMEM((STREAMS, 2, LATS, DEGREES), jnp.bfloat16),
            pltpu.SemaphoreType.DMA((STREAMS + 1,)),
            pltpu.VMEM((2, COLS, DEGREES), jnp.float32),
            pltpu.VMEM((8, COLS * 2 * PAIRS, 128), jnp.float32),
        ],
        compiler_params=pltpu.CompilerParams(vmem_limit_bytes=56 * MIB),
        cost_estimate=pl.CostEstimate(
            flops=2 * 32 * COLS * LATS * DEGREES, bytes_accessed=20 * MIB, transcendentals=0
        ),
        name="synthesis",
    )(it6, leg4)


def encode(x):
    return (x * jnp.abs(x)).astype(jnp.bfloat16)


def decode(coded):
    coded = coded.astype(jnp.float32)
    root = jnp.sqrt(jnp.abs(coded))
    return jnp.where(coded < 0, -root, root)


def prepare_kernel(
    id_ref, quad_ref, st_ref, it_ref, damp_ref,
    send0_ref, send1_ref, send2_ref, send3_ref, base_ref, dense_ref,
):
    node = id_ref[0]
    place = pl.program_id(0)
    z = (node + place) % 4
    total = quad_ref[node, 0] + quad_ref[node, 1] + quad_ref[node, 2] + quad_ref[node, 3]
    diag = quad_ref[node, node]
    for k in range(8):
        mode = 2 * (8 * (z % 2) + k) + z // 2
        for f in range(3):
            rate = damp_ref[f, pl.ds(mode, 1), :]
            mine = diag * rate
            inverse = 1.0 / (1.0 + mine)
            keep = (1.0 - rate * total) * inverse
            mine = mine * inverse
            for c in range(2):
                row = COLS * k + (c * 3 + f) * 4
                start, old = st_ref[c, k, f], it_ref[c, k, f]
                dense_ref[row : row + 4, :] = old - start
                base_ref[c, k, f] = start * keep + mine * old
    for s, ref in enumerate((send0_ref, send1_ref, send2_ref, send3_ref)):

        @pl.when(place == s)
        def _(ref=ref):
            ref[...] = encode(dense_ref[...])


def own_subset(i, s):
    z = (s[0] + i) % 4
    return (0, z % 2, 0, z // 2, 0, 0, 0)


STATE = (2, None, 8, None, 3, 4, DEGREES)


def prepare(ids, quad, st7, it7, damp):
    spec = pl.BlockSpec
    state = spec(STATE, own_subset)
    return pl.pallas_call(
        prepare_kernel,
        grid_spec=pltpu.PrefetchScalarGridSpec(
            num_scalar_prefetch=1,
            grid=(4,),
            in_specs=[
                spec(memory_space=pltpu.SMEM),
                state,
                state,
                spec((3, 32, DEGREES), lambda i, s: (0, 0, 0)),
            ],
            out_specs=[spec((8 * COLS, DEGREES), lambda i, s: (0, 0))] * 4 + [state],
            scratch_shapes=[pltpu.VMEM((8 * COLS, DEGREES), jnp.float32)],
        ),
        out_shape=[jax.ShapeDtypeStruct((8 * COLS, DEGREES), jnp.bfloat16)] * 4
        + [jax.ShapeDtypeStruct(it7.shape, jnp.float32)],
        compiler_params=pltpu.CompilerParams(vmem_limit_bytes=32 * MIB),
        cost_estimate=pl.CostEstimate(
            flops=8 * 32 * COLS * DEGREES, bytes_accessed=6 * MIB, transcendentals=0
        ),
        name="prepare",
    )(ids, quad, st7, it7, damp)


def split(x):
    high = x.astype(jnp.bfloat16)
    return high, (x - high.astype(jnp.float32)).astype(jnp.bfloat16)


def table_kernel(row1_ref, row2_ref, tab_ref, back_ref, keep_ref):
    first = lax.broadcasted_iota(jnp.int32, (1, 128), 1) == 0
    halve = jnp.where(first, 0.5, 1.0)
    for par in range(2):
        wave = (
            2 * lax.broadcasted_iota(jnp.int32, (1, HALF), 1) + par
        ).astype(jnp.float32) * (1.0 / MODES)

        def rows(j, _, par=par, wave=wave):
            lead_c = row1_ref[par, 0, pl.ds(j, 1), :]
            lead_s = row1_ref[par, 1, pl.ds(j, 1), :]
            cosine = lead_c * row2_ref[par, 0] - lead_s * row2_ref[par, 1]
            sine = lead_s * row2_ref[par, 0] + lead_c * row2_ref[par, 1]
            at = pl.ds(pl.multiple_of(16 * j, 16), 16)
            keep_ref[0, at, :] = cosine
            keep_ref[1, at, :] = sine
            for t, value in enumerate((cosine, sine, -wave * cosine, wave * sine)):
                high, low = split(value)
                tab_ref[4 * par + t, 0, at, :] = high
                tab_ref[4 * par + t, 1, at, :] = low
            return 0

        lax.fori_loop(0, ROWS // 16, rows, 0)
        for t in range(2):
            for block in range(4):
                cut = slice(128 * block, 128 * (block + 1))
                value = jnp.transpose(keep_ref[t, cut, :])
                if t == 1:
                    value = -value
                if block == 0:
                    value = value * halve
                high, low = split(value)
                back_ref[2 * par + t, 0, :, cut] = high
                back_ref[2 * par + t, 1, :, cut] = low


def small_tables():
    scale = 1.0 / math.sqrt(MODES)
    step = 2.0 * math.pi / POINTS
    rows1, rows2 = [], []
    for par in range(2):
        m = 2 * np.arange(HALF) + par

        def pair(k, factor):
            angle = ((k[:, None] * m[None, :]) % POINTS) * step
            return np.stack([np.cos(angle), np.sin(angle)]) * factor

        rows1.append(pair(16 * np.arange(ROWS // 16), 1.0))
        rows2.append(pair(np.arange(16), scale))
    return [np.stack(x).astype(np.float32) for x in (rows1, rows2)]


def tables(parts):
    return pl.pallas_call(
        table_kernel,
        out_shape=(
            jax.ShapeDtypeStruct((8, 2, ROWS, HALF), jnp.bfloat16),
            jax.ShapeDtypeStruct((4, 2, HALF, QUARTER), jnp.bfloat16),
        ),
        scratch_shapes=[pltpu.VMEM((2, ROWS, HALF), jnp.float32)],
        compiler_params=pltpu.CompilerParams(vmem_limit_bytes=48 * MIB),
        cost_estimate=pl.CostEstimate(
            flops=16 * ROWS * HALF, bytes_accessed=15 * MIB, transcendentals=0
        ),
        name="tables",
    )(*parts)


def grid_kernel(
    got_ref, tab_hbm, back_hbm, rows_ref,
    out_ref,
    tab_ref, back_ref, sems, x_ref, wave_ref, high_ref, low_ref, edge_ref,
):
    copies = [
        pltpu.make_async_copy(tab_hbm.at[t], tab_ref.at[t], sems.at[t]) for t in range(8)
    ] + [
        pltpu.make_async_copy(back_hbm.at[i], back_ref.at[i], sems.at[8 + i]) for i in range(4)
    ]
    for copy in copies[:3]:
        copy.start()
    for i in range(4):
        x_ref[i] = got_ref[:, i * PAIRS : (i + 1) * PAIRS, :].reshape(HALF, LANES)
    which = (0, 1, 1, 0, 2, 3, 3, 2)
    for t in range(8):
        copies[t].wait()
        copies[t + 3].start()
        x = x_ref[which[t]]
        wave_ref[t] = mm(tab_ref[t, 0], x) + mm(tab_ref[t, 1], x)
    copies[11].start()
    cor = rows_ref[0:1, :]

    def quads(base, at, lanes):
        ce, se = wave_ref[base, at, lanes], wave_ref[base + 1, at, lanes]
        co, so = wave_ref[base + 4, at, lanes], wave_ref[base + 5, at, lanes]
        a, b, s, d = ce + co, ce - co, se + so, se - so
        return a - s, b + d, b - d, a + s

    def tendency(at):
        cuts = [pl.ds(128 * f, 128) for f in range(3)]
        values = [quads(0, at, cut) for cut in cuts]
        slopes = [quads(2, at, cut) for cut in cuts]
        out = [[], [], []]
        for q in range(4):
            u, v, h = (values[f][q] for f in range(3))
            us, vs, hs = (slopes[f][q] for f in range(3))
            out[0].append(cor * v - u * us - hs)
            out[1].append(-u * vs - cor * u)
            out[2].append(-u * hs - (1.0 + h) * us)
        folded = []
        for t1, t2, t3, t4 in out:
            a, b, c, d = t1 + t4, t2 + t3, t1 - t4, t3 - t2
            folded.append((a + b, c + d, a - b, c - d))
        return folded

    def block(j, _):
        at = pl.ds(pl.multiple_of(16 * j, 16), 16)
        for f, folded in enumerate(tendency(at)):
            for i, value in enumerate(folded):
                high, low = split(value)
                high_ref[i, at, pl.ds(128 * f, 128)] = high
                low_ref[i, at, pl.ds(128 * f, 128)] = low
        return 0

    lax.fori_loop(0, QUARTER // 16, block, 0)
    for f, folded in enumerate(tendency(pl.ds(QUARTER, 16))):
        edge_ref[0, :, pl.ds(128 * f, 128)] = folded[0]
        edge_ref[1, :, pl.ds(128 * f, 128)] = folded[3]

    odd_row = (lax.broadcasted_iota(jnp.int32, (HALF, 1), 0) & 1) == 1
    half_scale = 0.5 / math.sqrt(MODES)
    sign = jnp.where(odd_row, -half_scale, half_scale)
    weight, signed = rows_ref[1:2, :], rows_ref[2:3, :]
    for par in range(2):
        both = []
        for c in range(2):
            i = 2 * par + c
            copies[8 + i].wait()
            out = mm(back_ref[i, 0], high_ref[i]) + mm(back_ref[i, 1], high_ref[i])
            out = out + mm(back_ref[i, 0], low_ref[i])
            if i == 0:
                out = out + sign * edge_ref[0, 0:1, :]
            if i == 3:
                out = out - sign * edge_ref[1, 0:1, :]
            both.append(out)
        for f in range(3):
            parts = []
            for out in both:
                part = out[:, 128 * f : 128 * (f + 1)]
                part = pltpu.roll(part, 64, 1) * weight + part * signed
                parts.append(part.reshape(NBAND, 2, 8, 128))
            joined = jnp.concatenate(parts, axis=2).astype(jnp.bfloat16)
            for h in range(2):
                z = 2 * par + h
                out_ref[z * NBAND : (z + 1) * NBAND, :, 128 * f : 128 * (f + 1)] = joined[:, h]


def grid_stage(got, tab, back, rows):
    return pl.pallas_call(
        grid_kernel,
        in_specs=[
            pl.BlockSpec(memory_space=pltpu.VMEM),
            pl.BlockSpec(memory_space=pl.ANY),
            pl.BlockSpec(memory_space=pl.ANY),
            pl.BlockSpec(memory_space=pltpu.VMEM),
        ],
        out_shape=jax.ShapeDtypeStruct((4 * NBAND, 16, LANES), jnp.bfloat16),
        scratch_shapes=[
            pltpu.VMEM((8, 2, ROWS, HALF), jnp.bfloat16),
            pltpu.VMEM((4, 2, HALF, QUARTER), jnp.bfloat16),
            pltpu.SemaphoreType.DMA((12,)),
            pltpu.VMEM((4, HALF, LANES), jnp.bfloat16),
            pltpu.VMEM((8, ROWS, LANES), jnp.float32),
            pltpu.VMEM((4, QUARTER, LANES), jnp.bfloat16),
            pltpu.VMEM((4, QUARTER, LANES), jnp.bfloat16),
            pltpu.VMEM((2, 16, LANES), jnp.float32),
        ],
        compiler_params=pltpu.CompilerParams(vmem_limit_bytes=48 * MIB),
        cost_estimate=pl.CostEstimate(
            flops=2 * 28 * ROWS * HALF * LANES, bytes_accessed=17 * MIB, transcendentals=0
        ),
        name="grid",
    )(got, tab, back, rows)


def analysis_kernel(
    id_ref, quad_ref, y_ref, leg_ref, move0_ref, move1_ref, move2_ref, move3_ref, st_ref, damp_ref,
    out0_ref, out1_ref, out2_ref, out3_ref, sums_ref,
    wide_ref, rate_ref, start_ref, mix_ref, acc_ref,
):
    step = pl.program_id(0)
    node = id_ref[0]
    order = [(node + 4 - s) % 4 for s in range(4)]

    @pl.when(step == 0)
    def _():
        acc_ref[...] = jnp.zeros_like(acc_ref)
        low = lax.broadcasted_iota(jnp.int32, (16, 128), 1) < 64
        for s in range(4):
            for f in range(3):
                for e in range(4):
                    for t in range(4):
                        first, second = (
                            y_ref[
                                order[s] * NBAND + 8 * e + 2 * t + g, :, 128 * f : 128 * (f + 1)
                            ].astype(jnp.float32)
                            for g in range(2)
                        )
                        symmetric = jnp.where(low, first, second)
                        antisymmetric = jnp.where(low, second, first)
                        for c in range(2):
                            row = (((s * 2 + c) * 3 + f) * 4 + e) * 8
                            wide_ref[0, t, row : row + 8, :] = symmetric[8 * c : 8 * c + 8]
                            wide_ref[1, t, row : row + 8, :] = antisymmetric[8 * c : 8 * c + 8]

    for k in range(MB):
        at = step * MB + k
        mode = 2 * (8 * (node % 2) + at) + node // 2
        for c in range(2):
            for f in range(3):
                row = (c * 3 + f) * 4
                rate_ref[pl.ds(row, 4), :] = jnp.broadcast_to(
                    damp_ref[f, pl.ds(mode, 1), :], (4, DEGREES)
                )
                start_ref[pl.ds(row, 4), :] = st_ref[c, k, f]
        halves = []
        for h in range(2):
            spec = jnp.concatenate(
                [wide_ref[h, t, pl.ds(at, 4 * COLS, stride=8), :] for t in range(4)], axis=1
            ).astype(jnp.bfloat16)
            if h == 0:
                table = leg_ref[k, :, :256]
            else:
                blocks = [leg_ref[k, 64 * (b ^ 1) : 64 * (b ^ 1) + 64, 256:] for b in range(8)]
                table = jnp.concatenate(blocks, axis=0)
            halves.append(mm(spec, table))
        for h in range(2):
            cut = slice(256 * h, 256 * (h + 1))
            rate, start = rate_ref[:, cut], start_ref[:, cut]
            moves = [
                decode(ref[k // 2, COLS * (k % 2) : COLS * (k % 2 + 1), cut])
                for ref in (move0_ref, move1_ref, move2_ref, move3_ref)
            ]
            forces = [
                halves[h][COLS * p : COLS * (p + 1)] - rate * moves[p] for p in range(4)
            ]
            change = jnp.zeros_like(start)
            for q in range(4):
                row = [quad_ref[order[q], order[p]] for p in range(4)]
                mine = row[q] * rate
                inverse = 1.0 / (1.0 + mine)
                mixed = (
                    row[0] * forces[0] + row[1] * forces[1] + row[2] * forces[2] + row[3] * forces[3]
                ) * inverse
                total = row[0] + row[1] + row[2] + row[3]
                old = start + moves[q]
                moved = mixed + (start * (1.0 - rate * total) + mine * old) * inverse - old
                change = change + moved * moved
                mix_ref[q, COLS * k : COLS * (k + 1), cut] = mixed
            acc_ref[0, :, cut] += change
            acc_ref[1, :, cut] += start * start
    for s, ref in enumerate((out0_ref, out1_ref, out2_ref, out3_ref)):
        ref[...] = encode(mix_ref[s])

    @pl.when(step == pl.num_programs(0) - 1)
    def _():
        field = lax.broadcasted_iota(jnp.int32, (COLS, 1), 0) // 4 % 3
        lane = lax.broadcasted_iota(jnp.int32, (1, 128), 1)
        sums = jnp.zeros((1, 128), jnp.float32)
        for s in range(2):
            per_row = jnp.sum(acc_ref[s], axis=1, keepdims=True)
            for f in range(3):
                value = jnp.sum(jnp.where(field == f, per_row, 0.0), axis=0, keepdims=True)
                sums = sums + jnp.where(lane == 3 * s + f, value, 0.0)
        sums_ref[...] = sums


def analysis(ids, quad, y, leg4, moves, st6, damp):
    spec = pl.BlockSpec
    return pl.pallas_call(
        analysis_kernel,
        grid_spec=pltpu.PrefetchScalarGridSpec(
            num_scalar_prefetch=1,
            grid=(2,),
            in_specs=[
                spec(memory_space=pltpu.SMEM),
                spec((4 * NBAND, 16, LANES), lambda i, s: (0, 0, 0)),
                spec(
                    (MB, None, LATS, DEGREES), lambda i, s: (s[0] % 2 * 2 + i, s[0] // 2, 0, 0)
                ),
                *[spec((2, 2 * COLS, DEGREES), lambda i, s: (i, 0, 0))] * 4,
                spec(
                    (2, MB, None, 3, 4, DEGREES),
                    lambda i, s: (0, s[0] % 2 * 2 + i, s[0] // 2, 0, 0, 0),
                ),
                spec((3, 32, DEGREES), lambda i, s: (0, 0, 0)),
            ],
            out_specs=(
                *[spec((MB * COLS, DEGREES), lambda i, s: (i, 0))] * 4,
                spec((1, 128), lambda i, s: (0, 0)),
            ),
            scratch_shapes=[
                pltpu.VMEM((2, 4, 4 * COLS * 8, 128), jnp.float32),
                pltpu.VMEM((COLS, DEGREES), jnp.float32),
                pltpu.VMEM((COLS, DEGREES), jnp.float32),
                pltpu.VMEM((4, MB * COLS, DEGREES), jnp.float32),
                pltpu.VMEM((2, COLS, DEGREES), jnp.float32),
            ],
        ),
        out_shape=(
            *[jax.ShapeDtypeStruct((8 * COLS, DEGREES), jnp.bfloat16)] * 4,
            jax.ShapeDtypeStruct((1, 128), jnp.float32),
        ),
        compiler_params=pltpu.CompilerParams(vmem_limit_bytes=56 * MIB),
        cost_estimate=pl.CostEstimate(
            flops=2 * 32 * COLS * LATS * DEGREES, bytes_accessed=10 * MIB, transcendentals=0
        ),
        name="analysis",
    )(ids, quad, y, leg4, *moves, st6, damp)


def update_kernel(
    id_ref, mixed0_ref, mixed1_ref, mixed2_ref, mixed3_ref, base_ref, out_ref, mix_ref
):
    place = pl.program_id(0)
    for s, ref in enumerate((mixed0_ref, mixed1_ref, mixed2_ref, mixed3_ref)):

        @pl.when(place == s)
        def _(ref=ref):
            mix_ref[...] = decode(ref[...])

    for k in range(8):
        for c in range(2):
            for f in range(3):
                row = COLS * k + (c * 3 + f) * 4
                out_ref[c, k, f] = base_ref[c, k, f] + mix_ref[row : row + 4, :]


def update(ids, mixed, base):
    spec = pl.BlockSpec
    state = spec(STATE, own_subset)
    return pl.pallas_call(
        update_kernel,
        grid_spec=pltpu.PrefetchScalarGridSpec(
            num_scalar_prefetch=1,
            grid=(4,),
            in_specs=[*[spec((8 * COLS, DEGREES), lambda i, s: (0, 0))] * 4, state],
            out_specs=state,
            scratch_shapes=[pltpu.VMEM((8 * COLS, DEGREES), jnp.float32)],
        ),
        out_shape=jax.ShapeDtypeStruct(base.shape, jnp.float32),
        compiler_params=pltpu.CompilerParams(vmem_limit_bytes=32 * MIB),
        cost_estimate=pl.CostEstimate(
            flops=4 * 32 * COLS * DEGREES, bytes_accessed=5 * MIB, transcendentals=0
        ),
        name="update",
    )(ids, *mixed, base)


def exchange(x, axes):
    return lax.all_to_all(x, axes, split_axis=0, concat_axis=0, tiled=True)


def shift(x, axis, by):
    return lax.ppermute(x, axis, [(i, (i + by) % 4) for i in range(4)])


def latitude_rows(band, coriolis, lat_weight):
    count = LATS // 8
    group = band % 8
    cor = lax.dynamic_slice_in_dim(coriolis, group * count, count, 1)
    weight = lax.dynamic_slice_in_dim(lat_weight, group * count, count, 0)
    swapped = group % 2 == 1
    cor = jnp.where(swapped, cor[::-1], cor).reshape(1, 128)
    weight = jnp.concatenate([weight, weight])[None]
    south = lax.broadcasted_iota(jnp.int32, (1, 128), 1) >= count
    signed = jnp.where(south != swapped, -weight, weight)
    return jnp.concatenate([cor, weight, signed], axis=0)


def body(state0, iterate, legendre, lat_weight, coriolis, damping, quadrature):
    node = lax.axis_index("node")
    band = lax.axis_index(BAND)
    spec = iterate[0].transpose(0, 1, 3, 2, 4)
    base = state0.transpose(0, 1, 3, 2, 4)
    it6 = spec.reshape(2, PAIRS, 2, 3, 4, DEGREES)
    st6 = base.reshape(2, PAIRS, 2, 3, 4, DEGREES)
    leg4 = legendre.reshape(PAIRS, 2, LATS, DEGREES)
    damp = damping.transpose(1, 0, 2)
    ids = jnp.reshape(node, (1,)).astype(jnp.int32)

    shape7 = (2, 2, 8, 2, 3, 4, DEGREES)
    sent = synthesis(it6, leg4)
    got = exchange(sent, BAND)
    parts = [jnp.asarray(x) for x in small_tables()]
    late, _ = lax.optimization_barrier(((parts, quadrature), sent))
    parts, quad = late
    *moves, settled = prepare(ids, quad, base.reshape(shape7), spec.reshape(shape7), damp)
    moves = [moves[0]] + [shift(moves[s], "node", s) for s in (1, 2, 3)]
    tab, back = tables(parts)
    rows = latitude_rows(band, coriolis, lat_weight)
    rows, moves = lax.optimization_barrier((rows, moves))
    moves = [x.reshape(4, 2 * COLS, DEGREES) for x in moves]
    spectra = exchange(grid_stage(got, tab, back, rows), NODE_BAND)
    *mixed, sums = analysis(ids, quadrature, spectra, leg4, moves, st6, damp)
    mixed = [mixed[0]] + [shift(mixed[s], "node", -s) for s in (1, 2, 3)]
    sums = exchange(jnp.broadcast_to(sums[None], (4 * NBAND, 1, 128)), NODE_BAND)
    out = update(ids, mixed, settled)
    sums, out = lax.optimization_barrier((sums, out))
    total = jnp.sum(sums, axis=(0, 1))
    ratio = jnp.sqrt(total[:3] / (4.0 * total[3:6] + 1e-06))
    out = out.reshape(2, 32, 3, 4, DEGREES).transpose(0, 1, 3, 2, 4)
    return (out[None], ratio)


def solution(mesh):
    torus = Mesh(
        mesh.devices.reshape(mesh.shape["node"], 4, 4, 2), ("node", "band_0", "band_1", "band_2")
    )
    return jax.shard_map(
        body,
        mesh=torus,
        in_specs=(
            P(None, BAND, None, None, None),
            P("node", None, BAND, None, None, None),
            P(BAND, None, None),
            P(),
            P(),
            P(BAND, None, None),
            P(),
        ),
        out_specs=(P("node", None, BAND, None, None, None), P()),
        check_vma=False,
    )
```

```python
import functools
import math

import jax
import jax.numpy as jnp
import numpy as np
from jax import lax
from jax.experimental import pallas as pl
from jax.experimental.pallas import tpu as pltpu
from jax.sharding import Mesh
from jax.sharding import PartitionSpec as P

BAND = ("band_0", "band_1", "band_2")
SEND = ("band_2", "band_1", "band_0")
SEND_NODE = SEND + ("node",)
MODES = 1024
POINTS = 2 * MODES
HALF = MODES // 2
QUARTER = POINTS // 4
ROWS = QUARTER + 16
LATS = 512
DEGREES = 512
NBAND = 32
PAIRS = 16
COLS = 24
LANES = 384
MB = 4
MIB = 1 << 20


NT = (((1,), (1,)), ((), ()))


def mm(a, b):
    return jnp.dot(a, b, preferred_element_type=jnp.float32)


STREAMS = 16


def synthesis_kernel(it_hbm, leg_hbm, out_ref, it_ref, leg_ref, sems, coef_ref, turn_ref, wide_ref):
    def stream(j):
        return pltpu.make_async_copy(
            leg_hbm.at[pl.ds(j % 8 * 2, 2), j // 8], leg_ref.at[j], sems.at[j]
        )

    coefficients = pltpu.make_async_copy(it_hbm, it_ref, sems.at[STREAMS])
    coefficients.start()
    for j in range(STREAMS):
        stream(j).start()
    coefficients.wait()
    low = lax.broadcasted_iota(jnp.int32, (COLS, 128), 1) < 64

    left = lax.broadcasted_iota(jnp.int32, (LATS, 128), 1) < 64

    def place(at, t, north, south):
        south = pltpu.roll(south, 64, 1)
        rows = pl.ds(at, COLS, stride=2 * PAIRS)
        wide_ref[2 * t, rows, :] = jnp.where(low, north, south)
        wide_ref[2 * t + 1, rows, :] = jnp.where(low, south, north)

    def four(j, _):
        stream(2 * j).wait()
        stream(2 * j + 1).wait()
        par, first = j // 4, j % 4 * 4
        at = par * PAIRS + first
        for k in range(4):
            for c in range(2):
                for f in range(3):
                    row = (c * 3 + f) * 4
                    value = it_ref[c, first + k, par, f]
                    if k < 2:
                        coef_ref[k, row : row + 4, :] = value
                    else:
                        row += 64 * (k - 2)
                        turn_ref[row : row + 4, :] = value
                        turn_ref[row + 32 : row + 36, :256] = value[:, :256]
                        turn_ref[row + 32 : row + 36, 256:] = -value[:, 256:]
        turned = jnp.transpose(turn_ref[...]).astype(jnp.bfloat16)
        both = jnp.where(
            left, mm(leg_ref[2 * j + 1, 0], turned), mm(leg_ref[2 * j + 1, 1], turned)
        )
        for k in range(2):
            coeff = coef_ref[k].astype(jnp.bfloat16)
            even = lax.dot_general(
                coeff[:, :256], leg_ref[2 * j, k, :, :256], NT, preferred_element_type=jnp.float32
            )
            odd = lax.dot_general(
                coeff[:, 256:], leg_ref[2 * j, k, :, 256:], NT, preferred_element_type=jnp.float32
            )
            for t in range(4):
                cut = slice(128 * t, 128 * (t + 1))
                place(at + k, t, even[:, cut] + odd[:, cut], even[:, cut] - odd[:, cut])
        for t in range(4):
            block = jnp.transpose(both[128 * t : 128 * (t + 1)])
            for k in range(2):
                north = block[64 * k : 64 * k + COLS]
                place(at + 2 + k, t, north, block[64 * k + 32 : 64 * k + 32 + COLS])
        return 0

    lax.fori_loop(0, STREAMS // 2, four, 0)
    for p in range(2):
        for c in range(2):
            for f in range(3):
                for e in range(4):
                    row = (((c * 3 + f) * 4 + e) * 2 + p) * PAIRS
                    out_ref[
                        8 * e : 8 * e + 8,
                        (2 * p + c) * PAIRS : (2 * p + c + 1) * PAIRS,
                        128 * f : 128 * (f + 1),
                    ] = wide_ref[:, row : row + PAIRS, :].astype(jnp.bfloat16)


def synthesis(it6, leg4):
    return pl.pallas_call(
        synthesis_kernel,
        in_specs=[pl.BlockSpec(memory_space=pl.ANY)] * 2,
        out_shape=jax.ShapeDtypeStruct((NBAND, 4 * PAIRS, LANES), jnp.bfloat16),
        scratch_shapes=[
            pltpu.VMEM(it6.shape, jnp.float32),
            pltpu.VMEM((STREAMS, 2, LATS, DEGREES), jnp.bfloat16),
            pltpu.SemaphoreType.DMA((STREAMS + 1,)),
            pltpu.VMEM((2, COLS, DEGREES), jnp.float32),
            pltpu.VMEM((128, DEGREES), jnp.float32),
            pltpu.VMEM((8, COLS * 2 * PAIRS, 128), jnp.float32),
        ],
        compiler_params=pltpu.CompilerParams(vmem_limit_bytes=56 * MIB),
        cost_estimate=pl.CostEstimate(
            flops=2 * 32 * COLS * LATS * DEGREES, bytes_accessed=20 * MIB, transcendentals=0
        ),
        name="synthesis",
    )(it6, leg4)


def encode(x):
    return (x * jnp.abs(x)).astype(jnp.bfloat16)


def decode(coded):
    coded = coded.astype(jnp.float32)
    root = jnp.sqrt(jnp.abs(coded))
    return jnp.where(coded < 0, -root, root)


def prepare_kernel(
    id_ref, quad_ref, st_ref, it_ref, damp_ref,
    send0_ref, send1_ref, send2_ref, send3_ref, base_ref, dense_ref,
):
    node = id_ref[0]
    place = pl.program_id(0)
    z = (node + place) % 4
    total = quad_ref[node, 0] + quad_ref[node, 1] + quad_ref[node, 2] + quad_ref[node, 3]
    diag = quad_ref[node, node]
    for k in range(8):
        mode = 2 * (8 * (z % 2) + k) + z // 2
        for f in range(3):
            rate = damp_ref[f, pl.ds(mode, 1), :]
            mine = diag * rate
            inverse = 1.0 / (1.0 + mine)
            keep = (1.0 - rate * total) * inverse
            mine = mine * inverse
            for c in range(2):
                row = COLS * k + (c * 3 + f) * 4
                start, old = st_ref[c, k, f], it_ref[c, k, f]
                dense_ref[row : row + 4, :] = old - start
                base_ref[c, k, f] = start * keep + mine * old
    for s, ref in enumerate((send0_ref, send1_ref, send2_ref, send3_ref)):

        @pl.when(place == s)
        def _(ref=ref):
            ref[...] = encode(dense_ref[...])


def own_subset(i, s):
    z = (s[0] + i) % 4
    return (0, z % 2, 0, z // 2, 0, 0, 0)


STATE = (2, None, 8, None, 3, 4, DEGREES)


def prepare(ids, quad, st7, it7, damp):
    spec = pl.BlockSpec
    state = spec(STATE, own_subset)
    return pl.pallas_call(
        prepare_kernel,
        grid_spec=pltpu.PrefetchScalarGridSpec(
            num_scalar_prefetch=1,
            grid=(4,),
            in_specs=[
                spec(memory_space=pltpu.SMEM),
                state,
                state,
                spec((3, 32, DEGREES), lambda i, s: (0, 0, 0)),
            ],
            out_specs=[spec((8 * COLS, DEGREES), lambda i, s: (0, 0))] * 4 + [state],
            scratch_shapes=[pltpu.VMEM((8 * COLS, DEGREES), jnp.float32)],
        ),
        out_shape=[jax.ShapeDtypeStruct((8 * COLS, DEGREES), jnp.bfloat16)] * 4
        + [jax.ShapeDtypeStruct(it7.shape, jnp.float32)],
        compiler_params=pltpu.CompilerParams(vmem_limit_bytes=32 * MIB),
        cost_estimate=pl.CostEstimate(
            flops=8 * 32 * COLS * DEGREES, bytes_accessed=6 * MIB, transcendentals=0
        ),
        name="prepare",
    )(ids, quad, st7, it7, damp)


def split(x):
    high = x.astype(jnp.bfloat16)
    return high, (x - high.astype(jnp.float32)).astype(jnp.bfloat16)


def table_kernel(row1_ref, row2_ref, wave_ref, tab_ref, back_ref, keep_ref):
    first = lax.broadcasted_iota(jnp.int32, (1, 128), 1) == 0
    halve = jnp.where(first, 0.5, 1.0)
    for par in range(2):
        wave = wave_ref[par]

        def rows(j, _, par=par, wave=wave):
            lead_c = row1_ref[par, 0, pl.ds(j, 1), :]
            lead_s = row1_ref[par, 1, pl.ds(j, 1), :]
            cosine = lead_c * row2_ref[par, 0] - lead_s * row2_ref[par, 1]
            sine = lead_s * row2_ref[par, 0] + lead_c * row2_ref[par, 1]
            at = pl.ds(pl.multiple_of(16 * j, 16), 16)
            keep_ref[0, at, :] = cosine
            keep_ref[1, at, :] = sine
            for t, value in enumerate((cosine, sine, -wave * cosine, wave * sine)):
                high, low = split(value)
                tab_ref[4 * par + t, 0, at, :] = high
                tab_ref[4 * par + t, 1, at, :] = low
            return 0

        lax.fori_loop(0, ROWS // 16, rows, 0)
        for t in range(2):
            for block in range(4):
                cut = slice(128 * block, 128 * (block + 1))
                value = jnp.transpose(keep_ref[t, cut, :])
                if t == 1:
                    value = -value
                if block == 0:
                    value = value * halve
                high, low = split(value)
                back_ref[2 * par + t, 0, :, cut] = high
                back_ref[2 * par + t, 1, :, cut] = low


def small_tables():
    scale = 1.0 / math.sqrt(MODES)
    step = 2.0 * math.pi / POINTS
    rows1, rows2, waves = [], [], []
    place = np.arange(NBAND)
    block = place % 4 * 8 + place // 4 % 4 * 2 + place // 16
    pairs = (block[:, None] * PAIRS + np.arange(PAIRS)).reshape(-1)
    for par in range(2):
        m = 2 * pairs + par

        def pair(k, factor):
            angle = ((k[:, None] * m[None, :]) % POINTS) * step
            return np.stack([np.cos(angle), np.sin(angle)]) * factor

        rows1.append(pair(16 * np.arange(ROWS // 16), 1.0))
        rows2.append(pair(np.arange(16), scale))
        waves.append(m[None, :] / MODES)
    return [np.stack(x).astype(np.float32) for x in (rows1, rows2, waves)]


def tables(parts):
    return pl.pallas_call(
        table_kernel,
        out_shape=(
            jax.ShapeDtypeStruct((8, 2, ROWS, HALF), jnp.bfloat16),
            jax.ShapeDtypeStruct((4, 2, HALF, QUARTER), jnp.bfloat16),
        ),
        scratch_shapes=[pltpu.VMEM((2, ROWS, HALF), jnp.float32)],
        compiler_params=pltpu.CompilerParams(vmem_limit_bytes=48 * MIB),
        cost_estimate=pl.CostEstimate(
            flops=16 * ROWS * HALF, bytes_accessed=15 * MIB, transcendentals=0
        ),
        name="tables",
    )(*parts)


def grid_kernel(
    got_ref, tab_hbm, back_hbm, rows_ref,
    out_ref,
    tab_ref, back_ref, sems, x_ref, wave_ref, fold_ref, edge_ref,
):
    copies = [
        pltpu.make_async_copy(tab_hbm.at[t], tab_ref.at[t], sems.at[t]) for t in range(8)
    ] + [
        pltpu.make_async_copy(back_hbm.at[i], back_ref.at[i], sems.at[8 + i]) for i in range(4)
    ]
    for copy in copies:
        copy.start()
    for i in range(4):
        x_ref[i] = got_ref[:, i * PAIRS : (i + 1) * PAIRS, :].reshape(HALF, LANES)
    which = (0, 1, 1, 0, 2, 3, 3, 2)
    for t in range(8):
        copies[t].wait()
        x = x_ref[which[t]]
        wave_ref[t] = mm(tab_ref[t, 0], x) + mm(tab_ref[t, 1], x)
    cor = rows_ref[0:1, :]

    def quads(base, at, lanes):
        ce, se = wave_ref[base, at, lanes], wave_ref[base + 1, at, lanes]
        co, so = wave_ref[base + 4, at, lanes], wave_ref[base + 5, at, lanes]
        a, b, s, d = ce + co, ce - co, se + so, se - so
        return a - s, b + d, b - d, a + s

    def tendency(at):
        cuts = [pl.ds(128 * f, 128) for f in range(3)]
        values = [quads(0, at, cut) for cut in cuts]
        slopes = [quads(2, at, cut) for cut in cuts]
        out = [[], [], []]
        for q in range(4):
            u, v, h = (values[f][q] for f in range(3))
            us, vs, hs = (slopes[f][q] for f in range(3))
            out[0].append(cor * v - u * us - hs)
            out[1].append(-u * vs - cor * u)
            out[2].append(-u * hs - (1.0 + h) * us)
        folded = []
        for t1, t2, t3, t4 in out:
            a, b, c, d = t1 + t4, t2 + t3, t1 - t4, t3 - t2
            folded.append((a + b, c + d, a - b, c - d))
        return folded

    def block(j, _):
        at = pl.ds(pl.multiple_of(16 * j, 16), 16)
        for f, folded in enumerate(tendency(at)):
            for i, value in enumerate(folded):
                high, low = split(value)
                fold_ref[i, at, pl.ds(128 * f, 128)] = high
                fold_ref[i, at, pl.ds(LANES + 128 * f, 128)] = low
        return 0

    lax.fori_loop(0, QUARTER // 16, block, 0)
    for f, folded in enumerate(tendency(pl.ds(QUARTER, 16))):
        edge_ref[0, :, pl.ds(128 * f, 128)] = folded[0]
        edge_ref[1, :, pl.ds(128 * f, 128)] = folded[3]

    odd_row = (lax.broadcasted_iota(jnp.int32, (HALF, 1), 0) & 1) == 1
    half_scale = 0.5 / math.sqrt(MODES)
    sign = jnp.where(odd_row, -half_scale, half_scale)
    weight, signed = rows_ref[1:2, :], rows_ref[2:3, :]
    for par in range(2):
        both = []
        for c in range(2):
            i = 2 * par + c
            copies[8 + i].wait()
            both_parts = mm(back_ref[i, 0], fold_ref[i])
            out = both_parts[:, :LANES] + both_parts[:, LANES:]
            out = out + mm(back_ref[i, 1], fold_ref[i, :, :LANES])
            if i == 0:
                out = out + sign * edge_ref[0, 0:1, :]
            if i == 3:
                out = out - sign * edge_ref[1, 0:1, :]
            both.append(out)
        for f in range(3):
            parts = []
            for out in both:
                part = out[:, 128 * f : 128 * (f + 1)]
                part = pltpu.roll(part, 64, 1) * weight + part * signed
                parts.append(part.reshape(NBAND, 2, 8, 128))
            joined = jnp.concatenate(parts, axis=2).astype(jnp.bfloat16)
            for h in range(2):
                out_ref[:, 2 * par + h, :, 128 * f : 128 * (f + 1)] = joined[:, h]


def grid_stage(got, tab, back, rows):
    return pl.pallas_call(
        grid_kernel,
        in_specs=[
            pl.BlockSpec(memory_space=pltpu.VMEM),
            pl.BlockSpec(memory_space=pl.ANY),
            pl.BlockSpec(memory_space=pl.ANY),
            pl.BlockSpec(memory_space=pltpu.VMEM),
        ],
        out_shape=jax.ShapeDtypeStruct((NBAND, 4, 16, LANES), jnp.bfloat16),
        scratch_shapes=[
            pltpu.VMEM((8, 2, ROWS, HALF), jnp.bfloat16),
            pltpu.VMEM((4, 2, HALF, QUARTER), jnp.bfloat16),
            pltpu.SemaphoreType.DMA((12,)),
            pltpu.VMEM((4, HALF, LANES), jnp.bfloat16),
            pltpu.VMEM((8, ROWS, LANES), jnp.float32),
            pltpu.VMEM((4, QUARTER, 2 * LANES), jnp.bfloat16),
            pltpu.VMEM((2, 16, LANES), jnp.float32),
        ],
        compiler_params=pltpu.CompilerParams(vmem_limit_bytes=48 * MIB),
        cost_estimate=pl.CostEstimate(
            flops=2 * 28 * ROWS * HALF * LANES, bytes_accessed=17 * MIB, transcendentals=0
        ),
        name="grid",
    )(got, tab, back, rows)


def analysis_kernel(
    id_ref, quad_ref, y_ref, leg_ref, move0_ref, move1_ref, move2_ref, move3_ref, st_ref, damp_ref,
    out0_ref, out1_ref, out2_ref, out3_ref, sums_ref,
    wide_ref, rate_ref, start_ref, mix_ref, acc_ref,
):
    step = pl.program_id(0)
    node = id_ref[0]
    order = [(node + 4 - s) % 4 for s in range(4)]

    @pl.when(step == 0)
    def _():
        acc_ref[...] = jnp.zeros_like(acc_ref)
        low = lax.broadcasted_iota(jnp.int32, (16, 128), 1) < 64
        for s in range(4):
            for f in range(3):
                for e in range(4):
                    for t in range(4):
                        first, second = (
                            y_ref[
                                (8 * e + 2 * t + g) * 4 + order[s], :, 128 * f : 128 * (f + 1)
                            ].astype(jnp.float32)
                            for g in range(2)
                        )
                        symmetric = jnp.where(low, first, second)
                        antisymmetric = jnp.where(low, second, first)
                        for c in range(2):
                            row = (((s * 2 + c) * 3 + f) * 4 + e) * 8
                            wide_ref[0, t, row : row + 8, :] = symmetric[8 * c : 8 * c + 8]
                            wide_ref[1, t, row : row + 8, :] = antisymmetric[8 * c : 8 * c + 8]

    for k in range(MB):
        at = step * MB + k
        mode = 2 * (8 * (node % 2) + at) + node // 2
        for c in range(2):
            for f in range(3):
                row = (c * 3 + f) * 4
                rate_ref[pl.ds(row, 4), :] = jnp.broadcast_to(
                    damp_ref[f, pl.ds(mode, 1), :], (4, DEGREES)
                )
                start_ref[pl.ds(row, 4), :] = st_ref[c, k, f]
        halves = []
        for h in range(2):
            spec = jnp.concatenate(
                [wide_ref[h, t, pl.ds(at, 4 * COLS, stride=8), :] for t in range(4)], axis=1
            ).astype(jnp.bfloat16)
            if h == 0:
                table = leg_ref[k, :, :256]
            else:
                blocks = [leg_ref[k, 64 * (b ^ 1) : 64 * (b ^ 1) + 64, 256:] for b in range(8)]
                table = jnp.concatenate(blocks, axis=0)
            halves.append(mm(spec, table))
        for h in range(2):
            cut = slice(256 * h, 256 * (h + 1))
            rate, start = rate_ref[:, cut], start_ref[:, cut]
            moves = [
                decode(ref[k // 2, COLS * (k % 2) : COLS * (k % 2 + 1), cut])
                for ref in (move0_ref, move1_ref, move2_ref, move3_ref)
            ]
            forces = [
                halves[h][COLS * p : COLS * (p + 1)] - rate * moves[p] for p in range(4)
            ]
            change = jnp.zeros_like(start)
            for q in range(4):
                row = [quad_ref[order[q], order[p]] for p in range(4)]
                mine = row[q] * rate
                inverse = 1.0 / (1.0 + mine)
                mixed = (
                    row[0] * forces[0] + row[1] * forces[1] + row[2] * forces[2] + row[3] * forces[3]
                ) * inverse
                total = row[0] + row[1] + row[2] + row[3]
                old = start + moves[q]
                moved = mixed + (start * (1.0 - rate * total) + mine * old) * inverse - old
                change = change + moved * moved
                mix_ref[q, COLS * k : COLS * (k + 1), cut] = mixed
            acc_ref[0, :, cut] += change
            acc_ref[1, :, cut] += start * start
    for s, ref in enumerate((out0_ref, out1_ref, out2_ref, out3_ref)):
        ref[...] = encode(mix_ref[s])

    @pl.when(step == pl.num_programs(0) - 1)
    def _():
        field = lax.broadcasted_iota(jnp.int32, (COLS, 1), 0) // 4 % 3
        lane = lax.broadcasted_iota(jnp.int32, (1, 128), 1)
        sums = jnp.zeros((1, 128), jnp.float32)
        for s in range(2):
            per_row = jnp.sum(acc_ref[s], axis=1, keepdims=True)
            for f in range(3):
                value = jnp.sum(jnp.where(field == f, per_row, 0.0), axis=0, keepdims=True)
                sums = sums + jnp.where(lane == 3 * s + f, value, 0.0)
        sums_ref[...] = jnp.broadcast_to(sums[None], sums_ref.shape)


def analysis(ids, quad, y, leg4, moves, st6, damp):
    spec = pl.BlockSpec
    return pl.pallas_call(
        analysis_kernel,
        grid_spec=pltpu.PrefetchScalarGridSpec(
            num_scalar_prefetch=1,
            grid=(2,),
            in_specs=[
                spec(memory_space=pltpu.SMEM),
                spec((4 * NBAND, 16, LANES), lambda i, s: (0, 0, 0)),
                spec(
                    (MB, None, LATS, DEGREES), lambda i, s: (s[0] % 2 * 2 + i, s[0] // 2, 0, 0)
                ),
                *[spec((2, 2 * COLS, DEGREES), lambda i, s: (i, 0, 0))] * 4,
                spec(
                    (2, MB, None, 3, 4, DEGREES),
                    lambda i, s: (0, s[0] % 2 * 2 + i, s[0] // 2, 0, 0, 0),
                ),
                spec((3, 32, DEGREES), lambda i, s: (0, 0, 0)),
            ],
            out_specs=(
                *[spec((MB * COLS, DEGREES), lambda i, s: (i, 0))] * 4,
                spec((4 * NBAND, 1, 128), lambda i, s: (0, 0, 0)),
            ),
            scratch_shapes=[
                pltpu.VMEM((2, 4, 4 * COLS * 8, 128), jnp.float32),
                pltpu.VMEM((COLS, DEGREES), jnp.float32),
                pltpu.VMEM((COLS, DEGREES), jnp.float32),
                pltpu.VMEM((4, MB * COLS, DEGREES), jnp.float32),
                pltpu.VMEM((2, COLS, DEGREES), jnp.float32),
            ],
        ),
        out_shape=(
            *[jax.ShapeDtypeStruct((8 * COLS, DEGREES), jnp.bfloat16)] * 4,
            jax.ShapeDtypeStruct((4 * NBAND, 1, 128), jnp.float32),
        ),
        compiler_params=pltpu.CompilerParams(vmem_limit_bytes=56 * MIB),
        cost_estimate=pl.CostEstimate(
            flops=2 * 32 * COLS * LATS * DEGREES, bytes_accessed=10 * MIB, transcendentals=0
        ),
        name="analysis",
    )(ids, quad, y, leg4, *moves, st6, damp)


def update_kernel(
    id_ref, mixed0_ref, mixed1_ref, mixed2_ref, mixed3_ref, base_ref, out_ref, mix_ref
):
    place = pl.program_id(0)
    for s, ref in enumerate((mixed0_ref, mixed1_ref, mixed2_ref, mixed3_ref)):

        @pl.when(place == s)
        def _(ref=ref):
            mix_ref[...] = decode(ref[...])

    for k in range(8):
        for c in range(2):
            for f in range(3):
                row = COLS * k + (c * 3 + f) * 4
                out_ref[c, k, f] = base_ref[c, k, f] + mix_ref[row : row + 4, :]


def update(ids, mixed, base):
    spec = pl.BlockSpec
    state = spec(STATE, own_subset)
    return pl.pallas_call(
        update_kernel,
        grid_spec=pltpu.PrefetchScalarGridSpec(
            num_scalar_prefetch=1,
            grid=(4,),
            in_specs=[*[spec((8 * COLS, DEGREES), lambda i, s: (0, 0))] * 4, state],
            out_specs=state,
            scratch_shapes=[pltpu.VMEM((8 * COLS, DEGREES), jnp.float32)],
        ),
        out_shape=jax.ShapeDtypeStruct(base.shape, jnp.float32),
        compiler_params=pltpu.CompilerParams(vmem_limit_bytes=32 * MIB),
        cost_estimate=pl.CostEstimate(
            flops=4 * 32 * COLS * DEGREES, bytes_accessed=5 * MIB, transcendentals=0
        ),
        name="update",
    )(ids, *mixed, base)


def exchange(x, axes):
    return lax.all_to_all(x, axes, split_axis=0, concat_axis=0, tiled=True)


def shift(x, axis, by):
    return lax.ppermute(x, axis, [(i, (i + by) % 4) for i in range(4)])


def latitude_rows(place, coriolis, lat_weight):
    count = LATS // 8
    group = place % 8
    cor = lax.dynamic_slice_in_dim(coriolis, group * count, count, 1)
    weight = lax.dynamic_slice_in_dim(lat_weight, group * count, count, 0)
    swapped = group % 2 == 1
    cor = jnp.where(swapped, cor[::-1], cor).reshape(1, 128)
    weight = jnp.concatenate([weight, weight])[None]
    south = lax.broadcasted_iota(jnp.int32, (1, 128), 1) >= count
    signed = jnp.where(south != swapped, -weight, weight)
    return jnp.concatenate([cor, weight, signed], axis=0)


def body(state0, iterate, legendre, lat_weight, coriolis, damping, quadrature):
    node = lax.axis_index("node")
    place = lax.axis_index(SEND)
    spec = iterate[0].transpose(0, 1, 3, 2, 4)
    base = state0.transpose(0, 1, 3, 2, 4)
    it6 = spec.reshape(2, PAIRS, 2, 3, 4, DEGREES)
    st6 = base.reshape(2, PAIRS, 2, 3, 4, DEGREES)
    leg4 = legendre.reshape(PAIRS, 2, LATS, DEGREES)
    damp = damping.transpose(1, 0, 2)
    ids = jnp.reshape(node, (1,)).astype(jnp.int32)

    shape7 = (2, 2, 8, 2, 3, 4, DEGREES)
    sent = synthesis(it6, leg4)
    got = exchange(sent, SEND)
    parts = [jnp.asarray(x) for x in small_tables()]
    late, _ = lax.optimization_barrier(((parts, quadrature), sent))
    parts, quad = late
    *moves, settled = prepare(ids, quad, base.reshape(shape7), spec.reshape(shape7), damp)
    moves = [moves[0]] + [shift(moves[s], "node", s) for s in (1, 2, 3)]
    tab, back = tables(parts)
    rows = latitude_rows(place, coriolis, lat_weight)
    rows, moves = lax.optimization_barrier((rows, moves))
    moves = [x.reshape(4, 2 * COLS, DEGREES) for x in moves]
    columns = grid_stage(got, tab, back, rows)
    spectra = exchange(columns.reshape(4 * NBAND, 16, LANES), SEND_NODE)
    *mixed, sums = analysis(ids, quadrature, spectra, leg4, moves, st6, damp)
    mixed = [mixed[0]] + [shift(mixed[s], "node", -s) for s in (1, 2, 3)]
    sums = exchange(sums, SEND_NODE)
    out = update(ids, mixed, settled)
    sums, out = lax.optimization_barrier((sums, out))
    total = jnp.sum(sums, axis=(0, 1))
    ratio = jnp.sqrt(total[:3] / (4.0 * total[3:6] + 1e-06))
    out = out.reshape(2, 32, 3, 4, DEGREES).transpose(0, 1, 3, 2, 4)
    return (out[None], ratio)


def solution(mesh):
    torus = Mesh(
        mesh.devices.reshape(mesh.shape["node"], 4, 4, 2), ("node", "band_0", "band_1", "band_2")
    )
    return jax.shard_map(
        body,
        mesh=torus,
        in_specs=(
            P(None, BAND, None, None, None),
            P("node", None, BAND, None, None, None),
            P(BAND, None, None),
            P(),
            P(),
            P(BAND, None, None),
            P(),
        ),
        out_specs=(P("node", None, BAND, None, None, None), P()),
        check_vma=False,
    )
```

```python
import functools
import math

import jax
import jax.numpy as jnp
import numpy as np
from jax import lax
from jax.experimental import pallas as pl
from jax.experimental.pallas import tpu as pltpu
from jax.sharding import Mesh
from jax.sharding import PartitionSpec as P

BAND = ("band_0", "band_1", "band_2")
SEND = ("band_2", "band_1", "band_0")
SEND_NODE = SEND + ("node",)
MODES = 1024
POINTS = 2 * MODES
HALF = MODES // 2
QUARTER = POINTS // 4
ROWS = QUARTER + 16
LATS = 512
DEGREES = 512
NBAND = 32
PAIRS = 16
COLS = 24
LANES = 384
MB = 4
MIB = 1 << 20


NT = (((1,), (1,)), ((), ()))


def mm(a, b):
    return jnp.dot(a, b, preferred_element_type=jnp.float32)


STREAMS = 16


def synthesis_kernel(it_hbm, leg_hbm, out_ref, it_ref, leg_ref, sems, coef_ref, turn_ref, wide_ref):
    def stream(j):
        return pltpu.make_async_copy(
            leg_hbm.at[pl.ds(j % 8 * 2, 2), j // 8], leg_ref.at[j], sems.at[j]
        )

    coefficients = pltpu.make_async_copy(it_hbm, it_ref, sems.at[STREAMS])
    coefficients.start()
    for j in range(STREAMS):
        stream(j).start()
    coefficients.wait()
    low = lax.broadcasted_iota(jnp.int32, (COLS, 128), 1) < 64

    left = lax.broadcasted_iota(jnp.int32, (LATS, 128), 1) < 64

    def place(at, t, north, south):
        south = pltpu.roll(south, 64, 1)
        rows = pl.ds(at, COLS, stride=2 * PAIRS)
        wide_ref[2 * t, rows, :] = jnp.where(low, north, south)
        wide_ref[2 * t + 1, rows, :] = jnp.where(low, south, north)

    def four(j, _):
        stream(2 * j).wait()
        stream(2 * j + 1).wait()
        par, first = j // 4, j % 4 * 4
        at = par * PAIRS + first
        for k in range(4):
            for c in range(2):
                for f in range(3):
                    row = (c * 3 + f) * 4
                    value = it_ref[c, first + k, par, f]
                    if k < 2:
                        coef_ref[k, row : row + 4, :] = value
                    else:
                        row += 64 * (k - 2)
                        turn_ref[row : row + 4, :] = value
                        turn_ref[row + 32 : row + 36, :256] = value[:, :256]
                        turn_ref[row + 32 : row + 36, 256:] = -value[:, 256:]
        turned = jnp.transpose(turn_ref[...]).astype(jnp.bfloat16)
        both = jnp.where(
            left, mm(leg_ref[2 * j + 1, 0], turned), mm(leg_ref[2 * j + 1, 1], turned)
        )
        for k in range(2):
            coeff = coef_ref[k].astype(jnp.bfloat16)
            even = lax.dot_general(
                coeff[:, :256], leg_ref[2 * j, k, :, :256], NT, preferred_element_type=jnp.float32
            )
            odd = lax.dot_general(
                coeff[:, 256:], leg_ref[2 * j, k, :, 256:], NT, preferred_element_type=jnp.float32
            )
            for t in range(4):
                cut = slice(128 * t, 128 * (t + 1))
                place(at + k, t, even[:, cut] + odd[:, cut], even[:, cut] - odd[:, cut])
        for t in range(4):
            block = jnp.transpose(both[128 * t : 128 * (t + 1)])
            for k in range(2):
                north = block[64 * k : 64 * k + COLS]
                place(at + 2 + k, t, north, block[64 * k + 32 : 64 * k + 32 + COLS])
        return 0

    lax.fori_loop(0, STREAMS // 2, four, 0)
    for p in range(2):
        for c in range(2):
            for f in range(3):
                for e in range(4):
                    row = (((c * 3 + f) * 4 + e) * 2 + p) * PAIRS
                    out_ref[
                        8 * e : 8 * e + 8,
                        (2 * p + c) * PAIRS : (2 * p + c + 1) * PAIRS,
                        128 * f : 128 * (f + 1),
                    ] = wide_ref[:, row : row + PAIRS, :].astype(jnp.bfloat16)


def synthesis(it6, leg4):
    return pl.pallas_call(
        synthesis_kernel,
        in_specs=[pl.BlockSpec(memory_space=pl.ANY)] * 2,
        out_shape=jax.ShapeDtypeStruct((NBAND, 4 * PAIRS, LANES), jnp.bfloat16),
        scratch_shapes=[
            pltpu.VMEM(it6.shape, jnp.float32),
            pltpu.VMEM((STREAMS, 2, LATS, DEGREES), jnp.bfloat16),
            pltpu.SemaphoreType.DMA((STREAMS + 1,)),
            pltpu.VMEM((2, COLS, DEGREES), jnp.float32),
            pltpu.VMEM((128, DEGREES), jnp.float32),
            pltpu.VMEM((8, COLS * 2 * PAIRS, 128), jnp.float32),
        ],
        compiler_params=pltpu.CompilerParams(vmem_limit_bytes=56 * MIB),
        cost_estimate=pl.CostEstimate(
            flops=2 * 32 * COLS * LATS * DEGREES, bytes_accessed=20 * MIB, transcendentals=0
        ),
        name="synthesis",
    )(it6, leg4)


def encode(x):
    return (x * jnp.abs(x)).astype(jnp.bfloat16)


def decode(coded):
    coded = coded.astype(jnp.float32)
    root = jnp.sqrt(jnp.abs(coded))
    return jnp.where(coded < 0, -root, root)


def prepare_kernel(
    id_ref, quad_ref, st_ref, it_ref, damp_ref,
    send0_ref, send1_ref, send2_ref, send3_ref, base_ref, dense_ref,
):
    node = id_ref[0]
    place = pl.program_id(0)
    z = (node + place) % 4
    total = quad_ref[node, 0] + quad_ref[node, 1] + quad_ref[node, 2] + quad_ref[node, 3]
    diag = quad_ref[node, node]
    for k in range(8):
        mode = 2 * (8 * (z % 2) + k) + z // 2
        for f in range(3):
            rate = damp_ref[f, pl.ds(mode, 1), :]
            mine = diag * rate
            inverse = 1.0 / (1.0 + mine)
            keep = (1.0 - rate * total) * inverse
            mine = mine * inverse
            for c in range(2):
                row = COLS * k + (c * 3 + f) * 4
                start, old = st_ref[c, k, f], it_ref[c, k, f]
                dense_ref[row : row + 4, :] = old - start
                base_ref[c, k, f] = start * keep + mine * old
    for s, ref in enumerate((send0_ref, send1_ref, send2_ref, send3_ref)):

        @pl.when(place == s)
        def _(ref=ref):
            ref[...] = encode(dense_ref[...])


def own_subset(i, s):
    z = (s[0] + i) % 4
    return (0, z % 2, 0, z // 2, 0, 0, 0)


STATE = (2, None, 8, None, 3, 4, DEGREES)


def prepare(ids, quad, st7, it7, damp):
    spec = pl.BlockSpec
    state = spec(STATE, own_subset)
    return pl.pallas_call(
        prepare_kernel,
        grid_spec=pltpu.PrefetchScalarGridSpec(
            num_scalar_prefetch=1,
            grid=(4,),
            in_specs=[
                spec(memory_space=pltpu.SMEM),
                state,
                state,
                spec((3, 32, DEGREES), lambda i, s: (0, 0, 0)),
            ],
            out_specs=[spec((8 * COLS, DEGREES), lambda i, s: (0, 0))] * 4 + [state],
            scratch_shapes=[pltpu.VMEM((8 * COLS, DEGREES), jnp.float32)],
        ),
        out_shape=[jax.ShapeDtypeStruct((8 * COLS, DEGREES), jnp.bfloat16)] * 4
        + [jax.ShapeDtypeStruct(it7.shape, jnp.float32)],
        compiler_params=pltpu.CompilerParams(vmem_limit_bytes=60 * MIB),
        cost_estimate=pl.CostEstimate(
            flops=8 * 32 * COLS * DEGREES, bytes_accessed=6 * MIB, transcendentals=0
        ),
        name="prepare",
    )(ids, quad, st7, it7, damp)


def split(x):
    high = x.astype(jnp.bfloat16)
    return high, (x - high.astype(jnp.float32)).astype(jnp.bfloat16)


def table_kernel(row1_ref, row2_ref, wave_ref, tab_ref, back_ref, keep_ref):
    first = lax.broadcasted_iota(jnp.int32, (1, 128), 1) == 0
    halve = jnp.where(first, 0.5, 1.0)
    wave = wave_ref[...]

    def rows(j, _):
        lead_c = row1_ref[0, pl.ds(j, 1), :]
        lead_s = row1_ref[1, pl.ds(j, 1), :]
        cosine = lead_c * row2_ref[0] - lead_s * row2_ref[1]
        sine = lead_s * row2_ref[0] + lead_c * row2_ref[1]
        at = pl.ds(pl.multiple_of(16 * j, 16), 16)
        keep_ref[0, at, :] = cosine
        keep_ref[1, at, :] = sine
        for t, value in enumerate((cosine, sine, -wave * cosine, wave * sine)):
            high, low = split(value)
            tab_ref[t, 0, at, :] = high
            tab_ref[t, 1, at, :] = low
        return 0

    lax.fori_loop(0, ROWS // 16, rows, 0)
    for t in range(2):
        for block in range(4):
            cut = slice(128 * block, 128 * (block + 1))
            value = jnp.transpose(keep_ref[t, cut, :])
            if t == 1:
                value = -value
            if block == 0:
                value = value * halve
            high, low = split(value)
            back_ref[t, 0, :, cut] = high
            back_ref[t, 1, :, cut] = low


def small_tables():
    scale = 1.0 / math.sqrt(MODES)
    step = 2.0 * math.pi / POINTS
    rows1, rows2, waves = [], [], []
    place = np.arange(NBAND)
    block = place % 4 * 8 + place // 4 % 4 * 2 + place // 16
    pairs = (block[:, None] * PAIRS + np.arange(PAIRS)).reshape(-1)
    for par in range(2):
        m = 2 * pairs + par

        def pair(k, factor):
            angle = ((k[:, None] * m[None, :]) % POINTS) * step
            return np.stack([np.cos(angle), np.sin(angle)]) * factor

        rows1.append(pair(16 * np.arange(ROWS // 16), 1.0))
        rows2.append(pair(np.arange(16), scale))
        waves.append(m[None, :] / MODES)
    return [np.stack(x).astype(np.float32) for x in (rows1, rows2, waves)]


def tables(parts):
    spec = pl.BlockSpec
    return pl.pallas_call(
        table_kernel,
        grid=(2,),
        in_specs=[
            spec((None,) + x.shape[1:], lambda i, n=x.ndim: (i,) + (0,) * (n - 1)) for x in parts
        ],
        out_specs=(
            spec((4, 2, ROWS, HALF), lambda i: (i, 0, 0, 0)),
            spec((2, 2, HALF, QUARTER), lambda i: (i, 0, 0, 0)),
        ),
        out_shape=(
            jax.ShapeDtypeStruct((8, 2, ROWS, HALF), jnp.bfloat16),
            jax.ShapeDtypeStruct((4, 2, HALF, QUARTER), jnp.bfloat16),
        ),
        scratch_shapes=[pltpu.VMEM((2, ROWS, HALF), jnp.float32)],
        compiler_params=pltpu.CompilerParams(vmem_limit_bytes=60 * MIB),
        cost_estimate=pl.CostEstimate(
            flops=16 * ROWS * HALF, bytes_accessed=15 * MIB, transcendentals=0
        ),
        name="tables",
    )(*parts)


def grid_kernel(
    got_ref, tab_hbm, back_hbm, rows_ref,
    out_ref,
    tab_ref, back_ref, sems, x_ref, wave_ref, fold_ref, edge_ref,
):
    copies = [
        pltpu.make_async_copy(tab_hbm.at[t], tab_ref.at[t], sems.at[t]) for t in range(8)
    ] + [
        pltpu.make_async_copy(back_hbm.at[i], back_ref.at[i], sems.at[8 + i]) for i in range(4)
    ]
    for copy in copies:
        copy.start()
    for i in range(4):
        x_ref[i] = got_ref[:, i * PAIRS : (i + 1) * PAIRS, :].reshape(HALF, LANES)
    which = (0, 1, 1, 0, 2, 3, 3, 2)
    for t in range(8):
        copies[t].wait()
        x = x_ref[which[t]]
        wave_ref[t] = mm(tab_ref[t, 0], x) + mm(tab_ref[t, 1], x)
    cor = rows_ref[0:1, :]

    def quads(base, at, lanes):
        ce, se = wave_ref[base, at, lanes], wave_ref[base + 1, at, lanes]
        co, so = wave_ref[base + 4, at, lanes], wave_ref[base + 5, at, lanes]
        a, b, s, d = ce + co, ce - co, se + so, se - so
        return a - s, b + d, b - d, a + s

    def tendency(at):
        cuts = [pl.ds(128 * f, 128) for f in range(3)]
        values = [quads(0, at, cut) for cut in cuts]
        slopes = [quads(2, at, cut) for cut in cuts]
        out = [[], [], []]
        for q in range(4):
            u, v, h = (values[f][q] for f in range(3))
            us, vs, hs = (slopes[f][q] for f in range(3))
            out[0].append(cor * v - u * us - hs)
            out[1].append(-u * vs - cor * u)
            out[2].append(-u * hs - (1.0 + h) * us)
        folded = []
        for t1, t2, t3, t4 in out:
            a, b, c, d = t1 + t4, t2 + t3, t1 - t4, t3 - t2
            folded.append((a + b, c + d, a - b, c - d))
        return folded

    def block(j, _):
        at = pl.ds(pl.multiple_of(16 * j, 16), 16)
        for f, folded in enumerate(tendency(at)):
            for i, value in enumerate(folded):
                high, low = split(value)
                fold_ref[i, at, pl.ds(128 * f, 128)] = high
                fold_ref[i, at, pl.ds(LANES + 128 * f, 128)] = low
        return 0

    lax.fori_loop(0, QUARTER // 16, block, 0)
    for f, folded in enumerate(tendency(pl.ds(QUARTER, 16))):
        edge_ref[0, :, pl.ds(128 * f, 128)] = folded[0]
        edge_ref[1, :, pl.ds(128 * f, 128)] = folded[3]

    odd_row = (lax.broadcasted_iota(jnp.int32, (HALF, 1), 0) & 1) == 1
    half_scale = 0.5 / math.sqrt(MODES)
    sign = jnp.where(odd_row, -half_scale, half_scale)
    weight, signed = rows_ref[1:2, :], rows_ref[2:3, :]
    for par in range(2):
        both = []
        for c in range(2):
            i = 2 * par + c
            copies[8 + i].wait()
            both_parts = mm(back_ref[i, 0], fold_ref[i])
            out = both_parts[:, :LANES] + both_parts[:, LANES:]
            out = out + mm(back_ref[i, 1], fold_ref[i, :, :LANES])
            if i == 0:
                out = out + sign * edge_ref[0, 0:1, :]
            if i == 3:
                out = out - sign * edge_ref[1, 0:1, :]
            both.append(out)
        for f in range(3):
            parts = []
            for out in both:
                part = out[:, 128 * f : 128 * (f + 1)]
                part = pltpu.roll(part, 64, 1) * weight + part * signed
                parts.append(part.reshape(NBAND, 2, 8, 128))
            joined = jnp.concatenate(parts, axis=2).astype(jnp.bfloat16)
            for h in range(2):
                out_ref[:, 2 * par + h, :, 128 * f : 128 * (f + 1)] = joined[:, h]


def grid_stage(got, tab, back, rows):
    return pl.pallas_call(
        grid_kernel,
        in_specs=[
            pl.BlockSpec(memory_space=pltpu.VMEM),
            pl.BlockSpec(memory_space=pl.ANY),
            pl.BlockSpec(memory_space=pl.ANY),
            pl.BlockSpec(memory_space=pltpu.VMEM),
        ],
        out_shape=jax.ShapeDtypeStruct((NBAND, 4, 16, LANES), jnp.bfloat16),
        scratch_shapes=[
            pltpu.VMEM((8, 2, ROWS, HALF), jnp.bfloat16),
            pltpu.VMEM((4, 2, HALF, QUARTER), jnp.bfloat16),
            pltpu.SemaphoreType.DMA((12,)),
            pltpu.VMEM((4, HALF, LANES), jnp.bfloat16),
            pltpu.VMEM((8, ROWS, LANES), jnp.float32),
            pltpu.VMEM((4, QUARTER, 2 * LANES), jnp.bfloat16),
            pltpu.VMEM((2, 16, LANES), jnp.float32),
        ],
        compiler_params=pltpu.CompilerParams(vmem_limit_bytes=48 * MIB),
        cost_estimate=pl.CostEstimate(
            flops=2 * 28 * ROWS * HALF * LANES, bytes_accessed=17 * MIB, transcendentals=0
        ),
        name="grid",
    )(got, tab, back, rows)


def analysis_kernel(
    id_ref, quad_ref, y_ref, leg_ref, move0_ref, move1_ref, move2_ref, move3_ref, st_ref, damp_ref,
    out0_ref, out1_ref, out2_ref, out3_ref, sums_ref,
    wide_ref, rate_ref, start_ref, mix_ref, acc_ref,
):
    step = pl.program_id(0)
    node = id_ref[0]
    order = [(node + 4 - s) % 4 for s in range(4)]

    @pl.when(step == 0)
    def _():
        acc_ref[...] = jnp.zeros_like(acc_ref)
        low = lax.broadcasted_iota(jnp.int32, (16, 128), 1) < 64
        for s in range(4):
            for f in range(3):
                for e in range(4):
                    for t in range(4):
                        first, second = (
                            y_ref[
                                (8 * e + 2 * t + g) * 4 + order[s], :, 128 * f : 128 * (f + 1)
                            ].astype(jnp.float32)
                            for g in range(2)
                        )
                        symmetric = jnp.where(low, first, second)
                        antisymmetric = jnp.where(low, second, first)
                        for c in range(2):
                            row = (((s * 2 + c) * 3 + f) * 4 + e) * 8
                            wide_ref[0, t, row : row + 8, :] = symmetric[8 * c : 8 * c + 8]
                            wide_ref[1, t, row : row + 8, :] = antisymmetric[8 * c : 8 * c + 8]

    for k in range(MB):
        at = step * MB + k
        mode = 2 * (8 * (node % 2) + at) + node // 2
        for c in range(2):
            for f in range(3):
                row = (c * 3 + f) * 4
                rate_ref[pl.ds(row, 4), :] = jnp.broadcast_to(
                    damp_ref[f, pl.ds(mode, 1), :], (4, DEGREES)
                )
                start_ref[pl.ds(row, 4), :] = st_ref[c, k, f]
        halves = []
        for h in range(2):
            spec = jnp.concatenate(
                [wide_ref[h, t, pl.ds(at, 4 * COLS, stride=8), :] for t in range(4)], axis=1
            ).astype(jnp.bfloat16)
            if h == 0:
                table = leg_ref[k, :, :256]
            else:
                blocks = [leg_ref[k, 64 * (b ^ 1) : 64 * (b ^ 1) + 64, 256:] for b in range(8)]
                table = jnp.concatenate(blocks, axis=0)
            halves.append(mm(spec, table))
        for h in range(2):
            cut = slice(256 * h, 256 * (h + 1))
            rate, start = rate_ref[:, cut], start_ref[:, cut]
            moves = [
                decode(ref[k // 2, COLS * (k % 2) : COLS * (k % 2 + 1), cut])
                for ref in (move0_ref, move1_ref, move2_ref, move3_ref)
            ]
            forces = [
                halves[h][COLS * p : COLS * (p + 1)] - rate * moves[p] for p in range(4)
            ]
            change = jnp.zeros_like(start)
            for q in range(4):
                row = [quad_ref[order[q], order[p]] for p in range(4)]
                mine = row[q] * rate
                inverse = 1.0 / (1.0 + mine)
                mixed = (
                    row[0] * forces[0] + row[1] * forces[1] + row[2] * forces[2] + row[3] * forces[3]
                ) * inverse
                total = row[0] + row[1] + row[2] + row[3]
                old = start + moves[q]
                moved = mixed + (start * (1.0 - rate * total) + mine * old) * inverse - old
                change = change + moved * moved
                mix_ref[q, COLS * k : COLS * (k + 1), cut] = mixed
            acc_ref[0, :, cut] += change
            acc_ref[1, :, cut] += start * start
    for s, ref in enumerate((out0_ref, out1_ref, out2_ref, out3_ref)):
        ref[...] = encode(mix_ref[s])

    @pl.when(step == pl.num_programs(0) - 1)
    def _():
        field = lax.broadcasted_iota(jnp.int32, (COLS, 1), 0) // 4 % 3
        lane = lax.broadcasted_iota(jnp.int32, (1, 128), 1)
        sums = jnp.zeros((1, 128), jnp.float32)
        for s in range(2):
            per_row = jnp.sum(acc_ref[s], axis=1, keepdims=True)
            for f in range(3):
                value = jnp.sum(jnp.where(field == f, per_row, 0.0), axis=0, keepdims=True)
                sums = sums + jnp.where(lane == 3 * s + f, value, 0.0)
        sums_ref[...] = jnp.broadcast_to(sums[None], sums_ref.shape)


def analysis(ids, quad, y, leg4, moves, st6, damp):
    spec = pl.BlockSpec
    return pl.pallas_call(
        analysis_kernel,
        grid_spec=pltpu.PrefetchScalarGridSpec(
            num_scalar_prefetch=1,
            grid=(2,),
            in_specs=[
                spec(memory_space=pltpu.SMEM),
                spec((4 * NBAND, 16, LANES), lambda i, s: (0, 0, 0)),
                spec(
                    (MB, None, LATS, DEGREES), lambda i, s: (s[0] % 2 * 2 + i, s[0] // 2, 0, 0)
                ),
                *[spec((2, 2 * COLS, DEGREES), lambda i, s: (i, 0, 0))] * 4,
                spec(
                    (2, MB, None, 3, 4, DEGREES),
                    lambda i, s: (0, s[0] % 2 * 2 + i, s[0] // 2, 0, 0, 0),
                ),
                spec((3, 32, DEGREES), lambda i, s: (0, 0, 0)),
            ],
            out_specs=(
                *[spec((MB * COLS, DEGREES), lambda i, s: (i, 0))] * 4,
                spec((4 * NBAND, 1, 128), lambda i, s: (0, 0, 0)),
            ),
            scratch_shapes=[
                pltpu.VMEM((2, 4, 4 * COLS * 8, 128), jnp.float32),
                pltpu.VMEM((COLS, DEGREES), jnp.float32),
                pltpu.VMEM((COLS, DEGREES), jnp.float32),
                pltpu.VMEM((4, MB * COLS, DEGREES), jnp.float32),
                pltpu.VMEM((2, COLS, DEGREES), jnp.float32),
            ],
        ),
        out_shape=(
            *[jax.ShapeDtypeStruct((8 * COLS, DEGREES), jnp.bfloat16)] * 4,
            jax.ShapeDtypeStruct((4 * NBAND, 1, 128), jnp.float32),
        ),
        compiler_params=pltpu.CompilerParams(vmem_limit_bytes=56 * MIB),
        cost_estimate=pl.CostEstimate(
            flops=2 * 32 * COLS * LATS * DEGREES, bytes_accessed=10 * MIB, transcendentals=0
        ),
        name="analysis",
    )(ids, quad, y, leg4, *moves, st6, damp)


def update_kernel(
    id_ref, mixed0_ref, mixed1_ref, mixed2_ref, mixed3_ref, base_ref, out_ref, mix_ref
):
    place = pl.program_id(0)
    for s, ref in enumerate((mixed0_ref, mixed1_ref, mixed2_ref, mixed3_ref)):

        @pl.when(place == s)
        def _(ref=ref):
            mix_ref[...] = decode(ref[...])

    for k in range(8):
        for c in range(2):
            for f in range(3):
                row = COLS * k + (c * 3 + f) * 4
                out_ref[c, k, f] = base_ref[c, k, f] + mix_ref[row : row + 4, :]


def update(ids, mixed, base):
    spec = pl.BlockSpec
    state = spec(STATE, own_subset)
    return pl.pallas_call(
        update_kernel,
        grid_spec=pltpu.PrefetchScalarGridSpec(
            num_scalar_prefetch=1,
            grid=(4,),
            in_specs=[*[spec((8 * COLS, DEGREES), lambda i, s: (0, 0))] * 4, state],
            out_specs=state,
            scratch_shapes=[pltpu.VMEM((8 * COLS, DEGREES), jnp.float32)],
        ),
        out_shape=jax.ShapeDtypeStruct(base.shape, jnp.float32),
        compiler_params=pltpu.CompilerParams(vmem_limit_bytes=32 * MIB),
        cost_estimate=pl.CostEstimate(
            flops=4 * 32 * COLS * DEGREES, bytes_accessed=5 * MIB, transcendentals=0
        ),
        name="update",
    )(ids, *mixed, base)


def exchange(x, axes):
    return lax.all_to_all(x, axes, split_axis=0, concat_axis=0, tiled=True)


def shift(x, axis, by):
    return lax.ppermute(x, axis, [(i, (i + by) % 4) for i in range(4)])


def latitude_rows(place, coriolis, lat_weight):
    count = LATS // 8
    group = place % 8
    cor = lax.dynamic_slice_in_dim(coriolis, group * count, count, 1)
    weight = lax.dynamic_slice_in_dim(lat_weight, group * count, count, 0)
    swapped = group % 2 == 1
    cor = jnp.where(swapped, cor[::-1], cor).reshape(1, 128)
    weight = jnp.concatenate([weight, weight])[None]
    south = lax.broadcasted_iota(jnp.int32, (1, 128), 1) >= count
    signed = jnp.where(south != swapped, -weight, weight)
    return jnp.concatenate([cor, weight, signed], axis=0)


def body(state0, iterate, legendre, lat_weight, coriolis, damping, quadrature):
    node = lax.axis_index("node")
    place = lax.axis_index(SEND)
    spec = iterate[0].transpose(0, 1, 3, 2, 4)
    base = state0.transpose(0, 1, 3, 2, 4)
    it6 = spec.reshape(2, PAIRS, 2, 3, 4, DEGREES)
    st6 = base.reshape(2, PAIRS, 2, 3, 4, DEGREES)
    leg4 = legendre.reshape(PAIRS, 2, LATS, DEGREES)
    damp = damping.transpose(1, 0, 2)
    ids = jnp.reshape(node, (1,)).astype(jnp.int32)

    shape7 = (2, 2, 8, 2, 3, 4, DEGREES)
    sent = synthesis(it6, leg4)
    got = exchange(sent, SEND)
    parts = [jnp.asarray(x) for x in small_tables()]
    late, _ = lax.optimization_barrier(((parts, quadrature), sent))
    parts, quad = late
    *moves, settled = prepare(ids, quad, base.reshape(shape7), spec.reshape(shape7), damp)
    moves = [moves[0]] + [shift(moves[s], "node", s) for s in (1, 2, 3)]
    tab, back = tables(parts)
    rows = latitude_rows(place, coriolis, lat_weight)
    rows, moves = lax.optimization_barrier((rows, moves))
    moves = [x.reshape(4, 2 * COLS, DEGREES) for x in moves]
    columns = grid_stage(got, tab, back, rows)
    spectra = exchange(columns.reshape(4 * NBAND, 16, LANES), SEND_NODE)
    *mixed, sums = analysis(ids, quadrature, spectra, leg4, moves, st6, damp)
    mixed = [mixed[0]] + [shift(mixed[s], "node", -s) for s in (1, 2, 3)]
    sums = exchange(sums, SEND_NODE)
    out = update(ids, mixed, settled)
    sums, out = lax.optimization_barrier((sums, out))
    total = jnp.sum(sums, axis=(0, 1))
    ratio = jnp.sqrt(total[:3] / (4.0 * total[3:6] + 1e-06))
    out = out.reshape(2, 32, 3, 4, DEGREES).transpose(0, 1, 3, 2, 4)
    return (out[None], ratio)


def solution(mesh):
    torus = Mesh(
        mesh.devices.reshape(mesh.shape["node"], 4, 4, 2), ("node", "band_0", "band_1", "band_2")
    )
    return jax.shard_map(
        body,
        mesh=torus,
        in_specs=(
            P(None, BAND, None, None, None),
            P("node", None, BAND, None, None, None),
            P(BAND, None, None),
            P(),
            P(),
            P(BAND, None, None),
            P(),
        ),
        out_specs=(P("node", None, BAND, None, None, None), P()),
        check_vma=False,
    )
```

```python
import functools
import math

import jax
import jax.numpy as jnp
import numpy as np
from jax import lax
from jax.experimental import pallas as pl
from jax.experimental.pallas import tpu as pltpu
from jax.sharding import Mesh
from jax.sharding import PartitionSpec as P

BAND = ("band_0", "band_1", "band_2")
SEND = ("band_2", "band_1", "band_0")
SEND_NODE = SEND + ("node",)
MODES = 1024
POINTS = 2 * MODES
HALF = MODES // 2
QUARTER = POINTS // 4
ROWS = QUARTER + 16
LATS = 512
DEGREES = 512
NBAND = 32
PAIRS = 16
COLS = 24
LANES = 384
MB = 4
MIB = 1 << 20


NT = (((1,), (1,)), ((), ()))


def mm(a, b):
    return jnp.dot(a, b, preferred_element_type=jnp.float32)


STREAMS = 16


def synthesis_kernel(it_hbm, leg_hbm, out_ref, it_ref, leg_ref, sems, coef_ref, turn_ref, wide_ref):
    def stream(j):
        return pltpu.make_async_copy(
            leg_hbm.at[pl.ds(j % 8 * 2, 2), j // 8], leg_ref.at[j], sems.at[j]
        )

    coefficients = pltpu.make_async_copy(it_hbm, it_ref, sems.at[STREAMS])
    coefficients.start()
    for j in range(STREAMS):
        stream(j).start()
    coefficients.wait()
    low = lax.broadcasted_iota(jnp.int32, (COLS, 128), 1) < 64

    left = lax.broadcasted_iota(jnp.int32, (LATS, 128), 1) < 64

    def place(at, t, north, south):
        south = pltpu.roll(south, 64, 1)
        rows = pl.ds(at, COLS, stride=2 * PAIRS)
        wide_ref[2 * t, rows, :] = jnp.where(low, north, south)
        wide_ref[2 * t + 1, rows, :] = jnp.where(low, south, north)

    def four(j, _):
        stream(2 * j).wait()
        stream(2 * j + 1).wait()
        par, first = j // 4, j % 4 * 4
        at = par * PAIRS + first
        for k in range(4):
            for c in range(2):
                for f in range(3):
                    row = (c * 3 + f) * 4
                    value = it_ref[c, first + k, par, f]
                    if k < 2:
                        coef_ref[k, row : row + 4, :] = value
                    else:
                        row += 64 * (k - 2)
                        turn_ref[row : row + 4, :] = value
                        turn_ref[row + 32 : row + 36, :256] = value[:, :256]
                        turn_ref[row + 32 : row + 36, 256:] = -value[:, 256:]
        turned = jnp.transpose(turn_ref[...]).astype(jnp.bfloat16)
        both = jnp.where(
            left, mm(leg_ref[2 * j + 1, 0], turned), mm(leg_ref[2 * j + 1, 1], turned)
        )
        for k in range(2):
            coeff = coef_ref[k].astype(jnp.bfloat16)
            even = lax.dot_general(
                coeff[:, :256], leg_ref[2 * j, k, :, :256], NT, preferred_element_type=jnp.float32
            )
            odd = lax.dot_general(
                coeff[:, 256:], leg_ref[2 * j, k, :, 256:], NT, preferred_element_type=jnp.float32
            )
            for t in range(4):
                cut = slice(128 * t, 128 * (t + 1))
                place(at + k, t, even[:, cut] + odd[:, cut], even[:, cut] - odd[:, cut])
        for t in range(4):
            block = jnp.transpose(both[128 * t : 128 * (t + 1)])
            for k in range(2):
                north = block[64 * k : 64 * k + COLS]
                place(at + 2 + k, t, north, block[64 * k + 32 : 64 * k + 32 + COLS])
        return 0

    lax.fori_loop(0, STREAMS // 2, four, 0)
    for p in range(2):
        for c in range(2):
            for f in range(3):
                for e in range(4):
                    row = (((c * 3 + f) * 4 + e) * 2 + p) * PAIRS
                    out_ref[
                        8 * e : 8 * e + 8,
                        (2 * p + c) * PAIRS : (2 * p + c + 1) * PAIRS,
                        128 * f : 128 * (f + 1),
                    ] = wide_ref[:, row : row + PAIRS, :].astype(jnp.bfloat16)


def synthesis(it6, leg4):
    return pl.pallas_call(
        synthesis_kernel,
        in_specs=[pl.BlockSpec(memory_space=pl.ANY)] * 2,
        out_shape=jax.ShapeDtypeStruct((NBAND, 4 * PAIRS, LANES), jnp.bfloat16),
        scratch_shapes=[
            pltpu.VMEM(it6.shape, jnp.float32),
            pltpu.VMEM((STREAMS, 2, LATS, DEGREES), jnp.bfloat16),
            pltpu.SemaphoreType.DMA((STREAMS + 1,)),
            pltpu.VMEM((2, COLS, DEGREES), jnp.float32),
            pltpu.VMEM((128, DEGREES), jnp.float32),
            pltpu.VMEM((8, COLS * 2 * PAIRS, 128), jnp.float32),
        ],
        compiler_params=pltpu.CompilerParams(vmem_limit_bytes=56 * MIB),
        cost_estimate=pl.CostEstimate(
            flops=2 * 32 * COLS * LATS * DEGREES, bytes_accessed=20 * MIB, transcendentals=0
        ),
        name="synthesis",
    )(it6, leg4)


def encode(x):
    return (x * jnp.abs(x)).astype(jnp.bfloat16)


def decode(coded):
    coded = coded.astype(jnp.float32)
    root = jnp.sqrt(jnp.abs(coded))
    return jnp.where(coded < 0, -root, root)


def prepare_kernel(
    id_ref, quad_ref, st_ref, it_ref, damp_ref,
    send0_ref, send1_ref, send2_ref, send3_ref, base_ref, dense_ref,
):
    node = id_ref[0]
    place = pl.program_id(0)
    z = (node + place) % 4
    total = quad_ref[node, 0] + quad_ref[node, 1] + quad_ref[node, 2] + quad_ref[node, 3]
    diag = quad_ref[node, node]
    for k in range(8):
        mode = 2 * (8 * (z % 2) + k) + z // 2
        for f in range(3):
            rate = damp_ref[f, pl.ds(mode, 1), :]
            mine = diag * rate
            inverse = 1.0 / (1.0 + mine)
            keep = (1.0 - rate * total) * inverse
            mine = mine * inverse
            for c in range(2):
                row = COLS * k + (c * 3 + f) * 4
                start, old = st_ref[c, k, f], it_ref[c, k, f]
                dense_ref[row : row + 4, :] = old - start
                base_ref[c, k, f] = start * keep + mine * old
    for s, ref in enumerate((send0_ref, send1_ref, send2_ref, send3_ref)):

        @pl.when(place == s)
        def _(ref=ref):
            ref[...] = encode(dense_ref[...])


def own_subset(i, s):
    z = (s[0] + i) % 4
    return (0, z % 2, 0, z // 2, 0, 0, 0)


STATE = (2, None, 8, None, 3, 4, DEGREES)


def prepare(ids, quad, st7, it7, damp):
    spec = pl.BlockSpec
    state = spec(STATE, own_subset)
    return pl.pallas_call(
        prepare_kernel,
        grid_spec=pltpu.PrefetchScalarGridSpec(
            num_scalar_prefetch=1,
            grid=(4,),
            in_specs=[
                spec(memory_space=pltpu.SMEM),
                state,
                state,
                spec((3, 32, DEGREES), lambda i, s: (0, 0, 0)),
            ],
            out_specs=[spec((8 * COLS, DEGREES), lambda i, s: (0, 0))] * 4 + [state],
            scratch_shapes=[pltpu.VMEM((8 * COLS, DEGREES), jnp.float32)],
        ),
        out_shape=[jax.ShapeDtypeStruct((8 * COLS, DEGREES), jnp.bfloat16)] * 4
        + [jax.ShapeDtypeStruct(it7.shape, jnp.float32)],
        compiler_params=pltpu.CompilerParams(vmem_limit_bytes=60 * MIB),
        cost_estimate=pl.CostEstimate(
            flops=8 * 32 * COLS * DEGREES, bytes_accessed=6 * MIB, transcendentals=0
        ),
        name="prepare",
    )(ids, quad, st7, it7, damp)


def split(x):
    high = x.astype(jnp.bfloat16)
    return high, (x - high.astype(jnp.float32)).astype(jnp.bfloat16)


def table_kernel(row1_ref, row2_ref, tab_ref, back_ref, keep_ref):
    first = lax.broadcasted_iota(jnp.int32, (1, 128), 1) == 0
    halve = jnp.where(first, 0.5, 1.0)

    def rows(j, _):
        lead_c = row1_ref[0, pl.ds(j, 1), :]
        lead_s = row1_ref[1, pl.ds(j, 1), :]
        cosine = lead_c * row2_ref[0] - lead_s * row2_ref[1]
        sine = lead_s * row2_ref[0] + lead_c * row2_ref[1]
        at = pl.ds(pl.multiple_of(16 * j, 16), 16)
        keep_ref[0, at, :] = cosine
        keep_ref[1, at, :] = sine
        for t, value in enumerate((cosine, sine)):
            high, low = split(value)
            tab_ref[t, 0, at, :] = high
            tab_ref[t, 1, at, :] = low
        return 0

    lax.fori_loop(0, ROWS // 16, rows, 0)
    for t in range(2):
        for block in range(4):
            cut = slice(128 * block, 128 * (block + 1))
            value = jnp.transpose(keep_ref[t, cut, :])
            if t == 1:
                value = -value
            if block == 0:
                value = value * halve
            high, low = split(value)
            back_ref[t, 0, :, cut] = high
            back_ref[t, 1, :, cut] = low


def small_tables():
    scale = 1.0 / math.sqrt(MODES)
    step = 2.0 * math.pi / POINTS
    rows1, rows2 = [], []
    place = np.arange(NBAND)
    block = place % 4 * 8 + place // 4 % 4 * 2 + place // 16
    pairs = (block[:, None] * PAIRS + np.arange(PAIRS)).reshape(-1)
    for par in range(2):
        m = 2 * pairs + par

        def pair(k, factor):
            angle = ((k[:, None] * m[None, :]) % POINTS) * step
            return np.stack([np.cos(angle), np.sin(angle)]) * factor

        rows1.append(pair(16 * np.arange(ROWS // 16), 1.0))
        rows2.append(pair(np.arange(16), scale))
    return [np.stack(x).astype(np.float32) for x in (rows1, rows2)]


def tables(parts):
    spec = pl.BlockSpec
    return pl.pallas_call(
        table_kernel,
        grid=(2,),
        in_specs=[
            spec((None,) + x.shape[1:], lambda i, n=x.ndim: (i,) + (0,) * (n - 1)) for x in parts
        ],
        out_specs=(
            spec((2, 2, ROWS, HALF), lambda i: (i, 0, 0, 0)),
            spec((2, 2, HALF, QUARTER), lambda i: (i, 0, 0, 0)),
        ),
        out_shape=(
            jax.ShapeDtypeStruct((4, 2, ROWS, HALF), jnp.bfloat16),
            jax.ShapeDtypeStruct((4, 2, HALF, QUARTER), jnp.bfloat16),
        ),
        scratch_shapes=[pltpu.VMEM((2, ROWS, HALF), jnp.float32)],
        compiler_params=pltpu.CompilerParams(vmem_limit_bytes=60 * MIB),
        cost_estimate=pl.CostEstimate(
            flops=16 * ROWS * HALF, bytes_accessed=9 * MIB, transcendentals=0
        ),
        name="tables",
    )(*parts)


def grid_kernel(
    got_ref, tab_hbm, back_hbm, rows_ref,
    out_ref,
    tab_ref, back_ref, sems, x_ref, rest_ref, wave_ref, fold_ref, edge_ref,
):
    copies = [
        pltpu.make_async_copy(tab_hbm.at[i], tab_ref.at[i], sems.at[i]) for i in range(4)
    ] + [
        pltpu.make_async_copy(back_hbm.at[i], back_ref.at[i], sems.at[4 + i]) for i in range(4)
    ]
    for copy in copies:
        copy.start()
    index = lax.broadcasted_iota(jnp.int32, (HALF, 1), 0)
    place = index >> 4
    first = ((place & 3) * 8 + (place >> 2 & 3) * 2 + (place >> 4)) * PAIRS + (index & 15)
    for par in range(2):
        ratio = (2 * first + par).astype(jnp.float32) * (1.0 / MODES)
        for c in range(2):
            at = (2 * par + c) * PAIRS
            value = got_ref[:, at : at + PAIRS, :].reshape(HALF, LANES)
            scaled = value.astype(jnp.float32) * (ratio if c == 0 else -ratio)
            high, low = split(scaled)
            x_ref[2 * par + c, :, :LANES] = value
            x_ref[2 * par + 1 - c, :, LANES:] = high
            rest_ref[2 * par + 1 - c] = low
    for i in range(4):
        copies[i].wait()
        wave_ref[i] = mm(tab_ref[i, 0], x_ref[i]) + mm(tab_ref[i, 1], x_ref[i])
        wave_ref[i, :, LANES:] += mm(tab_ref[i, 0], rest_ref[i])
    cor = rows_ref[0:1, :]

    def quads(base, at, lanes):
        ce, se, co, so = (wave_ref[i, at, base + lanes : base + lanes + 128] for i in range(4))
        a, b, s, d = ce + co, ce - co, se + so, se - so
        return a - s, b + d, b - d, a + s

    def tendency(at):
        values = [quads(0, at, 128 * f) for f in range(3)]
        slopes = [quads(LANES, at, 128 * f) for f in range(3)]
        out = [[], [], []]
        for q in range(4):
            u, v, h = (values[f][q] for f in range(3))
            us, vs, hs = (slopes[f][q] for f in range(3))
            out[0].append(cor * v - u * us - hs)
            out[1].append(-u * vs - cor * u)
            out[2].append(-u * hs - (1.0 + h) * us)
        folded = []
        for t1, t2, t3, t4 in out:
            a, b, c, d = t1 + t4, t2 + t3, t1 - t4, t3 - t2
            folded.append((a + b, c + d, a - b, c - d))
        return folded

    def block(j, _):
        at = pl.ds(pl.multiple_of(16 * j, 16), 16)
        for f, folded in enumerate(tendency(at)):
            for i, value in enumerate(folded):
                high, low = split(value)
                fold_ref[i, at, pl.ds(128 * f, 128)] = high
                fold_ref[i, at, pl.ds(LANES + 128 * f, 128)] = low
        return 0

    lax.fori_loop(0, QUARTER // 16, block, 0)
    for f, folded in enumerate(tendency(pl.ds(QUARTER, 16))):
        edge_ref[0, :, pl.ds(128 * f, 128)] = folded[0]
        edge_ref[1, :, pl.ds(128 * f, 128)] = folded[3]

    odd_row = (lax.broadcasted_iota(jnp.int32, (HALF, 1), 0) & 1) == 1
    half_scale = 0.5 / math.sqrt(MODES)
    sign = jnp.where(odd_row, -half_scale, half_scale)
    weight, signed = rows_ref[1:2, :], rows_ref[2:3, :]
    for par in range(2):
        both = []
        for c in range(2):
            i = 2 * par + c
            copies[4 + i].wait()
            both_parts = mm(back_ref[i, 0], fold_ref[i])
            out = both_parts[:, :LANES] + both_parts[:, LANES:]
            out = out + mm(back_ref[i, 1], fold_ref[i, :, :LANES])
            if i == 0:
                out = out + sign * edge_ref[0, 0:1, :]
            if i == 3:
                out = out - sign * edge_ref[1, 0:1, :]
            both.append(out)
        for f in range(3):
            parts = []
            for out in both:
                part = out[:, 128 * f : 128 * (f + 1)]
                part = pltpu.roll(part, 64, 1) * weight + part * signed
                parts.append(part.reshape(NBAND, 2, 8, 128))
            joined = jnp.concatenate(parts, axis=2).astype(jnp.bfloat16)
            for h in range(2):
                out_ref[:, 2 * par + h, :, 128 * f : 128 * (f + 1)] = joined[:, h]


def grid_stage(got, tab, back, rows):
    return pl.pallas_call(
        grid_kernel,
        in_specs=[
            pl.BlockSpec(memory_space=pltpu.VMEM),
            pl.BlockSpec(memory_space=pl.ANY),
            pl.BlockSpec(memory_space=pl.ANY),
            pl.BlockSpec(memory_space=pltpu.VMEM),
        ],
        out_shape=jax.ShapeDtypeStruct((NBAND, 4, 16, LANES), jnp.bfloat16),
        scratch_shapes=[
            pltpu.VMEM((4, 2, ROWS, HALF), jnp.bfloat16),
            pltpu.VMEM((4, 2, HALF, QUARTER), jnp.bfloat16),
            pltpu.SemaphoreType.DMA((8,)),
            pltpu.VMEM((4, HALF, 2 * LANES), jnp.bfloat16),
            pltpu.VMEM((4, HALF, LANES), jnp.bfloat16),
            pltpu.VMEM((4, ROWS, 2 * LANES), jnp.float32),
            pltpu.VMEM((4, QUARTER, 2 * LANES), jnp.bfloat16),
            pltpu.VMEM((2, 16, LANES), jnp.float32),
        ],
        compiler_params=pltpu.CompilerParams(vmem_limit_bytes=48 * MIB),
        cost_estimate=pl.CostEstimate(
            flops=2 * 28 * ROWS * HALF * LANES, bytes_accessed=17 * MIB, transcendentals=0
        ),
        name="grid",
    )(got, tab, back, rows)


def analysis_kernel(
    id_ref, quad_ref, y_ref, leg_ref, move0_ref, move1_ref, move2_ref, move3_ref, st_ref, damp_ref,
    out0_ref, out1_ref, out2_ref, out3_ref, sums_ref,
    wide_ref, rate_ref, start_ref, mix_ref, acc_ref,
):
    step = pl.program_id(0)
    node = id_ref[0]
    order = [(node + 4 - s) % 4 for s in range(4)]

    @pl.when(step == 0)
    def _():
        acc_ref[...] = jnp.zeros_like(acc_ref)
        low = lax.broadcasted_iota(jnp.int32, (16, 128), 1) < 64
        for s in range(4):
            for f in range(3):
                for e in range(4):
                    for t in range(4):
                        first, second = (
                            y_ref[
                                (8 * e + 2 * t + g) * 4 + order[s], :, 128 * f : 128 * (f + 1)
                            ].astype(jnp.float32)
                            for g in range(2)
                        )
                        symmetric = jnp.where(low, first, second)
                        antisymmetric = jnp.where(low, second, first)
                        for c in range(2):
                            row = (((s * 2 + c) * 3 + f) * 4 + e) * 8
                            wide_ref[0, t, row : row + 8, :] = symmetric[8 * c : 8 * c + 8]
                            wide_ref[1, t, row : row + 8, :] = antisymmetric[8 * c : 8 * c + 8]

    for k in range(MB):
        at = step * MB + k
        mode = 2 * (8 * (node % 2) + at) + node // 2
        for c in range(2):
            for f in range(3):
                row = (c * 3 + f) * 4
                rate_ref[pl.ds(row, 4), :] = jnp.broadcast_to(
                    damp_ref[f, pl.ds(mode, 1), :], (4, DEGREES)
                )
                start_ref[pl.ds(row, 4), :] = st_ref[c, k, f]
        halves = []
        for h in range(2):
            spec = jnp.concatenate(
                [wide_ref[h, t, pl.ds(at, 4 * COLS, stride=8), :] for t in range(4)], axis=1
            ).astype(jnp.bfloat16)
            if h == 0:
                table = leg_ref[k, :, :256]
            else:
                blocks = [leg_ref[k, 64 * (b ^ 1) : 64 * (b ^ 1) + 64, 256:] for b in range(8)]
                table = jnp.concatenate(blocks, axis=0)
            halves.append(mm(spec, table))
        for h in range(2):
            cut = slice(256 * h, 256 * (h + 1))
            rate, start = rate_ref[:, cut], start_ref[:, cut]
            moves = [
                decode(ref[k // 2, COLS * (k % 2) : COLS * (k % 2 + 1), cut])
                for ref in (move0_ref, move1_ref, move2_ref, move3_ref)
            ]
            forces = [
                halves[h][COLS * p : COLS * (p + 1)] - rate * moves[p] for p in range(4)
            ]
            change = jnp.zeros_like(start)
            for q in range(4):
                row = [quad_ref[order[q], order[p]] for p in range(4)]
                mine = row[q] * rate
                inverse = 1.0 / (1.0 + mine)
                mixed = (
                    row[0] * forces[0] + row[1] * forces[1] + row[2] * forces[2] + row[3] * forces[3]
                ) * inverse
                total = row[0] + row[1] + row[2] + row[3]
                old = start + moves[q]
                moved = mixed + (start * (1.0 - rate * total) + mine * old) * inverse - old
                change = change + moved * moved
                mix_ref[q, COLS * k : COLS * (k + 1), cut] = mixed
            acc_ref[0, :, cut] += change
            acc_ref[1, :, cut] += start * start
    for s, ref in enumerate((out0_ref, out1_ref, out2_ref, out3_ref)):
        ref[...] = encode(mix_ref[s])

    @pl.when(step == pl.num_programs(0) - 1)
    def _():
        field = lax.broadcasted_iota(jnp.int32, (COLS, 1), 0) // 4 % 3
        lane = lax.broadcasted_iota(jnp.int32, (1, 128), 1)
        sums = jnp.zeros((1, 128), jnp.float32)
        for s in range(2):
            per_row = jnp.sum(acc_ref[s], axis=1, keepdims=True)
            for f in range(3):
                value = jnp.sum(jnp.where(field == f, per_row, 0.0), axis=0, keepdims=True)
                sums = sums + jnp.where(lane == 3 * s + f, value, 0.0)
        sums_ref[...] = jnp.broadcast_to(sums[None], sums_ref.shape)


def analysis(ids, quad, y, leg4, moves, st6, damp):
    spec = pl.BlockSpec
    return pl.pallas_call(
        analysis_kernel,
        grid_spec=pltpu.PrefetchScalarGridSpec(
            num_scalar_prefetch=1,
            grid=(2,),
            in_specs=[
                spec(memory_space=pltpu.SMEM),
                spec((4 * NBAND, 16, LANES), lambda i, s: (0, 0, 0)),
                spec(
                    (MB, None, LATS, DEGREES), lambda i, s: (s[0] % 2 * 2 + i, s[0] // 2, 0, 0)
                ),
                *[spec((2, 2 * COLS, DEGREES), lambda i, s: (i, 0, 0))] * 4,
                spec(
                    (2, MB, None, 3, 4, DEGREES),
                    lambda i, s: (0, s[0] % 2 * 2 + i, s[0] // 2, 0, 0, 0),
                ),
                spec((3, 32, DEGREES), lambda i, s: (0, 0, 0)),
            ],
            out_specs=(
                *[spec((MB * COLS, DEGREES), lambda i, s: (i, 0))] * 4,
                spec((4 * NBAND, 1, 128), lambda i, s: (0, 0, 0)),
            ),
            scratch_shapes=[
                pltpu.VMEM((2, 4, 4 * COLS * 8, 128), jnp.float32),
                pltpu.VMEM((COLS, DEGREES), jnp.float32),
                pltpu.VMEM((COLS, DEGREES), jnp.float32),
                pltpu.VMEM((4, MB * COLS, DEGREES), jnp.float32),
                pltpu.VMEM((2, COLS, DEGREES), jnp.float32),
            ],
        ),
        out_shape=(
            *[jax.ShapeDtypeStruct((8 * COLS, DEGREES), jnp.bfloat16)] * 4,
            jax.ShapeDtypeStruct((4 * NBAND, 1, 128), jnp.float32),
        ),
        compiler_params=pltpu.CompilerParams(vmem_limit_bytes=46 * MIB),
        cost_estimate=pl.CostEstimate(
            flops=2 * 32 * COLS * LATS * DEGREES, bytes_accessed=10 * MIB, transcendentals=0
        ),
        name="analysis",
    )(ids, quad, y, leg4, *moves, st6, damp)


def update_kernel(
    id_ref, mixed0_ref, mixed1_ref, mixed2_ref, mixed3_ref, base_ref, out_ref, mix_ref
):
    place = pl.program_id(0)
    for s, ref in enumerate((mixed0_ref, mixed1_ref, mixed2_ref, mixed3_ref)):

        @pl.when(place == s)
        def _(ref=ref):
            mix_ref[...] = decode(ref[...])

    for k in range(8):
        for c in range(2):
            for f in range(3):
                row = COLS * k + (c * 3 + f) * 4
                out_ref[c, k, f] = base_ref[c, k, f] + mix_ref[row : row + 4, :]


def update(ids, mixed, base):
    spec = pl.BlockSpec
    state = spec(STATE, own_subset)
    return pl.pallas_call(
        update_kernel,
        grid_spec=pltpu.PrefetchScalarGridSpec(
            num_scalar_prefetch=1,
            grid=(4,),
            in_specs=[*[spec((8 * COLS, DEGREES), lambda i, s: (0, 0))] * 4, state],
            out_specs=state,
            scratch_shapes=[pltpu.VMEM((8 * COLS, DEGREES), jnp.float32)],
        ),
        out_shape=jax.ShapeDtypeStruct(base.shape, jnp.float32),
        compiler_params=pltpu.CompilerParams(vmem_limit_bytes=32 * MIB),
        cost_estimate=pl.CostEstimate(
            flops=4 * 32 * COLS * DEGREES, bytes_accessed=5 * MIB, transcendentals=0
        ),
        name="update",
    )(ids, *mixed, base)


def exchange(x, axes):
    return lax.all_to_all(x, axes, split_axis=0, concat_axis=0, tiled=True)


def shift(x, axis, by):
    return lax.ppermute(x, axis, [(i, (i + by) % 4) for i in range(4)])


def latitude_rows(place, coriolis, lat_weight):
    count = LATS // 8
    group = place % 8
    cor = lax.dynamic_slice_in_dim(coriolis, group * count, count, 1)
    weight = lax.dynamic_slice_in_dim(lat_weight, group * count, count, 0)
    swapped = group % 2 == 1
    cor = jnp.where(swapped, cor[::-1], cor).reshape(1, 128)
    weight = jnp.concatenate([weight, weight])[None]
    south = lax.broadcasted_iota(jnp.int32, (1, 128), 1) >= count
    signed = jnp.where(south != swapped, -weight, weight)
    return jnp.concatenate([cor, weight, signed], axis=0)


def body(state0, iterate, legendre, lat_weight, coriolis, damping, quadrature):
    node = lax.axis_index("node")
    place = lax.axis_index(SEND)
    spec = iterate[0].transpose(0, 1, 3, 2, 4)
    base = state0.transpose(0, 1, 3, 2, 4)
    it6 = spec.reshape(2, PAIRS, 2, 3, 4, DEGREES)
    st6 = base.reshape(2, PAIRS, 2, 3, 4, DEGREES)
    leg4 = legendre.reshape(PAIRS, 2, LATS, DEGREES)
    damp = damping.transpose(1, 0, 2)
    ids = jnp.reshape(node, (1,)).astype(jnp.int32)

    shape7 = (2, 2, 8, 2, 3, 4, DEGREES)
    sent = synthesis(it6, leg4)
    got = exchange(sent, SEND)
    parts = [jnp.asarray(x) for x in small_tables()]
    late, _ = lax.optimization_barrier(((parts, quadrature), sent))
    parts, quad = late
    *moves, settled = prepare(ids, quad, base.reshape(shape7), spec.reshape(shape7), damp)
    moves = [moves[0]] + [shift(moves[s], "node", s) for s in (1, 2, 3)]
    tab, back = tables(parts)
    rows = latitude_rows(place, coriolis, lat_weight)
    rows, moves = lax.optimization_barrier((rows, moves))
    moves = [x.reshape(4, 2 * COLS, DEGREES) for x in moves]
    columns = grid_stage(got, tab, back, rows)
    spectra = exchange(columns.reshape(4 * NBAND, 16, LANES), SEND_NODE)
    *mixed, sums = analysis(ids, quadrature, spectra, leg4, moves, st6, damp)
    mixed = [mixed[0]] + [shift(mixed[s], "node", -s) for s in (1, 2, 3)]
    sums = exchange(sums, SEND_NODE)
    out = update(ids, mixed, settled)
    sums, out = lax.optimization_barrier((sums, out))
    total = jnp.sum(sums, axis=(0, 1))
    ratio = jnp.sqrt(total[:3] / (4.0 * total[3:6] + 1e-06))
    out = out.reshape(2, 32, 3, 4, DEGREES).transpose(0, 1, 3, 2, 4)
    return (out[None], ratio)


def solution(mesh):
    torus = Mesh(
        mesh.devices.reshape(mesh.shape["node"], 4, 4, 2), ("node", "band_0", "band_1", "band_2")
    )
    return jax.shard_map(
        body,
        mesh=torus,
        in_specs=(
            P(None, BAND, None, None, None),
            P("node", None, BAND, None, None, None),
            P(BAND, None, None),
            P(),
            P(),
            P(BAND, None, None),
            P(),
        ),
        out_specs=(P("node", None, BAND, None, None, None), P()),
        check_vma=False,
    )
```

```python
import functools
import math

import jax
import jax.numpy as jnp
import numpy as np
from jax import lax
from jax.experimental import pallas as pl
from jax.experimental.pallas import tpu as pltpu
from jax.sharding import Mesh
from jax.sharding import PartitionSpec as P

BAND = ("band_0", "band_1", "band_2")
SEND = ("band_2", "band_1", "band_0")
SEND_NODE = SEND + ("node",)
MODES = 1024
POINTS = 2 * MODES
HALF = MODES // 2
QUARTER = POINTS // 4
ROWS = QUARTER + 16
LATS = 512
DEGREES = 512
NBAND = 32
PAIRS = 16
COLS = 24
LANES = 384
MB = 4
MIB = 1 << 20


NT = (((1,), (1,)), ((), ()))


def mm(a, b):
    return jnp.dot(a, b, preferred_element_type=jnp.float32)


STREAMS = 16


def synthesis_kernel(it_hbm, leg_hbm, out_ref, it_ref, leg_ref, sems, coef_ref, turn_ref, wide_ref):
    def stream(j):
        return pltpu.make_async_copy(
            leg_hbm.at[pl.ds(j % 8 * 2, 2), j // 8], leg_ref.at[j], sems.at[j]
        )

    coefficients = pltpu.make_async_copy(it_hbm, it_ref, sems.at[STREAMS])
    coefficients.start()
    for j in range(STREAMS):
        stream(j).start()
    coefficients.wait()
    low = lax.broadcasted_iota(jnp.int32, (COLS, 128), 1) < 64

    left = lax.broadcasted_iota(jnp.int32, (LATS, 128), 1) < 64

    def place(at, t, north, south):
        south = pltpu.roll(south, 64, 1)
        rows = pl.ds(at, COLS, stride=2 * PAIRS)
        wide_ref[2 * t, rows, :] = jnp.where(low, north, south)
        wide_ref[2 * t + 1, rows, :] = jnp.where(low, south, north)

    def four(j, _):
        stream(2 * j).wait()
        stream(2 * j + 1).wait()
        par, first = j // 4, j % 4 * 4
        at = par * PAIRS + first
        for k in range(4):
            for c in range(2):
                for f in range(3):
                    row = (c * 3 + f) * 4
                    value = it_ref[c, first + k, par, f]
                    if k < 2:
                        coef_ref[k, row : row + 4, :] = value
                    else:
                        row += 64 * (k - 2)
                        turn_ref[row : row + 4, :] = value
                        turn_ref[row + 32 : row + 36, :256] = value[:, :256]
                        turn_ref[row + 32 : row + 36, 256:] = -value[:, 256:]
        turned = jnp.transpose(turn_ref[...]).astype(jnp.bfloat16)
        both = jnp.where(
            left, mm(leg_ref[2 * j + 1, 0], turned), mm(leg_ref[2 * j + 1, 1], turned)
        )
        for k in range(2):
            coeff = coef_ref[k].astype(jnp.bfloat16)
            even = lax.dot_general(
                coeff[:, :256], leg_ref[2 * j, k, :, :256], NT, preferred_element_type=jnp.float32
            )
            odd = lax.dot_general(
                coeff[:, 256:], leg_ref[2 * j, k, :, 256:], NT, preferred_element_type=jnp.float32
            )
            for t in range(4):
                cut = slice(128 * t, 128 * (t + 1))
                place(at + k, t, even[:, cut] + odd[:, cut], even[:, cut] - odd[:, cut])
        for t in range(4):
            block = jnp.transpose(both[128 * t : 128 * (t + 1)])
            for k in range(2):
                north = block[64 * k : 64 * k + COLS]
                place(at + 2 + k, t, north, block[64 * k + 32 : 64 * k + 32 + COLS])
        return 0

    lax.fori_loop(0, STREAMS // 2, four, 0)
    for p in range(2):
        for c in range(2):
            for f in range(3):
                for e in range(4):
                    row = (((c * 3 + f) * 4 + e) * 2 + p) * PAIRS
                    out_ref[
                        8 * e : 8 * e + 8,
                        (2 * p + c) * PAIRS : (2 * p + c + 1) * PAIRS,
                        128 * f : 128 * (f + 1),
                    ] = wide_ref[:, row : row + PAIRS, :].astype(jnp.bfloat16)


def synthesis(it6, leg4):
    return pl.pallas_call(
        synthesis_kernel,
        in_specs=[pl.BlockSpec(memory_space=pl.ANY)] * 2,
        out_shape=jax.ShapeDtypeStruct((NBAND, 4 * PAIRS, LANES), jnp.bfloat16),
        scratch_shapes=[
            pltpu.VMEM(it6.shape, jnp.float32),
            pltpu.VMEM((STREAMS, 2, LATS, DEGREES), jnp.bfloat16),
            pltpu.SemaphoreType.DMA((STREAMS + 1,)),
            pltpu.VMEM((2, COLS, DEGREES), jnp.float32),
            pltpu.VMEM((128, DEGREES), jnp.float32),
            pltpu.VMEM((8, COLS * 2 * PAIRS, 128), jnp.float32),
        ],
        compiler_params=pltpu.CompilerParams(vmem_limit_bytes=56 * MIB),
        cost_estimate=pl.CostEstimate(
            flops=2 * 32 * COLS * LATS * DEGREES, bytes_accessed=20 * MIB, transcendentals=0
        ),
        name="synthesis",
    )(it6, leg4)


def encode(x):
    return (x * jnp.abs(x)).astype(jnp.bfloat16)


def decode(coded):
    coded = coded.astype(jnp.float32)
    root = jnp.sqrt(jnp.abs(coded))
    return jnp.where(coded < 0, -root, root)


def prepare_kernel(
    id_ref, quad_ref, st_ref, it_ref, damp_ref,
    send0_ref, send1_ref, send2_ref, send3_ref, base_ref, dense_ref,
):
    node = id_ref[0]
    place = pl.program_id(0)
    z = (node + place) % 4
    total = quad_ref[node, 0] + quad_ref[node, 1] + quad_ref[node, 2] + quad_ref[node, 3]
    diag = quad_ref[node, node]
    for k in range(8):
        mode = 2 * (8 * (z % 2) + k) + z // 2
        for f in range(3):
            rate = damp_ref[f, pl.ds(mode, 1), :]
            mine = diag * rate
            inverse = 1.0 / (1.0 + mine)
            keep = (1.0 - rate * total) * inverse
            mine = mine * inverse
            for c in range(2):
                row = COLS * k + (c * 3 + f) * 4
                start, old = st_ref[c, k, f], it_ref[c, k, f]
                dense_ref[row : row + 4, :] = old - start
                base_ref[c, k, f] = start * keep + mine * old
    for s, ref in enumerate((send0_ref, send1_ref, send2_ref, send3_ref)):

        @pl.when(place == s)
        def _(ref=ref):
            ref[...] = encode(dense_ref[...])


def own_subset(i, s):
    z = (s[0] + i) % 4
    return (0, z % 2, 0, z // 2, 0, 0, 0)


STATE = (2, None, 8, None, 3, 4, DEGREES)


def prepare(ids, quad, st7, it7, damp):
    spec = pl.BlockSpec
    state = spec(STATE, own_subset)
    return pl.pallas_call(
        prepare_kernel,
        grid_spec=pltpu.PrefetchScalarGridSpec(
            num_scalar_prefetch=1,
            grid=(4,),
            in_specs=[
                spec(memory_space=pltpu.SMEM),
                state,
                state,
                spec((3, 32, DEGREES), lambda i, s: (0, 0, 0)),
            ],
            out_specs=[spec((8 * COLS, DEGREES), lambda i, s: (0, 0))] * 4 + [state],
            scratch_shapes=[pltpu.VMEM((8 * COLS, DEGREES), jnp.float32)],
        ),
        out_shape=[jax.ShapeDtypeStruct((8 * COLS, DEGREES), jnp.bfloat16)] * 4
        + [jax.ShapeDtypeStruct(it7.shape, jnp.float32)],
        compiler_params=pltpu.CompilerParams(vmem_limit_bytes=60 * MIB),
        cost_estimate=pl.CostEstimate(
            flops=8 * 32 * COLS * DEGREES, bytes_accessed=6 * MIB, transcendentals=0
        ),
        name="prepare",
    )(ids, quad, st7, it7, damp)


def split(x):
    high = x.astype(jnp.bfloat16)
    return high, (x - high.astype(jnp.float32)).astype(jnp.bfloat16)


def table_kernel(row1_ref, row2_ref, tab_ref, back_ref, keep_ref):
    first = lax.broadcasted_iota(jnp.int32, (1, 128), 1) == 0
    halve = jnp.where(first, 0.5, 1.0)

    def rows(j, _):
        lead_c = row1_ref[0, pl.ds(j, 1), :]
        lead_s = row1_ref[1, pl.ds(j, 1), :]
        cosine = lead_c * row2_ref[0] - lead_s * row2_ref[1]
        sine = lead_s * row2_ref[0] + lead_c * row2_ref[1]
        at = pl.ds(pl.multiple_of(16 * j, 16), 16)
        keep_ref[0, at, :] = cosine
        keep_ref[1, at, :] = sine
        for t, value in enumerate((cosine, sine)):
            high, low = split(value)
            tab_ref[t, 0, at, :] = high
            tab_ref[t, 1, at, :] = low
        return 0

    lax.fori_loop(0, ROWS // 16, rows, 0)
    for t in range(2):
        for block in range(4):
            cut = slice(128 * block, 128 * (block + 1))
            value = jnp.transpose(keep_ref[t, cut, :])
            if t == 1:
                value = -value
            if block == 0:
                value = value * halve
            high, low = split(value)
            back_ref[t, 0, :, cut] = high
            back_ref[t, 1, :, cut] = low


def small_tables():
    scale = 1.0 / math.sqrt(MODES)
    step = 2.0 * math.pi / POINTS
    rows1, rows2 = [], []
    place = np.arange(NBAND)
    block = place % 4 * 8 + place // 4 % 4 * 2 + place // 16
    pairs = (block[:, None] * PAIRS + np.arange(PAIRS)).reshape(-1)
    for par in range(2):
        m = 2 * pairs + par

        def pair(k, factor):
            angle = ((k[:, None] * m[None, :]) % POINTS) * step
            return np.stack([np.cos(angle), np.sin(angle)]) * factor

        rows1.append(pair(16 * np.arange(ROWS // 16), 1.0))
        rows2.append(pair(np.arange(16), scale))
    return [np.stack(x).astype(np.float32) for x in (rows1, rows2)]


def tables(parts):
    spec = pl.BlockSpec
    return pl.pallas_call(
        table_kernel,
        grid=(2,),
        in_specs=[
            spec((None,) + x.shape[1:], lambda i, n=x.ndim: (i,) + (0,) * (n - 1)) for x in parts
        ],
        out_specs=(
            spec((2, 2, ROWS, HALF), lambda i: (i, 0, 0, 0)),
            spec((2, 2, HALF, QUARTER), lambda i: (i, 0, 0, 0)),
        ),
        out_shape=(
            jax.ShapeDtypeStruct((4, 2, ROWS, HALF), jnp.bfloat16),
            jax.ShapeDtypeStruct((4, 2, HALF, QUARTER), jnp.bfloat16),
        ),
        scratch_shapes=[pltpu.VMEM((2, ROWS, HALF), jnp.float32)],
        compiler_params=pltpu.CompilerParams(vmem_limit_bytes=60 * MIB),
        cost_estimate=pl.CostEstimate(
            flops=16 * ROWS * HALF, bytes_accessed=9 * MIB, transcendentals=0
        ),
        name="tables",
    )(*parts)


def grid_kernel(
    got_ref, tab_hbm, back_hbm, rows_ref,
    out_ref,
    tab_ref, back_ref, sems, x_ref, rest_ref, wave_ref, fold_ref, edge_ref,
):
    copies = [
        pltpu.make_async_copy(tab_hbm.at[i], tab_ref.at[i], sems.at[i]) for i in range(4)
    ] + [
        pltpu.make_async_copy(back_hbm.at[i], back_ref.at[i], sems.at[4 + i]) for i in range(4)
    ]
    for copy in copies:
        copy.start()
    index = lax.broadcasted_iota(jnp.int32, (HALF, 1), 0)
    place = index >> 4
    first = ((place & 3) * 8 + (place >> 2 & 3) * 2 + (place >> 4)) * PAIRS + (index & 15)
    for par in range(2):
        ratio = (2 * first + par).astype(jnp.float32) * (1.0 / MODES)
        for c in range(2):
            at = (2 * par + c) * PAIRS
            value = got_ref[:, at : at + PAIRS, :].reshape(HALF, LANES)
            scaled = value.astype(jnp.float32) * (ratio if c == 0 else -ratio)
            high, low = split(scaled)
            x_ref[2 * par + c, :, :LANES] = value
            x_ref[2 * par + 1 - c, :, LANES:] = high
            rest_ref[2 * par + 1 - c] = low
    for i in range(4):
        copies[i].wait()
        wave_ref[i] = mm(tab_ref[i, 0], x_ref[i]) + mm(tab_ref[i, 1], x_ref[i])
        wave_ref[i, :, LANES:] += mm(tab_ref[i, 0], rest_ref[i])
    cor = rows_ref[0:1, :]

    def quads(base, at, lanes):
        ce, se, co, so = (wave_ref[i, at, base + lanes : base + lanes + 128] for i in range(4))
        a, b, s, d = ce + co, ce - co, se + so, se - so
        return a - s, b + d, b - d, a + s

    def tendency(at):
        values = [quads(0, at, 128 * f) for f in range(3)]
        slopes = [quads(LANES, at, 128 * f) for f in range(3)]
        out = [[], [], []]
        for q in range(4):
            u, v, h = (values[f][q] for f in range(3))
            us, vs, hs = (slopes[f][q] for f in range(3))
            out[0].append(cor * v - u * us - hs)
            out[1].append(-u * vs - cor * u)
            out[2].append(-u * hs - (1.0 + h) * us)
        folded = []
        for t1, t2, t3, t4 in out:
            a, b, c, d = t1 + t4, t2 + t3, t1 - t4, t3 - t2
            folded.append((a + b, c + d, a - b, c - d))
        return folded

    def block(j, _):
        at = pl.ds(pl.multiple_of(16 * j, 16), 16)
        for f, folded in enumerate(tendency(at)):
            for i, value in enumerate(folded):
                high, low = split(value)
                fold_ref[i, at, pl.ds(128 * f, 128)] = high
                fold_ref[i, at, pl.ds(LANES + 128 * f, 128)] = low
        return 0

    lax.fori_loop(0, QUARTER // 16, block, 0)
    for f, folded in enumerate(tendency(pl.ds(QUARTER, 16))):
        edge_ref[0, :, pl.ds(128 * f, 128)] = folded[0]
        edge_ref[1, :, pl.ds(128 * f, 128)] = folded[3]

    odd_row = (lax.broadcasted_iota(jnp.int32, (HALF, 1), 0) & 1) == 1
    half_scale = 0.5 / math.sqrt(MODES)
    sign = jnp.where(odd_row, -half_scale, half_scale)
    weight, signed = rows_ref[1:2, :], rows_ref[2:3, :]
    for par in range(2):
        both = []
        for c in range(2):
            i = 2 * par + c
            copies[4 + i].wait()
            both_parts = mm(back_ref[i, 0], fold_ref[i])
            out = both_parts[:, :LANES] + both_parts[:, LANES:]
            out = out + mm(back_ref[i, 1], fold_ref[i, :, :LANES])
            if i == 0:
                out = out + sign * edge_ref[0, 0:1, :]
            if i == 3:
                out = out - sign * edge_ref[1, 0:1, :]
            both.append(out)
        for f in range(3):
            parts = []
            for out in both:
                part = out[:, 128 * f : 128 * (f + 1)]
                part = pltpu.roll(part, 64, 1) * weight + part * signed
                parts.append(part.reshape(NBAND, 2, 8, 128))
            joined = jnp.concatenate(parts, axis=2).astype(jnp.bfloat16)
            for h in range(2):
                out_ref[:, 2 * par + h, :, 128 * f : 128 * (f + 1)] = joined[:, h]


def grid_stage(got, tab, back, rows):
    return pl.pallas_call(
        grid_kernel,
        in_specs=[
            pl.BlockSpec(memory_space=pltpu.VMEM),
            pl.BlockSpec(memory_space=pl.ANY),
            pl.BlockSpec(memory_space=pl.ANY),
            pl.BlockSpec(memory_space=pltpu.VMEM),
        ],
        out_shape=jax.ShapeDtypeStruct((NBAND, 4, 16, LANES), jnp.bfloat16),
        scratch_shapes=[
            pltpu.VMEM((4, 2, ROWS, HALF), jnp.bfloat16),
            pltpu.VMEM((4, 2, HALF, QUARTER), jnp.bfloat16),
            pltpu.SemaphoreType.DMA((8,)),
            pltpu.VMEM((4, HALF, 2 * LANES), jnp.bfloat16),
            pltpu.VMEM((4, HALF, LANES), jnp.bfloat16),
            pltpu.VMEM((4, ROWS, 2 * LANES), jnp.float32),
            pltpu.VMEM((4, QUARTER, 2 * LANES), jnp.bfloat16),
            pltpu.VMEM((2, 16, LANES), jnp.float32),
        ],
        compiler_params=pltpu.CompilerParams(vmem_limit_bytes=48 * MIB),
        cost_estimate=pl.CostEstimate(
            flops=2 * 28 * ROWS * HALF * LANES, bytes_accessed=17 * MIB, transcendentals=0
        ),
        name="grid",
    )(got, tab, back, rows)


def analysis_kernel(
    id_ref, quad_ref, y_ref, leg_ref, move0_ref, move1_ref, move2_ref, move3_ref, st_ref, damp_ref,
    out0_ref, out1_ref, out2_ref, out3_ref, sums_ref,
    wide_ref, rate_ref, start_ref, mix_ref, acc_ref,
):
    step = pl.program_id(0)
    node = id_ref[0]
    order = [(node + 4 - s) % 4 for s in range(4)]

    @pl.when(step == 0)
    def _():
        acc_ref[...] = jnp.zeros_like(acc_ref)
        low = lax.broadcasted_iota(jnp.int32, (16, 128), 1) < 64
        for s in range(4):
            for f in range(3):
                for e in range(4):
                    for t in range(4):
                        first, second = (
                            y_ref[
                                (8 * e + 2 * t + g) * 4 + order[s], :, 128 * f : 128 * (f + 1)
                            ].astype(jnp.float32)
                            for g in range(2)
                        )
                        symmetric = jnp.where(low, first, second)
                        antisymmetric = jnp.where(low, second, first)
                        for c in range(2):
                            row = (((s * 2 + c) * 3 + f) * 4 + e) * 8
                            wide_ref[0, t, row : row + 8, :] = symmetric[8 * c : 8 * c + 8]
                            wide_ref[1, t, row : row + 8, :] = antisymmetric[8 * c : 8 * c + 8]

    for k in range(MB):
        at = step * MB + k
        mode = 2 * (8 * (node % 2) + at) + node // 2
        for c in range(2):
            for f in range(3):
                row = (c * 3 + f) * 4
                rate_ref[pl.ds(row, 4), :] = jnp.broadcast_to(
                    damp_ref[f, pl.ds(mode, 1), :], (4, DEGREES)
                )
                start_ref[pl.ds(row, 4), :] = st_ref[c, k, f]
        halves = []
        for h in range(2):
            spec = jnp.concatenate(
                [wide_ref[h, t, pl.ds(at, 4 * COLS, stride=8), :] for t in range(4)], axis=1
            ).astype(jnp.bfloat16)
            if h == 0:
                table = leg_ref[k, :, :256]
            else:
                blocks = [leg_ref[k, 64 * (b ^ 1) : 64 * (b ^ 1) + 64, 256:] for b in range(8)]
                table = jnp.concatenate(blocks, axis=0)
            halves.append(mm(spec, table))
        for h in range(2):
            cut = slice(256 * h, 256 * (h + 1))
            rate, start = rate_ref[:, cut], start_ref[:, cut]
            moves = [
                decode(ref[k // 2, COLS * (k % 2) : COLS * (k % 2 + 1), cut])
                for ref in (move0_ref, move1_ref, move2_ref, move3_ref)
            ]
            forces = [
                halves[h][COLS * p : COLS * (p + 1)] - rate * moves[p] for p in range(4)
            ]
            change = jnp.zeros_like(start)
            for q in range(4):
                row = [quad_ref[order[q], order[p]] for p in range(4)]
                mine = row[q] * rate
                inverse = 1.0 / (1.0 + mine)
                mixed = (
                    row[0] * forces[0] + row[1] * forces[1] + row[2] * forces[2] + row[3] * forces[3]
                ) * inverse
                total = row[0] + row[1] + row[2] + row[3]
                old = start + moves[q]
                moved = mixed + (start * (1.0 - rate * total) + mine * old) * inverse - old
                change = change + moved * moved
                mix_ref[q, COLS * k : COLS * (k + 1), cut] = mixed
            acc_ref[0, :, cut] += change
            acc_ref[1, :, cut] += start * start
    for s, ref in enumerate((out0_ref, out1_ref, out2_ref, out3_ref)):
        ref[...] = encode(mix_ref[s])

    @pl.when(step == pl.num_programs(0) - 1)
    def _():
        field = lax.broadcasted_iota(jnp.int32, (COLS, 1), 0) // 4 % 3
        lane = lax.broadcasted_iota(jnp.int32, (1, 128), 1)
        sums = jnp.zeros((1, 128), jnp.float32)
        for s in range(2):
            per_row = jnp.sum(acc_ref[s], axis=1, keepdims=True)
            for f in range(3):
                value = jnp.sum(jnp.where(field == f, per_row, 0.0), axis=0, keepdims=True)
                sums = sums + jnp.where(lane == 3 * s + f, value, 0.0)
        sums_ref[...] = jnp.broadcast_to(sums[None], sums_ref.shape)


def analysis(ids, quad, y, leg4, moves, st6, damp):
    spec = pl.BlockSpec
    return pl.pallas_call(
        analysis_kernel,
        grid_spec=pltpu.PrefetchScalarGridSpec(
            num_scalar_prefetch=1,
            grid=(2,),
            in_specs=[
                spec(memory_space=pltpu.SMEM),
                spec((4 * NBAND, 16, LANES), lambda i, s: (0, 0, 0)),
                spec(
                    (MB, None, LATS, DEGREES), lambda i, s: (s[0] % 2 * 2 + i, s[0] // 2, 0, 0)
                ),
                *[spec((2, 2 * COLS, DEGREES), lambda i, s: (i, 0, 0))] * 4,
                spec(
                    (2, MB, None, 3, 4, DEGREES),
                    lambda i, s: (0, s[0] % 2 * 2 + i, s[0] // 2, 0, 0, 0),
                ),
                spec((3, 32, DEGREES), lambda i, s: (0, 0, 0)),
            ],
            out_specs=(
                *[spec((MB * COLS, DEGREES), lambda i, s: (i, 0))] * 4,
                spec((NBAND, 1, 128), lambda i, s: (0, 0, 0)),
            ),
            scratch_shapes=[
                pltpu.VMEM((2, 4, 4 * COLS * 8, 128), jnp.float32),
                pltpu.VMEM((COLS, DEGREES), jnp.float32),
                pltpu.VMEM((COLS, DEGREES), jnp.float32),
                pltpu.VMEM((4, MB * COLS, DEGREES), jnp.float32),
                pltpu.VMEM((2, COLS, DEGREES), jnp.float32),
            ],
        ),
        out_shape=(
            *[jax.ShapeDtypeStruct((8 * COLS, DEGREES), jnp.bfloat16)] * 4,
            jax.ShapeDtypeStruct((NBAND, 1, 128), jnp.float32),
        ),
        compiler_params=pltpu.CompilerParams(vmem_limit_bytes=46 * MIB),
        cost_estimate=pl.CostEstimate(
            flops=2 * 32 * COLS * LATS * DEGREES, bytes_accessed=10 * MIB, transcendentals=0
        ),
        name="analysis",
    )(ids, quad, y, leg4, *moves, st6, damp)


def update_kernel(
    id_ref, mixed0_ref, mixed1_ref, mixed2_ref, mixed3_ref, base_ref, out_ref, mix_ref
):
    place = pl.program_id(0)
    for s, ref in enumerate((mixed0_ref, mixed1_ref, mixed2_ref, mixed3_ref)):

        @pl.when(place == s)
        def _(ref=ref):
            mix_ref[...] = decode(ref[...])

    for k in range(8):
        for c in range(2):
            for f in range(3):
                row = COLS * k + (c * 3 + f) * 4
                out_ref[c, k, f] = base_ref[c, k, f] + mix_ref[row : row + 4, :]


def update(ids, mixed, base):
    spec = pl.BlockSpec
    state = spec(STATE, own_subset)
    return pl.pallas_call(
        update_kernel,
        grid_spec=pltpu.PrefetchScalarGridSpec(
            num_scalar_prefetch=1,
            grid=(4,),
            in_specs=[*[spec((8 * COLS, DEGREES), lambda i, s: (0, 0))] * 4, state],
            out_specs=state,
            scratch_shapes=[pltpu.VMEM((8 * COLS, DEGREES), jnp.float32)],
        ),
        out_shape=jax.ShapeDtypeStruct(base.shape, jnp.float32),
        compiler_params=pltpu.CompilerParams(vmem_limit_bytes=32 * MIB),
        cost_estimate=pl.CostEstimate(
            flops=4 * 32 * COLS * DEGREES, bytes_accessed=5 * MIB, transcendentals=0
        ),
        name="update",
    )(ids, *mixed, base)


def exchange(x, axes):
    return lax.all_to_all(x, axes, split_axis=0, concat_axis=0, tiled=True)


def shift(x, axis, by):
    return lax.ppermute(x, axis, [(i, (i + by) % 4) for i in range(4)])


def latitude_rows(place, coriolis, lat_weight):
    count = LATS // 8
    group = place % 8
    cor = lax.dynamic_slice_in_dim(coriolis, group * count, count, 1)
    weight = lax.dynamic_slice_in_dim(lat_weight, group * count, count, 0)
    swapped = group % 2 == 1
    cor = jnp.where(swapped, cor[::-1], cor).reshape(1, 128)
    weight = jnp.concatenate([weight, weight])[None]
    south = lax.broadcasted_iota(jnp.int32, (1, 128), 1) >= count
    signed = jnp.where(south != swapped, -weight, weight)
    return jnp.concatenate([cor, weight, signed], axis=0)


def body(state0, iterate, legendre, lat_weight, coriolis, damping, quadrature):
    node = lax.axis_index("node")
    place = lax.axis_index(SEND)
    spec = iterate[0].transpose(0, 1, 3, 2, 4)
    base = state0.transpose(0, 1, 3, 2, 4)
    it6 = spec.reshape(2, PAIRS, 2, 3, 4, DEGREES)
    st6 = base.reshape(2, PAIRS, 2, 3, 4, DEGREES)
    leg4 = legendre.reshape(PAIRS, 2, LATS, DEGREES)
    damp = damping.transpose(1, 0, 2)
    ids = jnp.reshape(node, (1,)).astype(jnp.int32)

    shape7 = (2, 2, 8, 2, 3, 4, DEGREES)
    sent = synthesis(it6, leg4)
    got = exchange(sent, SEND)
    parts = [jnp.asarray(x) for x in small_tables()]
    late, _ = lax.optimization_barrier(((parts, quadrature), sent))
    parts, quad = late
    *moves, settled = prepare(ids, quad, base.reshape(shape7), spec.reshape(shape7), damp)
    moves = [moves[0]] + [shift(moves[s], "node", s) for s in (1, 2, 3)]
    tab, back = tables(parts)
    rows = latitude_rows(place, coriolis, lat_weight)
    rows, moves = lax.optimization_barrier((rows, moves))
    moves = [x.reshape(4, 2 * COLS, DEGREES) for x in moves]
    columns = grid_stage(got, tab, back, rows)
    spectra = exchange(columns.reshape(4 * NBAND, 16, LANES), SEND_NODE)
    *mixed, sums = analysis(ids, quadrature, spectra, leg4, moves, st6, damp)
    mixed = [mixed[0]] + [shift(mixed[s], "node", -s) for s in (1, 2, 3)]
    near = shift(sums, "node", 1) + shift(sums, "node", -1)
    sums = exchange((sums + shift(sums, "node", 2)) + near, SEND)
    out = update(ids, mixed, settled)
    sums, out = lax.optimization_barrier((sums, out))
    total = jnp.sum(sums, axis=(0, 1))
    ratio = jnp.sqrt(total[:3] / (4.0 * total[3:6] + 1e-06))
    out = out.reshape(2, 32, 3, 4, DEGREES).transpose(0, 1, 3, 2, 4)
    return (out[None], ratio)


def solution(mesh):
    torus = Mesh(
        mesh.devices.reshape(mesh.shape["node"], 4, 4, 2), ("node", "band_0", "band_1", "band_2")
    )
    return jax.shard_map(
        body,
        mesh=torus,
        in_specs=(
            P(None, BAND, None, None, None),
            P("node", None, BAND, None, None, None),
            P(BAND, None, None),
            P(),
            P(),
            P(BAND, None, None),
            P(),
        ),
        out_specs=(P("node", None, BAND, None, None, None), P()),
        check_vma=False,
    )
```

```python
import functools
import math

import jax
import jax.numpy as jnp
import numpy as np
from jax import lax
from jax.experimental import pallas as pl
from jax.experimental.pallas import tpu as pltpu
from jax.sharding import Mesh
from jax.sharding import PartitionSpec as P

BAND = ("band_0", "band_1", "band_2")
SEND = ("band_2", "band_1", "band_0")
SEND_NODE = SEND + ("node",)
MODES = 1024
POINTS = 2 * MODES
HALF = MODES // 2
QUARTER = POINTS // 4
ROWS = QUARTER + 16
LATS = 512
DEGREES = 512
NBAND = 32
PAIRS = 16
COLS = 24
LANES = 384
MB = 4
MIB = 1 << 20


NT = (((1,), (1,)), ((), ()))


def mm(a, b):
    return jnp.dot(a, b, preferred_element_type=jnp.float32)


STREAMS = 16


def synthesis_kernel(it_hbm, leg_hbm, out_ref, it_ref, leg_ref, sems, coef_ref, turn_ref, wide_ref):
    def stream(j):
        return pltpu.make_async_copy(
            leg_hbm.at[pl.ds(j % 8 * 2, 2), j // 8], leg_ref.at[j], sems.at[j]
        )

    coefficients = pltpu.make_async_copy(it_hbm, it_ref, sems.at[STREAMS])
    coefficients.start()
    for j in range(STREAMS):
        stream(j).start()
    coefficients.wait()
    low = lax.broadcasted_iota(jnp.int32, (COLS, 128), 1) < 64

    left = lax.broadcasted_iota(jnp.int32, (LATS, 128), 1) < 64

    def place(at, t, north, south):
        south = pltpu.roll(south, 64, 1)
        rows = pl.ds(at, COLS, stride=2 * PAIRS)
        wide_ref[2 * t, rows, :] = jnp.where(low, north, south)
        wide_ref[2 * t + 1, rows, :] = jnp.where(low, south, north)

    def four(j, _):
        stream(2 * j).wait()
        stream(2 * j + 1).wait()
        par, first = j // 4, j % 4 * 4
        at = par * PAIRS + first
        for k in range(4):
            for c in range(2):
                for f in range(3):
                    row = (c * 3 + f) * 4
                    value = it_ref[c, first + k, par, f]
                    if k < 2:
                        coef_ref[k, row : row + 4, :] = value
                    else:
                        row += 64 * (k - 2)
                        turn_ref[row : row + 4, :] = value
                        turn_ref[row + 32 : row + 36, :256] = value[:, :256]
                        turn_ref[row + 32 : row + 36, 256:] = -value[:, 256:]
        turned = jnp.transpose(turn_ref[...]).astype(jnp.bfloat16)
        both = jnp.where(
            left, mm(leg_ref[2 * j + 1, 0], turned), mm(leg_ref[2 * j + 1, 1], turned)
        )
        for k in range(2):
            coeff = coef_ref[k].astype(jnp.bfloat16)
            even = lax.dot_general(
                coeff[:, :256], leg_ref[2 * j, k, :, :256], NT, preferred_element_type=jnp.float32
            )
            odd = lax.dot_general(
                coeff[:, 256:], leg_ref[2 * j, k, :, 256:], NT, preferred_element_type=jnp.float32
            )
            for t in range(4):
                cut = slice(128 * t, 128 * (t + 1))
                place(at + k, t, even[:, cut] + odd[:, cut], even[:, cut] - odd[:, cut])
        for t in range(4):
            block = jnp.transpose(both[128 * t : 128 * (t + 1)])
            for k in range(2):
                north = block[64 * k : 64 * k + COLS]
                place(at + 2 + k, t, north, block[64 * k + 32 : 64 * k + 32 + COLS])
        return 0

    lax.fori_loop(0, STREAMS // 2, four, 0)
    for p in range(2):
        for c in range(2):
            for f in range(3):
                for e in range(4):
                    row = (((c * 3 + f) * 4 + e) * 2 + p) * PAIRS
                    out_ref[
                        8 * e : 8 * e + 8,
                        (2 * p + c) * PAIRS : (2 * p + c + 1) * PAIRS,
                        128 * f : 128 * (f + 1),
                    ] = wide_ref[:, row : row + PAIRS, :].astype(jnp.bfloat16)


def synthesis(it6, leg4):
    return pl.pallas_call(
        synthesis_kernel,
        in_specs=[pl.BlockSpec(memory_space=pl.ANY)] * 2,
        out_shape=jax.ShapeDtypeStruct((NBAND, 4 * PAIRS, LANES), jnp.bfloat16),
        scratch_shapes=[
            pltpu.VMEM(it6.shape, jnp.float32),
            pltpu.VMEM((STREAMS, 2, LATS, DEGREES), jnp.bfloat16),
            pltpu.SemaphoreType.DMA((STREAMS + 1,)),
            pltpu.VMEM((2, COLS, DEGREES), jnp.float32),
            pltpu.VMEM((128, DEGREES), jnp.float32),
            pltpu.VMEM((8, COLS * 2 * PAIRS, 128), jnp.float32),
        ],
        compiler_params=pltpu.CompilerParams(vmem_limit_bytes=56 * MIB),
        cost_estimate=pl.CostEstimate(
            flops=2 * 32 * COLS * LATS * DEGREES, bytes_accessed=20 * MIB, transcendentals=0
        ),
        name="synthesis",
    )(it6, leg4)


def encode(x):
    return (x * jnp.abs(x)).astype(jnp.bfloat16)


def decode(coded):
    coded = coded.astype(jnp.float32)
    root = jnp.sqrt(jnp.abs(coded))
    return jnp.where(coded < 0, -root, root)


def prepare_kernel(
    id_ref, quad_ref, st_ref, it_ref, damp_ref,
    send0_ref, send1_ref, send2_ref, send3_ref, base_ref, dense_ref,
):
    node = id_ref[0]
    place = pl.program_id(0)
    z = (node + place) % 4
    total = quad_ref[node, 0] + quad_ref[node, 1] + quad_ref[node, 2] + quad_ref[node, 3]
    diag = quad_ref[node, node]
    for k in range(8):
        mode = 2 * (8 * (z % 2) + k) + z // 2
        for f in range(3):
            rate = damp_ref[f, pl.ds(mode, 1), :]
            mine = diag * rate
            inverse = 1.0 / (1.0 + mine)
            keep = (1.0 - rate * total) * inverse
            mine = mine * inverse
            for c in range(2):
                row = COLS * k + (c * 3 + f) * 4
                start, old = st_ref[c, k, f], it_ref[c, k, f]
                dense_ref[row : row + 4, :] = old - start
                base_ref[c, k, f] = start * keep + mine * old
    for s, ref in enumerate((send0_ref, send1_ref, send2_ref, send3_ref)):

        @pl.when(place == s)
        def _(ref=ref):
            ref[...] = encode(dense_ref[...])


def own_subset(i, s):
    z = (s[0] + i) % 4
    return (0, z % 2, 0, z // 2, 0, 0, 0)


STATE = (2, None, 8, None, 3, 4, DEGREES)


def prepare(ids, quad, st7, it7, damp):
    spec = pl.BlockSpec
    state = spec(STATE, own_subset)
    return pl.pallas_call(
        prepare_kernel,
        grid_spec=pltpu.PrefetchScalarGridSpec(
            num_scalar_prefetch=1,
            grid=(4,),
            in_specs=[
                spec(memory_space=pltpu.SMEM),
                state,
                state,
                spec((3, 32, DEGREES), lambda i, s: (0, 0, 0)),
            ],
            out_specs=[spec((8 * COLS, DEGREES), lambda i, s: (0, 0))] * 4 + [state],
            scratch_shapes=[pltpu.VMEM((8 * COLS, DEGREES), jnp.float32)],
        ),
        out_shape=[jax.ShapeDtypeStruct((8 * COLS, DEGREES), jnp.bfloat16)] * 4
        + [jax.ShapeDtypeStruct(it7.shape, jnp.float32)],
        compiler_params=pltpu.CompilerParams(vmem_limit_bytes=60 * MIB),
        cost_estimate=pl.CostEstimate(
            flops=8 * 32 * COLS * DEGREES, bytes_accessed=6 * MIB, transcendentals=0
        ),
        name="prepare",
    )(ids, quad, st7, it7, damp)


def split(x):
    high = x.astype(jnp.bfloat16)
    return high, (x - high.astype(jnp.float32)).astype(jnp.bfloat16)


def table_kernel(row1_ref, row2_ref, tab_ref, back_ref, keep_ref):
    first = lax.broadcasted_iota(jnp.int32, (1, 128), 1) == 0
    halve = jnp.where(first, 0.5, 1.0)

    def rows(j, _):
        lead_c = row1_ref[0, pl.ds(j, 1), :]
        lead_s = row1_ref[1, pl.ds(j, 1), :]
        cosine = lead_c * row2_ref[0] - lead_s * row2_ref[1]
        sine = lead_s * row2_ref[0] + lead_c * row2_ref[1]
        at = pl.ds(pl.multiple_of(16 * j, 16), 16)
        keep_ref[0, at, :] = cosine
        keep_ref[1, at, :] = sine
        for t, value in enumerate((cosine, sine)):
            high, low = split(value)
            tab_ref[t, 0, at, :] = high
            tab_ref[t, 1, at, :] = low
        return 0

    lax.fori_loop(0, ROWS // 16, rows, 0)
    for t in range(2):
        for block in range(4):
            cut = slice(128 * block, 128 * (block + 1))
            value = jnp.transpose(keep_ref[t, cut, :])
            if t == 1:
                value = -value
            if block == 0:
                value = value * halve
            high, low = split(value)
            back_ref[t, 0, :, cut] = high
            back_ref[t, 1, :, cut] = low


def small_tables():
    scale = 1.0 / math.sqrt(MODES)
    step = 2.0 * math.pi / POINTS
    rows1, rows2 = [], []
    place = np.arange(NBAND)
    block = place % 4 * 8 + place // 4 % 4 * 2 + place // 16
    pairs = (block[:, None] * PAIRS + np.arange(PAIRS)).reshape(-1)
    for par in range(2):
        m = 2 * pairs + par

        def pair(k, factor):
            angle = ((k[:, None] * m[None, :]) % POINTS) * step
            return np.stack([np.cos(angle), np.sin(angle)]) * factor

        rows1.append(pair(16 * np.arange(ROWS // 16), 1.0))
        rows2.append(pair(np.arange(16), scale))
    return [np.stack(x).astype(np.float32) for x in (rows1, rows2)]


def tables(parts):
    spec = pl.BlockSpec
    return pl.pallas_call(
        table_kernel,
        grid=(2,),
        in_specs=[
            spec((None,) + x.shape[1:], lambda i, n=x.ndim: (i,) + (0,) * (n - 1)) for x in parts
        ],
        out_specs=(
            spec((2, 2, ROWS, HALF), lambda i: (i, 0, 0, 0)),
            spec((2, 2, HALF, QUARTER), lambda i: (i, 0, 0, 0)),
        ),
        out_shape=(
            jax.ShapeDtypeStruct((4, 2, ROWS, HALF), jnp.bfloat16),
            jax.ShapeDtypeStruct((4, 2, HALF, QUARTER), jnp.bfloat16),
        ),
        scratch_shapes=[pltpu.VMEM((2, ROWS, HALF), jnp.float32)],
        compiler_params=pltpu.CompilerParams(vmem_limit_bytes=60 * MIB),
        cost_estimate=pl.CostEstimate(
            flops=16 * ROWS * HALF, bytes_accessed=9 * MIB, transcendentals=0
        ),
        name="tables",
    )(*parts)


def grid_kernel(
    got_ref, tab_hbm, back_hbm, rows_ref,
    out_ref,
    tab_ref, back_ref, sems, x_ref, rest_ref, wave_ref, fold_ref, edge_ref,
):
    copies = [
        pltpu.make_async_copy(tab_hbm.at[i], tab_ref.at[i], sems.at[i]) for i in range(4)
    ] + [
        pltpu.make_async_copy(back_hbm.at[i], back_ref.at[i], sems.at[4 + i]) for i in range(4)
    ]
    for copy in copies:
        copy.start()
    index = lax.broadcasted_iota(jnp.int32, (HALF, 1), 0)
    place = index >> 4
    first = ((place & 3) * 8 + (place >> 2 & 3) * 2 + (place >> 4)) * PAIRS + (index & 15)
    for par in range(2):
        ratio = (2 * first + par).astype(jnp.float32) * (1.0 / MODES)
        for c in range(2):
            at = (2 * par + c) * PAIRS
            value = got_ref[:, at : at + PAIRS, :].reshape(HALF, LANES)
            scaled = value.astype(jnp.float32) * (ratio if c == 0 else -ratio)
            high, low = split(scaled)
            x_ref[2 * par + c, :, :LANES] = value
            x_ref[2 * par + 1 - c, :, LANES:] = high
            rest_ref[2 * par + 1 - c] = low
    for i in range(4):
        copies[i].wait()
        wave_ref[i] = mm(tab_ref[i, 0], x_ref[i]) + mm(tab_ref[i, 1], x_ref[i])
        wave_ref[i, :, LANES:] += mm(tab_ref[i, 0], rest_ref[i])
    cor = rows_ref[0:1, :]

    def quads(base, at, lanes):
        ce, se, co, so = (wave_ref[i, at, base + lanes : base + lanes + 128] for i in range(4))
        a, b, s, d = ce + co, ce - co, se + so, se - so
        return a - s, b + d, b - d, a + s

    def tendency(at):
        values = [quads(0, at, 128 * f) for f in range(3)]
        slopes = [quads(LANES, at, 128 * f) for f in range(3)]
        out = [[], [], []]
        for q in range(4):
            u, v, h = (values[f][q] for f in range(3))
            us, vs, hs = (slopes[f][q] for f in range(3))
            out[0].append(cor * v - u * us - hs)
            out[1].append(-u * vs - cor * u)
            out[2].append(-u * hs - (1.0 + h) * us)
        folded = []
        for t1, t2, t3, t4 in out:
            a, b, c, d = t1 + t4, t2 + t3, t1 - t4, t3 - t2
            folded.append((a + b, c + d, a - b, c - d))
        return folded

    def block(j, _):
        at = pl.ds(pl.multiple_of(16 * j, 16), 16)
        for f, folded in enumerate(tendency(at)):
            for i, value in enumerate(folded):
                high, low = split(value)
                fold_ref[i, at, pl.ds(128 * f, 128)] = high
                fold_ref[i, at, pl.ds(LANES + 128 * f, 128)] = low
        return 0

    lax.fori_loop(0, QUARTER // 16, block, 0)
    for f, folded in enumerate(tendency(pl.ds(QUARTER, 16))):
        edge_ref[0, :, pl.ds(128 * f, 128)] = folded[0]
        edge_ref[1, :, pl.ds(128 * f, 128)] = folded[3]

    odd_row = (lax.broadcasted_iota(jnp.int32, (HALF, 1), 0) & 1) == 1
    half_scale = 0.5 / math.sqrt(MODES)
    sign = jnp.where(odd_row, -half_scale, half_scale)
    weight, signed = rows_ref[1:2, :], rows_ref[2:3, :]
    for par in range(2):
        both = []
        for c in range(2):
            i = 2 * par + c
            copies[4 + i].wait()
            both_parts = mm(back_ref[i, 0], fold_ref[i])
            out = both_parts[:, :LANES] + both_parts[:, LANES:]
            out = out + mm(back_ref[i, 1], fold_ref[i, :, :LANES])
            if i == 0:
                out = out + sign * edge_ref[0, 0:1, :]
            if i == 3:
                out = out - sign * edge_ref[1, 0:1, :]
            both.append(out)
        for f in range(3):
            parts = []
            for out in both:
                part = out[:, 128 * f : 128 * (f + 1)]
                part = pltpu.roll(part, 64, 1) * weight + part * signed
                parts.append(part.reshape(NBAND, 2, 8, 128))
            joined = jnp.concatenate(parts, axis=2).astype(jnp.bfloat16)
            for h in range(2):
                out_ref[:, 2 * par + h, :, 128 * f : 128 * (f + 1)] = joined[:, h]


def grid_stage(got, tab, back, rows):
    return pl.pallas_call(
        grid_kernel,
        in_specs=[
            pl.BlockSpec(memory_space=pltpu.VMEM),
            pl.BlockSpec(memory_space=pl.ANY),
            pl.BlockSpec(memory_space=pl.ANY),
            pl.BlockSpec(memory_space=pltpu.VMEM),
        ],
        out_shape=jax.ShapeDtypeStruct((NBAND, 4, 16, LANES), jnp.bfloat16),
        scratch_shapes=[
            pltpu.VMEM((4, 2, ROWS, HALF), jnp.bfloat16),
            pltpu.VMEM((4, 2, HALF, QUARTER), jnp.bfloat16),
            pltpu.SemaphoreType.DMA((8,)),
            pltpu.VMEM((4, HALF, 2 * LANES), jnp.bfloat16),
            pltpu.VMEM((4, HALF, LANES), jnp.bfloat16),
            pltpu.VMEM((4, ROWS, 2 * LANES), jnp.float32),
            pltpu.VMEM((4, QUARTER, 2 * LANES), jnp.bfloat16),
            pltpu.VMEM((2, 16, LANES), jnp.float32),
        ],
        compiler_params=pltpu.CompilerParams(vmem_limit_bytes=48 * MIB),
        cost_estimate=pl.CostEstimate(
            flops=2 * 28 * ROWS * HALF * LANES, bytes_accessed=17 * MIB, transcendentals=0
        ),
        name="grid",
    )(got, tab, back, rows)


def analysis_kernel(
    id_ref, quad_ref, y_ref, leg_ref, move0_ref, move1_ref, move2_ref, move3_ref, st_ref, damp_ref,
    out0_ref, out1_ref, out2_ref, out3_ref, sums_ref,
    wide_ref, rate_ref, start_ref, mix_ref, acc_ref,
):
    step = pl.program_id(0)
    node = id_ref[0]
    order = [(node + 4 - s) % 4 for s in range(4)]

    @pl.when(step == 0)
    def _():
        acc_ref[...] = jnp.zeros_like(acc_ref)
        low = lax.broadcasted_iota(jnp.int32, (16, 128), 1) < 64
        for s in range(4):
            for f in range(3):
                for e in range(4):
                    for t in range(4):
                        first, second = (
                            y_ref[
                                (8 * e + 2 * t + g) * 4 + order[s], :, 128 * f : 128 * (f + 1)
                            ].astype(jnp.float32)
                            for g in range(2)
                        )
                        symmetric = jnp.where(low, first, second)
                        antisymmetric = jnp.where(low, second, first)
                        for c in range(2):
                            row = (((s * 2 + c) * 3 + f) * 4 + e) * 8
                            wide_ref[0, t, row : row + 8, :] = symmetric[8 * c : 8 * c + 8]
                            wide_ref[1, t, row : row + 8, :] = antisymmetric[8 * c : 8 * c + 8]

    for k in range(MB):
        at = step * MB + k
        mode = 2 * (8 * (node % 2) + at) + node // 2
        for c in range(2):
            for f in range(3):
                row = (c * 3 + f) * 4
                rate_ref[pl.ds(row, 4), :] = jnp.broadcast_to(
                    damp_ref[f, pl.ds(mode, 1), :], (4, DEGREES)
                )
                start_ref[pl.ds(row, 4), :] = st_ref[c, k, f]
        halves = []
        for h in range(2):
            spec = jnp.concatenate(
                [wide_ref[h, t, pl.ds(at, 4 * COLS, stride=8), :] for t in range(4)], axis=1
            ).astype(jnp.bfloat16)
            if h == 0:
                table = leg_ref[k, :, :256]
            else:
                blocks = [leg_ref[k, 64 * (b ^ 1) : 64 * (b ^ 1) + 64, 256:] for b in range(8)]
                table = jnp.concatenate(blocks, axis=0)
            halves.append(mm(spec, table))
        for h in range(2):
            cut = slice(256 * h, 256 * (h + 1))
            rate, start = rate_ref[:, cut], start_ref[:, cut]
            moves = [
                decode(ref[k // 2, COLS * (k % 2) : COLS * (k % 2 + 1), cut])
                for ref in (move0_ref, move1_ref, move2_ref, move3_ref)
            ]
            forces = [
                halves[h][COLS * p : COLS * (p + 1)] - rate * moves[p] for p in range(4)
            ]
            change = jnp.zeros_like(start)
            for q in range(4):
                row = [quad_ref[order[q], order[p]] for p in range(4)]
                mine = row[q] * rate
                inverse = 1.0 / (1.0 + mine)
                mixed = (
                    row[0] * forces[0] + row[1] * forces[1] + row[2] * forces[2] + row[3] * forces[3]
                ) * inverse
                total = row[0] + row[1] + row[2] + row[3]
                old = start + moves[q]
                moved = mixed + (start * (1.0 - rate * total) + mine * old) * inverse - old
                change = change + moved * moved
                mix_ref[q, COLS * k : COLS * (k + 1), cut] = mixed
            acc_ref[0, :, cut] += change
            acc_ref[1, :, cut] += start * start
    for s, ref in enumerate((out0_ref, out1_ref, out2_ref, out3_ref)):
        ref[...] = encode(mix_ref[s])

    @pl.when(step == pl.num_programs(0) - 1)
    def _():
        field = lax.broadcasted_iota(jnp.int32, (COLS, 1), 0) // 4 % 3
        lane = lax.broadcasted_iota(jnp.int32, (1, 128), 1)
        sums = jnp.zeros((1, 128), jnp.float32)
        for s in range(2):
            per_row = jnp.sum(acc_ref[s], axis=1, keepdims=True)
            for f in range(3):
                value = jnp.sum(jnp.where(field == f, per_row, 0.0), axis=0, keepdims=True)
                sums = sums + jnp.where(lane == 3 * s + f, value, 0.0)
        sums_ref[...] = jnp.broadcast_to(sums[None], sums_ref.shape)


def analysis(ids, quad, y, leg4, moves, st6, damp):
    spec = pl.BlockSpec
    return pl.pallas_call(
        analysis_kernel,
        grid_spec=pltpu.PrefetchScalarGridSpec(
            num_scalar_prefetch=1,
            grid=(2,),
            in_specs=[
                spec(memory_space=pltpu.SMEM),
                spec((4 * NBAND, 16, LANES), lambda i, s: (0, 0, 0)),
                spec(
                    (MB, None, LATS, DEGREES), lambda i, s: (s[0] % 2 * 2 + i, s[0] // 2, 0, 0)
                ),
                *[spec((2, 2 * COLS, DEGREES), lambda i, s: (i, 0, 0))] * 4,
                spec(
                    (2, MB, None, 3, 4, DEGREES),
                    lambda i, s: (0, s[0] % 2 * 2 + i, s[0] // 2, 0, 0, 0),
                ),
                spec((3, 32, DEGREES), lambda i, s: (0, 0, 0)),
            ],
            out_specs=(
                *[spec((MB * COLS, DEGREES), lambda i, s: (i, 0))] * 4,
                spec((NBAND // 2, 8, 128), lambda i, s: (0, 0, 0)),
            ),
            scratch_shapes=[
                pltpu.VMEM((2, 4, 4 * COLS * 8, 128), jnp.float32),
                pltpu.VMEM((COLS, DEGREES), jnp.float32),
                pltpu.VMEM((COLS, DEGREES), jnp.float32),
                pltpu.VMEM((4, MB * COLS, DEGREES), jnp.float32),
                pltpu.VMEM((2, COLS, DEGREES), jnp.float32),
            ],
        ),
        out_shape=(
            *[jax.ShapeDtypeStruct((8 * COLS, DEGREES), jnp.bfloat16)] * 4,
            jax.ShapeDtypeStruct((NBAND // 2, 8, 128), jnp.float32),
        ),
        compiler_params=pltpu.CompilerParams(vmem_limit_bytes=46 * MIB),
        cost_estimate=pl.CostEstimate(
            flops=2 * 32 * COLS * LATS * DEGREES, bytes_accessed=10 * MIB, transcendentals=0
        ),
        name="analysis",
    )(ids, quad, y, leg4, *moves, st6, damp)


def update_kernel(
    id_ref, mixed0_ref, mixed1_ref, mixed2_ref, mixed3_ref, base_ref, out_ref, mix_ref
):
    place = pl.program_id(0)
    for s, ref in enumerate((mixed0_ref, mixed1_ref, mixed2_ref, mixed3_ref)):

        @pl.when(place == s)
        def _(ref=ref):
            mix_ref[...] = decode(ref[...])

    for k in range(8):
        for c in range(2):
            for f in range(3):
                row = COLS * k + (c * 3 + f) * 4
                out_ref[c, k, f] = base_ref[c, k, f] + mix_ref[row : row + 4, :]


def update(ids, mixed, base):
    spec = pl.BlockSpec
    state = spec(STATE, own_subset)
    return pl.pallas_call(
        update_kernel,
        grid_spec=pltpu.PrefetchScalarGridSpec(
            num_scalar_prefetch=1,
            grid=(4,),
            in_specs=[*[spec((8 * COLS, DEGREES), lambda i, s: (0, 0))] * 4, state],
            out_specs=state,
            scratch_shapes=[pltpu.VMEM((8 * COLS, DEGREES), jnp.float32)],
        ),
        out_shape=jax.ShapeDtypeStruct(base.shape, jnp.float32),
        compiler_params=pltpu.CompilerParams(vmem_limit_bytes=32 * MIB),
        cost_estimate=pl.CostEstimate(
            flops=4 * 32 * COLS * DEGREES, bytes_accessed=5 * MIB, transcendentals=0
        ),
        name="update",
    )(ids, *mixed, base)


def exchange(x, axes):
    return lax.all_to_all(x, axes, split_axis=0, concat_axis=0, tiled=True)


def shift(x, axis, by):
    return lax.ppermute(x, axis, [(i, (i + by) % 4) for i in range(4)])


def latitude_rows(place, coriolis, lat_weight):
    count = LATS // 8
    group = place % 8
    cor = lax.dynamic_slice_in_dim(coriolis, group * count, count, 1)
    weight = lax.dynamic_slice_in_dim(lat_weight, group * count, count, 0)
    swapped = group % 2 == 1
    cor = jnp.where(swapped, cor[::-1], cor).reshape(1, 128)
    weight = jnp.concatenate([weight, weight])[None]
    south = lax.broadcasted_iota(jnp.int32, (1, 128), 1) >= count
    signed = jnp.where(south != swapped, -weight, weight)
    return jnp.concatenate([cor, weight, signed], axis=0)


def body(state0, iterate, legendre, lat_weight, coriolis, damping, quadrature):
    node = lax.axis_index("node")
    place = lax.axis_index(SEND)
    spec = iterate[0].transpose(0, 1, 3, 2, 4)
    base = state0.transpose(0, 1, 3, 2, 4)
    it6 = spec.reshape(2, PAIRS, 2, 3, 4, DEGREES)
    st6 = base.reshape(2, PAIRS, 2, 3, 4, DEGREES)
    leg4 = legendre.reshape(PAIRS, 2, LATS, DEGREES)
    damp = damping.transpose(1, 0, 2)
    ids = jnp.reshape(node, (1,)).astype(jnp.int32)

    shape7 = (2, 2, 8, 2, 3, 4, DEGREES)
    sent = synthesis(it6, leg4)
    got = exchange(sent, SEND)
    parts = [jnp.asarray(x) for x in small_tables()]
    late, _ = lax.optimization_barrier(((parts, quadrature), sent))
    parts, quad = late
    *moves, settled = prepare(ids, quad, base.reshape(shape7), spec.reshape(shape7), damp)
    moves = [moves[0]] + [shift(moves[s], "node", s) for s in (1, 2, 3)]
    tab, back = tables(parts)
    rows = latitude_rows(place, coriolis, lat_weight)
    rows, moves = lax.optimization_barrier((rows, moves))
    moves = [x.reshape(4, 2 * COLS, DEGREES) for x in moves]
    columns = grid_stage(got, tab, back, rows)
    spectra = exchange(columns.reshape(4 * NBAND, 16, LANES), SEND_NODE)
    *mixed, sums = analysis(ids, quadrature, spectra, leg4, moves, st6, damp)
    mixed = [mixed[0]] + [shift(mixed[s], "node", -s) for s in (1, 2, 3)]
    sums = exchange(sums.reshape(4 * NBAND, 1, 128), SEND_NODE)
    out = update(ids, mixed, settled)
    sums, out = lax.optimization_barrier((sums, out))
    total = jnp.sum(sums, axis=(0, 1))
    ratio = jnp.sqrt(total[:3] / (4.0 * total[3:6] + 1e-06))
    out = out.reshape(2, 32, 3, 4, DEGREES).transpose(0, 1, 3, 2, 4)
    return (out[None], ratio)


def solution(mesh):
    torus = Mesh(
        mesh.devices.reshape(mesh.shape["node"], 4, 4, 2), ("node", "band_0", "band_1", "band_2")
    )
    return jax.shard_map(
        body,
        mesh=torus,
        in_specs=(
            P(None, BAND, None, None, None),
            P("node", None, BAND, None, None, None),
            P(BAND, None, None),
            P(),
            P(),
            P(BAND, None, None),
            P(),
        ),
        out_specs=(P("node", None, BAND, None, None, None), P()),
        check_vma=False,
    )
```

```python
import functools
import math

import jax
import jax.numpy as jnp
import numpy as np
from jax import lax
from jax.experimental import pallas as pl
from jax.experimental.pallas import tpu as pltpu
from jax.sharding import Mesh
from jax.sharding import PartitionSpec as P

BAND = ("band_0", "band_1", "band_2")
SEND = ("band_2", "band_1", "band_0")
SEND_NODE = SEND + ("node",)
MODES = 1024
POINTS = 2 * MODES
HALF = MODES // 2
QUARTER = POINTS // 4
ROWS = QUARTER + 16
LATS = 512
DEGREES = 512
NBAND = 32
PAIRS = 16
COLS = 24
LANES = 384
MB = 4
MIB = 1 << 20


NT = (((1,), (1,)), ((), ()))


def mm(a, b):
    return jnp.dot(a, b, preferred_element_type=jnp.float32)


STREAMS = 16


def synthesis_kernel(it_hbm, leg_hbm, out_ref, it_ref, leg_ref, sems, coef_ref, turn_ref, wide_ref):
    def stream(j):
        return pltpu.make_async_copy(
            leg_hbm.at[pl.ds(j % 8 * 2, 2), j // 8], leg_ref.at[j], sems.at[j]
        )

    coefficients = pltpu.make_async_copy(it_hbm, it_ref, sems.at[STREAMS])
    coefficients.start()
    for j in range(STREAMS):
        stream(j).start()
    coefficients.wait()
    low = lax.broadcasted_iota(jnp.int32, (COLS, 128), 1) < 64

    left = lax.broadcasted_iota(jnp.int32, (LATS, 128), 1) < 64

    def place(at, t, north, south):
        south = pltpu.roll(south, 64, 1)
        rows = pl.ds(at, COLS, stride=2 * PAIRS)
        wide_ref[2 * t, rows, :] = jnp.where(low, north, south)
        wide_ref[2 * t + 1, rows, :] = jnp.where(low, south, north)

    def four(j, _):
        stream(2 * j).wait()
        stream(2 * j + 1).wait()
        par, first = j // 4, j % 4 * 4
        at = par * PAIRS + first
        for k in range(4):
            for c in range(2):
                for f in range(3):
                    row = (c * 3 + f) * 4
                    value = it_ref[c, first + k, par, f]
                    if k < 2:
                        coef_ref[k, row : row + 4, :] = value
                    else:
                        row += 64 * (k - 2)
                        turn_ref[row : row + 4, :] = value
                        turn_ref[row + 32 : row + 36, :256] = value[:, :256]
                        turn_ref[row + 32 : row + 36, 256:] = -value[:, 256:]
        turned = jnp.transpose(turn_ref[...]).astype(jnp.bfloat16)
        both = jnp.where(
            left, mm(leg_ref[2 * j + 1, 0], turned), mm(leg_ref[2 * j + 1, 1], turned)
        )
        for k in range(2):
            coeff = coef_ref[k].astype(jnp.bfloat16)
            even = lax.dot_general(
                coeff[:, :256], leg_ref[2 * j, k, :, :256], NT, preferred_element_type=jnp.float32
            )
            odd = lax.dot_general(
                coeff[:, 256:], leg_ref[2 * j, k, :, 256:], NT, preferred_element_type=jnp.float32
            )
            for t in range(4):
                cut = slice(128 * t, 128 * (t + 1))
                place(at + k, t, even[:, cut] + odd[:, cut], even[:, cut] - odd[:, cut])
        for t in range(4):
            block = jnp.transpose(both[128 * t : 128 * (t + 1)])
            for k in range(2):
                north = block[64 * k : 64 * k + COLS]
                place(at + 2 + k, t, north, block[64 * k + 32 : 64 * k + 32 + COLS])
        return 0

    lax.fori_loop(0, STREAMS // 2, four, 0)
    for p in range(2):
        for c in range(2):
            for f in range(3):
                for e in range(4):
                    row = (((c * 3 + f) * 4 + e) * 2 + p) * PAIRS
                    out_ref[
                        8 * e : 8 * e + 8,
                        (2 * p + c) * PAIRS : (2 * p + c + 1) * PAIRS,
                        128 * f : 128 * (f + 1),
                    ] = wide_ref[:, row : row + PAIRS, :].astype(jnp.bfloat16)


def synthesis(it6, leg4):
    return pl.pallas_call(
        synthesis_kernel,
        in_specs=[pl.BlockSpec(memory_space=pl.ANY)] * 2,
        out_shape=jax.ShapeDtypeStruct((NBAND, 4 * PAIRS, LANES), jnp.bfloat16),
        scratch_shapes=[
            pltpu.VMEM(it6.shape, jnp.float32),
            pltpu.VMEM((STREAMS, 2, LATS, DEGREES), jnp.bfloat16),
            pltpu.SemaphoreType.DMA((STREAMS + 1,)),
            pltpu.VMEM((2, COLS, DEGREES), jnp.float32),
            pltpu.VMEM((128, DEGREES), jnp.float32),
            pltpu.VMEM((8, (COLS + 1) * 2 * PAIRS, 128), jnp.float32),
        ],
        compiler_params=pltpu.CompilerParams(vmem_limit_bytes=56 * MIB),
        cost_estimate=pl.CostEstimate(
            flops=2 * 32 * COLS * LATS * DEGREES, bytes_accessed=20 * MIB, transcendentals=0
        ),
        name="synthesis",
    )(it6, leg4)


def encode(x):
    return (x * jnp.abs(x)).astype(jnp.bfloat16)


def decode(coded):
    coded = coded.astype(jnp.float32)
    root = jnp.sqrt(jnp.abs(coded))
    return jnp.where(coded < 0, -root, root)


def prepare_kernel(
    id_ref, quad_ref, st_ref, it_ref, damp_ref,
    send0_ref, send1_ref, send2_ref, send3_ref, base_ref, dense_ref,
):
    node = id_ref[0]
    place = pl.program_id(0)
    z = (node + place) % 4
    total = quad_ref[node, 0] + quad_ref[node, 1] + quad_ref[node, 2] + quad_ref[node, 3]
    diag = quad_ref[node, node]
    for k in range(8):
        mode = 2 * (8 * (z % 2) + k) + z // 2
        for f in range(3):
            rate = damp_ref[f, pl.ds(mode, 1), :]
            mine = diag * rate
            inverse = 1.0 / (1.0 + mine)
            keep = (1.0 - rate * total) * inverse
            mine = mine * inverse
            for c in range(2):
                row = COLS * k + (c * 3 + f) * 4
                start, old = st_ref[c, k, f], it_ref[c, k, f]
                dense_ref[row : row + 4, :] = old - start
                base_ref[c, k, f] = start * keep + mine * old
    for s, ref in enumerate((send0_ref, send1_ref, send2_ref, send3_ref)):

        @pl.when(place == s)
        def _(ref=ref):
            ref[...] = encode(dense_ref[...])


def own_subset(i, s):
    z = (s[0] + i) % 4
    return (0, z % 2, 0, z // 2, 0, 0, 0)


STATE = (2, None, 8, None, 3, 4, DEGREES)


def prepare(ids, quad, st7, it7, damp):
    spec = pl.BlockSpec
    state = spec(STATE, own_subset)
    return pl.pallas_call(
        prepare_kernel,
        grid_spec=pltpu.PrefetchScalarGridSpec(
            num_scalar_prefetch=1,
            grid=(4,),
            in_specs=[
                spec(memory_space=pltpu.SMEM),
                state,
                state,
                spec((3, 32, DEGREES), lambda i, s: (0, 0, 0)),
            ],
            out_specs=[spec((8 * COLS, DEGREES), lambda i, s: (0, 0))] * 4 + [state],
            scratch_shapes=[pltpu.VMEM((8 * COLS, DEGREES), jnp.float32)],
        ),
        out_shape=[jax.ShapeDtypeStruct((8 * COLS, DEGREES), jnp.bfloat16)] * 4
        + [jax.ShapeDtypeStruct(it7.shape, jnp.float32)],
        compiler_params=pltpu.CompilerParams(vmem_limit_bytes=60 * MIB),
        cost_estimate=pl.CostEstimate(
            flops=8 * 32 * COLS * DEGREES, bytes_accessed=6 * MIB, transcendentals=0
        ),
        name="prepare",
    )(ids, quad, st7, it7, damp)


def split(x):
    high = x.astype(jnp.bfloat16)
    return high, (x - high.astype(jnp.float32)).astype(jnp.bfloat16)


def table_kernel(row1_ref, row2_ref, tab_ref, back_ref, keep_ref):
    first = lax.broadcasted_iota(jnp.int32, (1, 128), 1) == 0
    halve = jnp.where(first, 0.5, 1.0)

    def rows(j, _):
        lead_c = row1_ref[0, pl.ds(j, 1), :]
        lead_s = row1_ref[1, pl.ds(j, 1), :]
        cosine = lead_c * row2_ref[0] - lead_s * row2_ref[1]
        sine = lead_s * row2_ref[0] + lead_c * row2_ref[1]
        at = pl.ds(pl.multiple_of(16 * j, 16), 16)
        keep_ref[0, at, :] = cosine
        keep_ref[1, at, :] = sine
        for t, value in enumerate((cosine, sine)):
            high, low = split(value)
            tab_ref[t, 0, at, :] = high
            tab_ref[t, 1, at, :] = low
        return 0

    lax.fori_loop(0, ROWS // 16, rows, 0)
    for t in range(2):
        for block in range(4):
            cut = slice(128 * block, 128 * (block + 1))
            value = jnp.transpose(keep_ref[t, cut, :])
            if t == 1:
                value = -value
            if block == 0:
                value = value * halve
            high, low = split(value)
            back_ref[t, 0, :, cut] = high
            back_ref[t, 1, :, cut] = low


def small_tables():
    scale = 1.0 / math.sqrt(MODES)
    step = 2.0 * math.pi / POINTS
    rows1, rows2 = [], []
    place = np.arange(NBAND)
    block = place % 4 * 8 + place // 4 % 4 * 2 + place // 16
    pairs = (block[:, None] * PAIRS + np.arange(PAIRS)).reshape(-1)
    for par in range(2):
        m = 2 * pairs + par

        def pair(k, factor):
            angle = ((k[:, None] * m[None, :]) % POINTS) * step
            return np.stack([np.cos(angle), np.sin(angle)]) * factor

        rows1.append(pair(16 * np.arange(ROWS // 16), 1.0))
        rows2.append(pair(np.arange(16), scale))
    return [np.stack(x).astype(np.float32) for x in (rows1, rows2)]


def tables(parts):
    spec = pl.BlockSpec
    return pl.pallas_call(
        table_kernel,
        grid=(2,),
        in_specs=[
            spec((None,) + x.shape[1:], lambda i, n=x.ndim: (i,) + (0,) * (n - 1)) for x in parts
        ],
        out_specs=(
            spec((2, 2, ROWS, HALF), lambda i: (i, 0, 0, 0)),
            spec((2, 2, HALF, QUARTER), lambda i: (i, 0, 0, 0)),
        ),
        out_shape=(
            jax.ShapeDtypeStruct((4, 2, ROWS, HALF), jnp.bfloat16),
            jax.ShapeDtypeStruct((4, 2, HALF, QUARTER), jnp.bfloat16),
        ),
        scratch_shapes=[pltpu.VMEM((2, ROWS, HALF), jnp.float32)],
        compiler_params=pltpu.CompilerParams(vmem_limit_bytes=60 * MIB),
        cost_estimate=pl.CostEstimate(
            flops=16 * ROWS * HALF, bytes_accessed=9 * MIB, transcendentals=0
        ),
        name="tables",
    )(*parts)


def grid_kernel(
    got_ref, tab_hbm, back_hbm, rows_ref,
    out_ref,
    tab_ref, back_ref, sems, x_ref, rest_ref, wave_ref, fold_ref, edge_ref,
):
    copies = [
        pltpu.make_async_copy(tab_hbm.at[i], tab_ref.at[i], sems.at[i]) for i in range(4)
    ] + [
        pltpu.make_async_copy(back_hbm.at[i], back_ref.at[i], sems.at[4 + i]) for i in range(4)
    ]
    for copy in copies:
        copy.start()
    index = lax.broadcasted_iota(jnp.int32, (HALF, 1), 0)
    place = index >> 4
    first = ((place & 3) * 8 + (place >> 2 & 3) * 2 + (place >> 4)) * PAIRS + (index & 15)
    for par in range(2):
        ratio = (2 * first + par).astype(jnp.float32) * (1.0 / MODES)
        for c in range(2):
            at = (2 * par + c) * PAIRS
            value = got_ref[:, at : at + PAIRS, :].reshape(HALF, LANES)
            scaled = value.astype(jnp.float32) * (ratio if c == 0 else -ratio)
            high, low = split(scaled)
            x_ref[2 * par + c, :, :LANES] = value
            x_ref[2 * par + 1 - c, :, LANES:] = high
            rest_ref[2 * par + 1 - c] = low
    for i in range(4):
        copies[i].wait()
        wave_ref[i] = mm(tab_ref[i, 0], x_ref[i]) + mm(tab_ref[i, 1], x_ref[i])
        wave_ref[i, :, LANES:] += mm(tab_ref[i, 0], rest_ref[i])
    cor = rows_ref[0:1, :]

    def quads(base, at, lanes):
        ce, se, co, so = (wave_ref[i, at, base + lanes : base + lanes + 128] for i in range(4))
        a, b, s, d = ce + co, ce - co, se + so, se - so
        return a - s, b + d, b - d, a + s

    def tendency(at):
        values = [quads(0, at, 128 * f) for f in range(3)]
        slopes = [quads(LANES, at, 128 * f) for f in range(3)]
        out = [[], [], []]
        for q in range(4):
            u, v, h = (values[f][q] for f in range(3))
            us, vs, hs = (slopes[f][q] for f in range(3))
            out[0].append(cor * v - u * us - hs)
            out[1].append(-u * vs - cor * u)
            out[2].append(-u * hs - (1.0 + h) * us)
        folded = []
        for t1, t2, t3, t4 in out:
            a, b, c, d = t1 + t4, t2 + t3, t1 - t4, t3 - t2
            folded.append((a + b, c + d, a - b, c - d))
        return folded

    def block(j, _):
        at = pl.ds(pl.multiple_of(16 * j, 16), 16)
        for f, folded in enumerate(tendency(at)):
            for i, value in enumerate(folded):
                high, low = split(value)
                fold_ref[i, at, pl.ds(128 * f, 128)] = high
                fold_ref[i, at, pl.ds(LANES + 128 * f, 128)] = low
        return 0

    lax.fori_loop(0, QUARTER // 16, block, 0)
    for f, folded in enumerate(tendency(pl.ds(QUARTER, 16))):
        edge_ref[0, :, pl.ds(128 * f, 128)] = folded[0]
        edge_ref[1, :, pl.ds(128 * f, 128)] = folded[3]

    odd_row = (lax.broadcasted_iota(jnp.int32, (HALF, 1), 0) & 1) == 1
    half_scale = 0.5 / math.sqrt(MODES)
    sign = jnp.where(odd_row, -half_scale, half_scale)
    weight, signed = rows_ref[1:2, :], rows_ref[2:3, :]
    for par in range(2):
        both = []
        for c in range(2):
            i = 2 * par + c
            copies[4 + i].wait()
            both_parts = mm(back_ref[i, 0], fold_ref[i])
            out = both_parts[:, :LANES] + both_parts[:, LANES:]
            out = out + mm(back_ref[i, 1], fold_ref[i, :, :LANES])
            if i == 0:
                out = out + sign * edge_ref[0, 0:1, :]
            if i == 3:
                out = out - sign * edge_ref[1, 0:1, :]
            both.append(out)
        for f in range(3):
            parts = []
            for out in both:
                part = out[:, 128 * f : 128 * (f + 1)]
                part = pltpu.roll(part, 64, 1) * weight + part * signed
                parts.append(part.reshape(NBAND, 2, 8, 128))
            joined = jnp.concatenate(parts, axis=2).astype(jnp.bfloat16)
            for h in range(2):
                out_ref[:, 2 * par + h, :, 128 * f : 128 * (f + 1)] = joined[:, h]


def grid_stage(got, tab, back, rows):
    return pl.pallas_call(
        grid_kernel,
        in_specs=[
            pl.BlockSpec(memory_space=pltpu.VMEM),
            pl.BlockSpec(memory_space=pl.ANY),
            pl.BlockSpec(memory_space=pl.ANY),
            pl.BlockSpec(memory_space=pltpu.VMEM),
        ],
        out_shape=jax.ShapeDtypeStruct((NBAND, 4, 16, LANES), jnp.bfloat16),
        scratch_shapes=[
            pltpu.VMEM((4, 2, ROWS, HALF), jnp.bfloat16),
            pltpu.VMEM((4, 2, HALF, QUARTER), jnp.bfloat16),
            pltpu.SemaphoreType.DMA((8,)),
            pltpu.VMEM((4, HALF, 2 * LANES), jnp.bfloat16),
            pltpu.VMEM((4, HALF, LANES), jnp.bfloat16),
            pltpu.VMEM((4, ROWS, 2 * LANES), jnp.float32),
            pltpu.VMEM((4, QUARTER, 2 * LANES), jnp.bfloat16),
            pltpu.VMEM((2, 16, LANES), jnp.float32),
        ],
        compiler_params=pltpu.CompilerParams(vmem_limit_bytes=48 * MIB),
        cost_estimate=pl.CostEstimate(
            flops=2 * 28 * ROWS * HALF * LANES, bytes_accessed=17 * MIB, transcendentals=0
        ),
        name="grid",
    )(got, tab, back, rows)


def analysis_kernel(
    id_ref, quad_ref, y_ref, leg_ref, move0_ref, move1_ref, move2_ref, move3_ref, st_ref, damp_ref,
    out0_ref, out1_ref, out2_ref, out3_ref, sums_ref,
    wide_ref, rate_ref, start_ref, mix_ref, acc_ref,
):
    step = pl.program_id(0)
    node = id_ref[0]
    order = [(node + 4 - s) % 4 for s in range(4)]

    @pl.when(step == 0)
    def _():
        acc_ref[...] = jnp.zeros_like(acc_ref)
        low = lax.broadcasted_iota(jnp.int32, (16, 128), 1) < 64
        for s in range(4):
            for f in range(3):
                for e in range(4):
                    for t in range(4):
                        first, second = (
                            y_ref[
                                (8 * e + 2 * t + g) * 4 + order[s], :, 128 * f : 128 * (f + 1)
                            ].astype(jnp.float32)
                            for g in range(2)
                        )
                        symmetric = jnp.where(low, first, second)
                        antisymmetric = jnp.where(low, second, first)
                        for c in range(2):
                            row = (((s * 2 + c) * 3 + f) * 4 + e) * 8
                            wide_ref[0, t, row : row + 8, :] = symmetric[8 * c : 8 * c + 8]
                            wide_ref[1, t, row : row + 8, :] = antisymmetric[8 * c : 8 * c + 8]

    for k in range(MB):
        at = step * MB + k
        mode = 2 * (8 * (node % 2) + at) + node // 2
        for c in range(2):
            for f in range(3):
                row = (c * 3 + f) * 4
                rate_ref[pl.ds(row, 4), :] = jnp.broadcast_to(
                    damp_ref[f, pl.ds(mode, 1), :], (4, DEGREES)
                )
                start_ref[pl.ds(row, 4), :] = st_ref[c, k, f]
        halves = []
        for h in range(2):
            spec = jnp.concatenate(
                [wide_ref[h, t, pl.ds(at, 4 * COLS, stride=8), :] for t in range(4)], axis=1
            ).astype(jnp.bfloat16)
            if h == 0:
                table = leg_ref[k, :, :256]
            else:
                blocks = [leg_ref[k, 64 * (b ^ 1) : 64 * (b ^ 1) + 64, 256:] for b in range(8)]
                table = jnp.concatenate(blocks, axis=0)
            halves.append(mm(spec, table))
        for h in range(2):
            cut = slice(256 * h, 256 * (h + 1))
            rate, start = rate_ref[:, cut], start_ref[:, cut]
            moves = [
                decode(ref[k // 2, COLS * (k % 2) : COLS * (k % 2 + 1), cut])
                for ref in (move0_ref, move1_ref, move2_ref, move3_ref)
            ]
            forces = [
                halves[h][COLS * p : COLS * (p + 1)] - rate * moves[p] for p in range(4)
            ]
            change = jnp.zeros_like(start)
            for q in range(4):
                row = [quad_ref[order[q], order[p]] for p in range(4)]
                mine = row[q] * rate
                inverse = 1.0 / (1.0 + mine)
                mixed = (
                    row[0] * forces[0] + row[1] * forces[1] + row[2] * forces[2] + row[3] * forces[3]
                ) * inverse
                total = row[0] + row[1] + row[2] + row[3]
                old = start + moves[q]
                moved = mixed + (start * (1.0 - rate * total) + mine * old) * inverse - old
                change = change + moved * moved
                mix_ref[q, COLS * k : COLS * (k + 1), cut] = mixed
            acc_ref[0, :, cut] += change
            acc_ref[1, :, cut] += start * start
    for s, ref in enumerate((out0_ref, out1_ref, out2_ref, out3_ref)):
        ref[...] = encode(mix_ref[s])

    @pl.when(step == pl.num_programs(0) - 1)
    def _():
        field = lax.broadcasted_iota(jnp.int32, (COLS, 1), 0) // 4 % 3
        lane = lax.broadcasted_iota(jnp.int32, (1, 128), 1)
        sums = jnp.zeros((1, 128), jnp.float32)
        for s in range(2):
            per_row = jnp.sum(acc_ref[s], axis=1, keepdims=True)
            for f in range(3):
                value = jnp.sum(jnp.where(field == f, per_row, 0.0), axis=0, keepdims=True)
                sums = sums + jnp.where(lane == 3 * s + f, value, 0.0)
        sums_ref[...] = jnp.broadcast_to(sums[None], sums_ref.shape)


def analysis(ids, quad, y, leg4, moves, st6, damp):
    spec = pl.BlockSpec
    return pl.pallas_call(
        analysis_kernel,
        grid_spec=pltpu.PrefetchScalarGridSpec(
            num_scalar_prefetch=1,
            grid=(2,),
            in_specs=[
                spec(memory_space=pltpu.SMEM),
                spec((4 * NBAND, 16, LANES), lambda i, s: (0, 0, 0)),
                spec(
                    (MB, None, LATS, DEGREES), lambda i, s: (s[0] % 2 * 2 + i, s[0] // 2, 0, 0)
                ),
                *[spec((2, 2 * COLS, DEGREES), lambda i, s: (i, 0, 0))] * 4,
                spec(
                    (2, MB, None, 3, 4, DEGREES),
                    lambda i, s: (0, s[0] % 2 * 2 + i, s[0] // 2, 0, 0, 0),
                ),
                spec((3, 32, DEGREES), lambda i, s: (0, 0, 0)),
            ],
            out_specs=(
                *[spec((MB * COLS, DEGREES), lambda i, s: (i, 0))] * 4,
                spec((NBAND // 2, 8, 128), lambda i, s: (0, 0, 0)),
            ),
            scratch_shapes=[
                pltpu.VMEM((2, 4, (4 * COLS + 1) * 8, 128), jnp.float32),
                pltpu.VMEM((COLS, DEGREES), jnp.float32),
                pltpu.VMEM((COLS, DEGREES), jnp.float32),
                pltpu.VMEM((4, MB * COLS, DEGREES), jnp.float32),
                pltpu.VMEM((2, COLS, DEGREES), jnp.float32),
            ],
        ),
        out_shape=(
            *[jax.ShapeDtypeStruct((8 * COLS, DEGREES), jnp.bfloat16)] * 4,
            jax.ShapeDtypeStruct((NBAND // 2, 8, 128), jnp.float32),
        ),
        compiler_params=pltpu.CompilerParams(vmem_limit_bytes=46 * MIB),
        cost_estimate=pl.CostEstimate(
            flops=2 * 32 * COLS * LATS * DEGREES, bytes_accessed=10 * MIB, transcendentals=0
        ),
        name="analysis",
    )(ids, quad, y, leg4, *moves, st6, damp)


def update_kernel(
    id_ref, mixed0_ref, mixed1_ref, mixed2_ref, mixed3_ref, base_ref, out_ref, mix_ref
):
    place = pl.program_id(0)
    for s, ref in enumerate((mixed0_ref, mixed1_ref, mixed2_ref, mixed3_ref)):

        @pl.when(place == s)
        def _(ref=ref):
            mix_ref[...] = decode(ref[...])

    for k in range(8):
        for c in range(2):
            for f in range(3):
                row = COLS * k + (c * 3 + f) * 4
                out_ref[c, k, f] = base_ref[c, k, f] + mix_ref[row : row + 4, :]


def update(ids, mixed, base):
    spec = pl.BlockSpec
    state = spec(STATE, own_subset)
    return pl.pallas_call(
        update_kernel,
        grid_spec=pltpu.PrefetchScalarGridSpec(
            num_scalar_prefetch=1,
            grid=(4,),
            in_specs=[*[spec((8 * COLS, DEGREES), lambda i, s: (0, 0))] * 4, state],
            out_specs=state,
            scratch_shapes=[pltpu.VMEM((8 * COLS, DEGREES), jnp.float32)],
        ),
        out_shape=jax.ShapeDtypeStruct(base.shape, jnp.float32),
        compiler_params=pltpu.CompilerParams(vmem_limit_bytes=32 * MIB),
        cost_estimate=pl.CostEstimate(
            flops=4 * 32 * COLS * DEGREES, bytes_accessed=5 * MIB, transcendentals=0
        ),
        name="update",
    )(ids, *mixed, base)


def exchange(x, axes):
    return lax.all_to_all(x, axes, split_axis=0, concat_axis=0, tiled=True)


def shift(x, axis, by):
    return lax.ppermute(x, axis, [(i, (i + by) % 4) for i in range(4)])


def latitude_rows(place, coriolis, lat_weight):
    count = LATS // 8
    group = place % 8
    cor = lax.dynamic_slice_in_dim(coriolis, group * count, count, 1)
    weight = lax.dynamic_slice_in_dim(lat_weight, group * count, count, 0)
    swapped = group % 2 == 1
    cor = jnp.where(swapped, cor[::-1], cor).reshape(1, 128)
    weight = jnp.concatenate([weight, weight])[None]
    south = lax.broadcasted_iota(jnp.int32, (1, 128), 1) >= count
    signed = jnp.where(south != swapped, -weight, weight)
    return jnp.concatenate([cor, weight, signed], axis=0)


def body(state0, iterate, legendre, lat_weight, coriolis, damping, quadrature):
    node = lax.axis_index("node")
    place = lax.axis_index(SEND)
    spec = iterate[0].transpose(0, 1, 3, 2, 4)
    base = state0.transpose(0, 1, 3, 2, 4)
    it6 = spec.reshape(2, PAIRS, 2, 3, 4, DEGREES)
    st6 = base.reshape(2, PAIRS, 2, 3, 4, DEGREES)
    leg4 = legendre.reshape(PAIRS, 2, LATS, DEGREES)
    damp = damping.transpose(1, 0, 2)
    ids = jnp.reshape(node, (1,)).astype(jnp.int32)

    shape7 = (2, 2, 8, 2, 3, 4, DEGREES)
    sent = synthesis(it6, leg4)
    got = exchange(sent, SEND)
    parts = [jnp.asarray(x) for x in small_tables()]
    late, _ = lax.optimization_barrier(((parts, quadrature), sent))
    parts, quad = late
    *moves, settled = prepare(ids, quad, base.reshape(shape7), spec.reshape(shape7), damp)
    moves = [moves[0]] + [shift(moves[s], "node", s) for s in (1, 2, 3)]
    tab, back = tables(parts)
    rows = latitude_rows(place, coriolis, lat_weight)
    rows, moves = lax.optimization_barrier((rows, moves))
    moves = [x.reshape(4, 2 * COLS, DEGREES) for x in moves]
    columns = grid_stage(got, tab, back, rows)
    spectra = exchange(columns.reshape(4 * NBAND, 16, LANES), SEND_NODE)
    *mixed, sums = analysis(ids, quadrature, spectra, leg4, moves, st6, damp)
    mixed = [mixed[0]] + [shift(mixed[s], "node", -s) for s in (1, 2, 3)]
    sums = exchange(sums.reshape(4 * NBAND, 1, 128), SEND_NODE)
    out = update(ids, mixed, settled)
    sums, out = lax.optimization_barrier((sums, out))
    total = jnp.sum(sums, axis=(0, 1))
    ratio = jnp.sqrt(total[:3] / (4.0 * total[3:6] + 1e-06))
    out = out.reshape(2, 32, 3, 4, DEGREES).transpose(0, 1, 3, 2, 4)
    return (out[None], ratio)


def solution(mesh):
    torus = Mesh(
        mesh.devices.reshape(mesh.shape["node"], 4, 4, 2), ("node", "band_0", "band_1", "band_2")
    )
    return jax.shard_map(
        body,
        mesh=torus,
        in_specs=(
            P(None, BAND, None, None, None),
            P("node", None, BAND, None, None, None),
            P(BAND, None, None),
            P(),
            P(),
            P(BAND, None, None),
            P(),
        ),
        out_specs=(P("node", None, BAND, None, None, None), P()),
        check_vma=False,
    )
```

```python
import functools
import math

import jax
import jax.numpy as jnp
import numpy as np
from jax import lax
from jax.experimental import pallas as pl
from jax.experimental.pallas import tpu as pltpu
from jax.sharding import Mesh
from jax.sharding import PartitionSpec as P

BAND = ("band_0", "band_1", "band_2")
SEND = ("band_2", "band_1", "band_0")
SEND_NODE = SEND + ("node",)
MODES = 1024
POINTS = 2 * MODES
HALF = MODES // 2
QUARTER = POINTS // 4
ROWS = QUARTER + 16
LATS = 512
DEGREES = 512
NBAND = 32
PAIRS = 16
COLS = 24
LANES = 384
MB = 4
MIB = 1 << 20


NT = (((1,), (1,)), ((), ()))


def mm(a, b):
    return jnp.dot(a, b, preferred_element_type=jnp.float32)


STREAMS = 16


def synthesis_kernel(it_hbm, leg_hbm, out_ref, it_ref, leg_ref, sems, coef_ref, turn_ref, wide_ref):
    def stream(j):
        return pltpu.make_async_copy(
            leg_hbm.at[pl.ds(j % 8 * 2, 2), j // 8], leg_ref.at[j], sems.at[j]
        )

    coefficients = [
        pltpu.make_async_copy(it_hbm.at[:, :, p], it_ref.at[:, :, p], sems.at[STREAMS + p])
        for p in range(2)
    ]
    for p in range(2):
        coefficients[p].start()
        for j in range(8 * p, 8 * p + 8):
            stream(j).start()
    low = lax.broadcasted_iota(jnp.int32, (COLS, 128), 1) < 64

    left = lax.broadcasted_iota(jnp.int32, (LATS, 128), 1) < 64

    def place(at, t, north, south):
        south = pltpu.roll(south, 64, 1)
        rows = pl.ds(at, COLS, stride=2 * PAIRS)
        wide_ref[2 * t, rows, :] = jnp.where(low, north, south)
        wide_ref[2 * t + 1, rows, :] = jnp.where(low, south, north)

    def four(j, _):
        stream(2 * j).wait()
        stream(2 * j + 1).wait()
        par, first = j // 4, j % 4 * 4
        at = par * PAIRS + first
        for k in range(4):
            for c in range(2):
                for f in range(3):
                    row = (c * 3 + f) * 4
                    value = it_ref[c, first + k, par, f]
                    if k < 2:
                        coef_ref[k, row : row + 4, :] = value
                    else:
                        row += 64 * (k - 2)
                        turn_ref[row : row + 4, :] = value
                        turn_ref[row + 32 : row + 36, :256] = value[:, :256]
                        turn_ref[row + 32 : row + 36, 256:] = -value[:, 256:]
        turned = jnp.transpose(turn_ref[...]).astype(jnp.bfloat16)
        both = jnp.where(
            left, mm(leg_ref[2 * j + 1, 0], turned), mm(leg_ref[2 * j + 1, 1], turned)
        )
        for k in range(2):
            coeff = coef_ref[k].astype(jnp.bfloat16)
            even = lax.dot_general(
                coeff[:, :256], leg_ref[2 * j, k, :, :256], NT, preferred_element_type=jnp.float32
            )
            odd = lax.dot_general(
                coeff[:, 256:], leg_ref[2 * j, k, :, 256:], NT, preferred_element_type=jnp.float32
            )
            for t in range(4):
                cut = slice(128 * t, 128 * (t + 1))
                place(at + k, t, even[:, cut] + odd[:, cut], even[:, cut] - odd[:, cut])
        for t in range(4):
            block = jnp.transpose(both[128 * t : 128 * (t + 1)])
            for k in range(2):
                north = block[64 * k : 64 * k + COLS]
                place(at + 2 + k, t, north, block[64 * k + 32 : 64 * k + 32 + COLS])
        return 0

    for p in range(2):
        coefficients[p].wait()
        lax.fori_loop(4 * p, 4 * p + 4, four, 0)
    for p in range(2):
        for c in range(2):
            for f in range(3):
                for e in range(4):
                    row = (((c * 3 + f) * 4 + e) * 2 + p) * PAIRS
                    out_ref[
                        8 * e : 8 * e + 8,
                        (2 * p + c) * PAIRS : (2 * p + c + 1) * PAIRS,
                        128 * f : 128 * (f + 1),
                    ] = wide_ref[:, row : row + PAIRS, :].astype(jnp.bfloat16)


def synthesis(it6, leg4):
    return pl.pallas_call(
        synthesis_kernel,
        in_specs=[pl.BlockSpec(memory_space=pl.ANY)] * 2,
        out_shape=jax.ShapeDtypeStruct((NBAND, 4 * PAIRS, LANES), jnp.bfloat16),
        scratch_shapes=[
            pltpu.VMEM(it6.shape, jnp.float32),
            pltpu.VMEM((STREAMS, 2, LATS, DEGREES), jnp.bfloat16),
            pltpu.SemaphoreType.DMA((STREAMS + 2,)),
            pltpu.VMEM((2, COLS, DEGREES), jnp.float32),
            pltpu.VMEM((128, DEGREES), jnp.float32),
            pltpu.VMEM((8, (COLS + 1) * 2 * PAIRS, 128), jnp.float32),
        ],
        compiler_params=pltpu.CompilerParams(vmem_limit_bytes=56 * MIB),
        cost_estimate=pl.CostEstimate(
            flops=2 * 32 * COLS * LATS * DEGREES, bytes_accessed=20 * MIB, transcendentals=0
        ),
        name="synthesis",
    )(it6, leg4)


def encode(x):
    return (x * jnp.abs(x)).astype(jnp.bfloat16)


def decode(coded):
    coded = coded.astype(jnp.float32)
    root = jnp.sqrt(jnp.abs(coded))
    return jnp.where(coded < 0, -root, root)


def prepare_kernel(
    id_ref, quad_ref, st_ref, it_ref, damp_ref,
    send0_ref, send1_ref, send2_ref, send3_ref, base_ref, dense_ref,
):
    node = id_ref[0]
    place = pl.program_id(0)
    z = (node + place) % 4
    total = quad_ref[node, 0] + quad_ref[node, 1] + quad_ref[node, 2] + quad_ref[node, 3]
    diag = quad_ref[node, node]
    for k in range(8):
        mode = 2 * (8 * (z % 2) + k) + z // 2
        for f in range(3):
            rate = damp_ref[f, pl.ds(mode, 1), :]
            mine = diag * rate
            inverse = 1.0 / (1.0 + mine)
            keep = (1.0 - rate * total) * inverse
            mine = mine * inverse
            for c in range(2):
                row = COLS * k + (c * 3 + f) * 4
                start, old = st_ref[c, k, f], it_ref[c, k, f]
                dense_ref[row : row + 4, :] = old - start
                base_ref[c, k, f] = start * keep + mine * old
    for s, ref in enumerate((send0_ref, send1_ref, send2_ref, send3_ref)):

        @pl.when(place == s)
        def _(ref=ref):
            ref[...] = encode(dense_ref[...])


def own_subset(i, s):
    z = (s[0] + i) % 4
    return (0, z % 2, 0, z // 2, 0, 0, 0)


STATE = (2, None, 8, None, 3, 4, DEGREES)


def prepare(ids, quad, st7, it7, damp):
    spec = pl.BlockSpec
    state = spec(STATE, own_subset)
    return pl.pallas_call(
        prepare_kernel,
        grid_spec=pltpu.PrefetchScalarGridSpec(
            num_scalar_prefetch=1,
            grid=(4,),
            in_specs=[
                spec(memory_space=pltpu.SMEM),
                state,
                state,
                spec((3, 32, DEGREES), lambda i, s: (0, 0, 0)),
            ],
            out_specs=[spec((8 * COLS, DEGREES), lambda i, s: (0, 0))] * 4 + [state],
            scratch_shapes=[pltpu.VMEM((8 * COLS, DEGREES), jnp.float32)],
        ),
        out_shape=[jax.ShapeDtypeStruct((8 * COLS, DEGREES), jnp.bfloat16)] * 4
        + [jax.ShapeDtypeStruct(it7.shape, jnp.float32)],
        compiler_params=pltpu.CompilerParams(vmem_limit_bytes=60 * MIB),
        cost_estimate=pl.CostEstimate(
            flops=8 * 32 * COLS * DEGREES, bytes_accessed=6 * MIB, transcendentals=0
        ),
        name="prepare",
    )(ids, quad, st7, it7, damp)


def split(x):
    high = x.astype(jnp.bfloat16)
    return high, (x - high.astype(jnp.float32)).astype(jnp.bfloat16)


def table_kernel(row1_ref, row2_ref, tab_ref, back_ref, keep_ref):
    first = lax.broadcasted_iota(jnp.int32, (1, 128), 1) == 0
    halve = jnp.where(first, 0.5, 1.0)

    def rows(j, _):
        lead_c = row1_ref[0, pl.ds(j, 1), :]
        lead_s = row1_ref[1, pl.ds(j, 1), :]
        cosine = lead_c * row2_ref[0] - lead_s * row2_ref[1]
        sine = lead_s * row2_ref[0] + lead_c * row2_ref[1]
        at = pl.ds(pl.multiple_of(16 * j, 16), 16)
        keep_ref[0, at, :] = cosine
        keep_ref[1, at, :] = sine
        for t, value in enumerate((cosine, sine)):
            high, low = split(value)
            tab_ref[t, 0, at, :] = high
            tab_ref[t, 1, at, :] = low
        return 0

    lax.fori_loop(0, ROWS // 16, rows, 0)
    for t in range(2):
        for block in range(4):
            cut = slice(128 * block, 128 * (block + 1))
            value = jnp.transpose(keep_ref[t, cut, :])
            if t == 1:
                value = -value
            if block == 0:
                value = value * halve
            high, low = split(value)
            back_ref[t, 0, :, cut] = high
            back_ref[t, 1, :, cut] = low


def small_tables():
    scale = 1.0 / math.sqrt(MODES)
    step = 2.0 * math.pi / POINTS
    rows1, rows2 = [], []
    place = np.arange(NBAND)
    block = place % 4 * 8 + place // 4 % 4 * 2 + place // 16
    pairs = (block[:, None] * PAIRS + np.arange(PAIRS)).reshape(-1)
    for par in range(2):
        m = 2 * pairs + par

        def pair(k, factor):
            angle = ((k[:, None] * m[None, :]) % POINTS) * step
            return np.stack([np.cos(angle), np.sin(angle)]) * factor

        rows1.append(pair(16 * np.arange(ROWS // 16), 1.0))
        rows2.append(pair(np.arange(16), scale))
    return [np.stack(x).astype(np.float32) for x in (rows1, rows2)]


def tables(parts):
    spec = pl.BlockSpec
    return pl.pallas_call(
        table_kernel,
        grid=(2,),
        in_specs=[
            spec((None,) + x.shape[1:], lambda i, n=x.ndim: (i,) + (0,) * (n - 1)) for x in parts
        ],
        out_specs=(
            spec((2, 2, ROWS, HALF), lambda i: (i, 0, 0, 0)),
            spec((2, 2, HALF, QUARTER), lambda i: (i, 0, 0, 0)),
        ),
        out_shape=(
            jax.ShapeDtypeStruct((4, 2, ROWS, HALF), jnp.bfloat16),
            jax.ShapeDtypeStruct((4, 2, HALF, QUARTER), jnp.bfloat16),
        ),
        scratch_shapes=[pltpu.VMEM((2, ROWS, HALF), jnp.float32)],
        compiler_params=pltpu.CompilerParams(vmem_limit_bytes=60 * MIB),
        cost_estimate=pl.CostEstimate(
            flops=16 * ROWS * HALF, bytes_accessed=9 * MIB, transcendentals=0
        ),
        name="tables",
    )(*parts)


def grid_kernel(
    got_ref, tab_hbm, back_hbm, rows_ref,
    out_ref,
    tab_ref, back_ref, sems, x_ref, rest_ref, wave_ref, fold_ref, edge_ref,
):
    copies = [
        pltpu.make_async_copy(tab_hbm.at[i], tab_ref.at[i], sems.at[i]) for i in range(4)
    ] + [
        pltpu.make_async_copy(back_hbm.at[i], back_ref.at[i], sems.at[4 + i]) for i in range(4)
    ]
    for copy in copies:
        copy.start()
    index = lax.broadcasted_iota(jnp.int32, (HALF, 1), 0)
    place = index >> 4
    first = ((place & 3) * 8 + (place >> 2 & 3) * 2 + (place >> 4)) * PAIRS + (index & 15)
    for par in range(2):
        ratio = (2 * first + par).astype(jnp.float32) * (1.0 / MODES)
        for c in range(2):
            at = (2 * par + c) * PAIRS
            value = got_ref[:, at : at + PAIRS, :].reshape(HALF, LANES)
            scaled = value.astype(jnp.float32) * (ratio if c == 0 else -ratio)
            high, low = split(scaled)
            x_ref[2 * par + c, :, :LANES] = value
            x_ref[2 * par + 1 - c, :, LANES:] = high
            rest_ref[2 * par + 1 - c] = low
    for i in range(4):
        copies[i].wait()
        wave_ref[i] = mm(tab_ref[i, 0], x_ref[i]) + mm(tab_ref[i, 1], x_ref[i])
        wave_ref[i, :, LANES:] += mm(tab_ref[i, 0], rest_ref[i])
    cor = rows_ref[0:1, :]

    def quads(base, at, lanes):
        ce, se, co, so = (wave_ref[i, at, base + lanes : base + lanes + 128] for i in range(4))
        a, b, s, d = ce + co, ce - co, se + so, se - so
        return a - s, b + d, b - d, a + s

    def tendency(at):
        values = [quads(0, at, 128 * f) for f in range(3)]
        slopes = [quads(LANES, at, 128 * f) for f in range(3)]
        out = [[], [], []]
        for q in range(4):
            u, v, h = (values[f][q] for f in range(3))
            us, vs, hs = (slopes[f][q] for f in range(3))
            out[0].append(cor * v - u * us - hs)
            out[1].append(-u * vs - cor * u)
            out[2].append(-u * hs - (1.0 + h) * us)
        folded = []
        for t1, t2, t3, t4 in out:
            a, b, c, d = t1 + t4, t2 + t3, t1 - t4, t3 - t2
            folded.append((a + b, c + d, a - b, c - d))
        return folded

    def block(j, _):
        at = pl.ds(pl.multiple_of(16 * j, 16), 16)
        for f, folded in enumerate(tendency(at)):
            for i, value in enumerate(folded):
                high, low = split(value)
                fold_ref[i, at, pl.ds(128 * f, 128)] = high
                fold_ref[i, at, pl.ds(LANES + 128 * f, 128)] = low
        return 0

    lax.fori_loop(0, QUARTER // 16, block, 0)
    for f, folded in enumerate(tendency(pl.ds(QUARTER, 16))):
        edge_ref[0, :, pl.ds(128 * f, 128)] = folded[0]
        edge_ref[1, :, pl.ds(128 * f, 128)] = folded[3]

    odd_row = (lax.broadcasted_iota(jnp.int32, (HALF, 1), 0) & 1) == 1
    half_scale = 0.5 / math.sqrt(MODES)
    sign = jnp.where(odd_row, -half_scale, half_scale)
    weight, signed = rows_ref[1:2, :], rows_ref[2:3, :]
    for par in range(2):
        both = []
        for c in range(2):
            i = 2 * par + c
            copies[4 + i].wait()
            both_parts = mm(back_ref[i, 0], fold_ref[i])
            out = both_parts[:, :LANES] + both_parts[:, LANES:]
            out = out + mm(back_ref[i, 1], fold_ref[i, :, :LANES])
            if i == 0:
                out = out + sign * edge_ref[0, 0:1, :]
            if i == 3:
                out = out - sign * edge_ref[1, 0:1, :]
            both.append(out)
        for f in range(3):
            parts = []
            for out in both:
                part = out[:, 128 * f : 128 * (f + 1)]
                part = pltpu.roll(part, 64, 1) * weight + part * signed
                parts.append(part.reshape(NBAND, 2, 8, 128))
            joined = jnp.concatenate(parts, axis=2).astype(jnp.bfloat16)
            for h in range(2):
                out_ref[:, 2 * par + h, :, 128 * f : 128 * (f + 1)] = joined[:, h]


def grid_stage(got, tab, back, rows):
    return pl.pallas_call(
        grid_kernel,
        in_specs=[
            pl.BlockSpec(memory_space=pltpu.VMEM),
            pl.BlockSpec(memory_space=pl.ANY),
            pl.BlockSpec(memory_space=pl.ANY),
            pl.BlockSpec(memory_space=pltpu.VMEM),
        ],
        out_shape=jax.ShapeDtypeStruct((NBAND, 4, 16, LANES), jnp.bfloat16),
        scratch_shapes=[
            pltpu.VMEM((4, 2, ROWS, HALF), jnp.bfloat16),
            pltpu.VMEM((4, 2, HALF, QUARTER), jnp.bfloat16),
            pltpu.SemaphoreType.DMA((8,)),
            pltpu.VMEM((4, HALF, 2 * LANES), jnp.bfloat16),
            pltpu.VMEM((4, HALF, LANES), jnp.bfloat16),
            pltpu.VMEM((4, ROWS, 2 * LANES), jnp.float32),
            pltpu.VMEM((4, QUARTER, 2 * LANES), jnp.bfloat16),
            pltpu.VMEM((2, 16, LANES), jnp.float32),
        ],
        compiler_params=pltpu.CompilerParams(vmem_limit_bytes=48 * MIB),
        cost_estimate=pl.CostEstimate(
            flops=2 * 28 * ROWS * HALF * LANES, bytes_accessed=17 * MIB, transcendentals=0
        ),
        name="grid",
    )(got, tab, back, rows)


def analysis_kernel(
    id_ref, quad_ref, y_ref, leg_ref, move0_ref, move1_ref, move2_ref, move3_ref, st_ref, damp_ref,
    out0_ref, out1_ref, out2_ref, out3_ref, sums_ref,
    wide_ref, rate_ref, start_ref, mix_ref, acc_ref,
):
    step = pl.program_id(0)
    node = id_ref[0]
    order = [(node + 4 - s) % 4 for s in range(4)]

    @pl.when(step == 0)
    def _():
        acc_ref[...] = jnp.zeros_like(acc_ref)
        low = lax.broadcasted_iota(jnp.int32, (16, 128), 1) < 64
        for s in range(4):
            for f in range(3):
                for e in range(4):
                    for t in range(4):
                        first, second = (
                            y_ref[
                                (8 * e + 2 * t + g) * 4 + order[s], :, 128 * f : 128 * (f + 1)
                            ].astype(jnp.float32)
                            for g in range(2)
                        )
                        symmetric = jnp.where(low, first, second)
                        antisymmetric = jnp.where(low, second, first)
                        for c in range(2):
                            row = (((s * 2 + c) * 3 + f) * 4 + e) * 8
                            wide_ref[0, t, row : row + 8, :] = symmetric[8 * c : 8 * c + 8]
                            wide_ref[1, t, row : row + 8, :] = antisymmetric[8 * c : 8 * c + 8]

    for k in range(MB):
        at = step * MB + k
        mode = 2 * (8 * (node % 2) + at) + node // 2
        for c in range(2):
            for f in range(3):
                row = (c * 3 + f) * 4
                rate_ref[pl.ds(row, 4), :] = jnp.broadcast_to(
                    damp_ref[f, pl.ds(mode, 1), :], (4, DEGREES)
                )
                start_ref[pl.ds(row, 4), :] = st_ref[c, k, f]
        halves = []
        for h in range(2):
            spec = jnp.concatenate(
                [wide_ref[h, t, pl.ds(at, 4 * COLS, stride=8), :] for t in range(4)], axis=1
            ).astype(jnp.bfloat16)
            if h == 0:
                table = leg_ref[k, :, :256]
            else:
                blocks = [leg_ref[k, 64 * (b ^ 1) : 64 * (b ^ 1) + 64, 256:] for b in range(8)]
                table = jnp.concatenate(blocks, axis=0)
            halves.append(mm(spec, table))
        for h in range(2):
            cut = slice(256 * h, 256 * (h + 1))
            rate, start = rate_ref[:, cut], start_ref[:, cut]
            moves = [
                decode(ref[k // 2, COLS * (k % 2) : COLS * (k % 2 + 1), cut])
                for ref in (move0_ref, move1_ref, move2_ref, move3_ref)
            ]
            forces = [
                halves[h][COLS * p : COLS * (p + 1)] - rate * moves[p] for p in range(4)
            ]
            change = jnp.zeros_like(start)
            for q in range(4):
                row = [quad_ref[order[q], order[p]] for p in range(4)]
                mine = row[q] * rate
                inverse = 1.0 / (1.0 + mine)
                mixed = (
                    row[0] * forces[0] + row[1] * forces[1] + row[2] * forces[2] + row[3] * forces[3]
                ) * inverse
                total = row[0] + row[1] + row[2] + row[3]
                old = start + moves[q]
                moved = mixed + (start * (1.0 - rate * total) + mine * old) * inverse - old
                change = change + moved * moved
                mix_ref[q, COLS * k : COLS * (k + 1), cut] = mixed
            acc_ref[0, :, cut] += change
            acc_ref[1, :, cut] += start * start
    for s, ref in enumerate((out0_ref, out1_ref, out2_ref, out3_ref)):
        ref[...] = encode(mix_ref[s])

    @pl.when(step == pl.num_programs(0) - 1)
    def _():
        field = lax.broadcasted_iota(jnp.int32, (COLS, 1), 0) // 4 % 3
        lane = lax.broadcasted_iota(jnp.int32, (1, 128), 1)
        sums = jnp.zeros((1, 128), jnp.float32)
        for s in range(2):
            per_row = jnp.sum(acc_ref[s], axis=1, keepdims=True)
            for f in range(3):
                value = jnp.sum(jnp.where(field == f, per_row, 0.0), axis=0, keepdims=True)
                sums = sums + jnp.where(lane == 3 * s + f, value, 0.0)
        sums_ref[...] = jnp.broadcast_to(sums[None], sums_ref.shape)


def analysis(ids, quad, y, leg4, moves, st6, damp):
    spec = pl.BlockSpec
    return pl.pallas_call(
        analysis_kernel,
        grid_spec=pltpu.PrefetchScalarGridSpec(
            num_scalar_prefetch=1,
            grid=(2,),
            in_specs=[
                spec(memory_space=pltpu.SMEM),
                spec((4 * NBAND, 16, LANES), lambda i, s: (0, 0, 0)),
                spec(
                    (MB, None, LATS, DEGREES), lambda i, s: (s[0] % 2 * 2 + i, s[0] // 2, 0, 0)
                ),
                *[spec((2, 2 * COLS, DEGREES), lambda i, s: (i, 0, 0))] * 4,
                spec(
                    (2, MB, None, 3, 4, DEGREES),
                    lambda i, s: (0, s[0] % 2 * 2 + i, s[0] // 2, 0, 0, 0),
                ),
                spec((3, 32, DEGREES), lambda i, s: (0, 0, 0)),
            ],
            out_specs=(
                *[spec((MB * COLS, DEGREES), lambda i, s: (i, 0))] * 4,
                spec((NBAND // 2, 8, 128), lambda i, s: (0, 0, 0)),
            ),
            scratch_shapes=[
                pltpu.VMEM((2, 4, (4 * COLS + 1) * 8, 128), jnp.float32),
                pltpu.VMEM((COLS, DEGREES), jnp.float32),
                pltpu.VMEM((COLS, DEGREES), jnp.float32),
                pltpu.VMEM((4, MB * COLS, DEGREES), jnp.float32),
                pltpu.VMEM((2, COLS, DEGREES), jnp.float32),
            ],
        ),
        out_shape=(
            *[jax.ShapeDtypeStruct((8 * COLS, DEGREES), jnp.bfloat16)] * 4,
            jax.ShapeDtypeStruct((NBAND // 2, 8, 128), jnp.float32),
        ),
        compiler_params=pltpu.CompilerParams(vmem_limit_bytes=46 * MIB),
        cost_estimate=pl.CostEstimate(
            flops=2 * 32 * COLS * LATS * DEGREES, bytes_accessed=10 * MIB, transcendentals=0
        ),
        name="analysis",
    )(ids, quad, y, leg4, *moves, st6, damp)


def update_kernel(
    id_ref, mixed0_ref, mixed1_ref, mixed2_ref, mixed3_ref, base_ref, out_ref, mix_ref
):
    place = pl.program_id(0)
    for s, ref in enumerate((mixed0_ref, mixed1_ref, mixed2_ref, mixed3_ref)):

        @pl.when(place == s)
        def _(ref=ref):
            mix_ref[...] = decode(ref[...])

    for k in range(8):
        for c in range(2):
            for f in range(3):
                row = COLS * k + (c * 3 + f) * 4
                out_ref[c, k, f] = base_ref[c, k, f] + mix_ref[row : row + 4, :]


def update(ids, mixed, base):
    spec = pl.BlockSpec
    state = spec(STATE, own_subset)
    return pl.pallas_call(
        update_kernel,
        grid_spec=pltpu.PrefetchScalarGridSpec(
            num_scalar_prefetch=1,
            grid=(4,),
            in_specs=[*[spec((8 * COLS, DEGREES), lambda i, s: (0, 0))] * 4, state],
            out_specs=state,
            scratch_shapes=[pltpu.VMEM((8 * COLS, DEGREES), jnp.float32)],
        ),
        out_shape=jax.ShapeDtypeStruct(base.shape, jnp.float32),
        compiler_params=pltpu.CompilerParams(vmem_limit_bytes=32 * MIB),
        cost_estimate=pl.CostEstimate(
            flops=4 * 32 * COLS * DEGREES, bytes_accessed=5 * MIB, transcendentals=0
        ),
        name="update",
    )(ids, *mixed, base)


def exchange(x, axes):
    return lax.all_to_all(x, axes, split_axis=0, concat_axis=0, tiled=True)


def shift(x, axis, by):
    return lax.ppermute(x, axis, [(i, (i + by) % 4) for i in range(4)])


def latitude_rows(place, coriolis, lat_weight):
    count = LATS // 8
    group = place % 8
    cor = lax.dynamic_slice_in_dim(coriolis, group * count, count, 1)
    weight = lax.dynamic_slice_in_dim(lat_weight, group * count, count, 0)
    swapped = group % 2 == 1
    cor = jnp.where(swapped, cor[::-1], cor).reshape(1, 128)
    weight = jnp.concatenate([weight, weight])[None]
    south = lax.broadcasted_iota(jnp.int32, (1, 128), 1) >= count
    signed = jnp.where(south != swapped, -weight, weight)
    return jnp.concatenate([cor, weight, signed], axis=0)


def body(state0, iterate, legendre, lat_weight, coriolis, damping, quadrature):
    node = lax.axis_index("node")
    place = lax.axis_index(SEND)
    spec = iterate[0].transpose(0, 1, 3, 2, 4)
    base = state0.transpose(0, 1, 3, 2, 4)
    it6 = spec.reshape(2, PAIRS, 2, 3, 4, DEGREES)
    st6 = base.reshape(2, PAIRS, 2, 3, 4, DEGREES)
    leg4 = legendre.reshape(PAIRS, 2, LATS, DEGREES)
    damp = damping.transpose(1, 0, 2)
    ids = jnp.reshape(node, (1,)).astype(jnp.int32)

    shape7 = (2, 2, 8, 2, 3, 4, DEGREES)
    sent = synthesis(it6, leg4)
    got = exchange(sent, SEND)
    parts = [jnp.asarray(x) for x in small_tables()]
    late, _ = lax.optimization_barrier(((parts, quadrature), sent))
    parts, quad = late
    *moves, settled = prepare(ids, quad, base.reshape(shape7), spec.reshape(shape7), damp)
    moves = [moves[0]] + [shift(moves[s], "node", s) for s in (1, 2, 3)]
    tab, back = tables(parts)
    rows = latitude_rows(place, coriolis, lat_weight)
    rows, moves = lax.optimization_barrier((rows, moves))
    moves = [x.reshape(4, 2 * COLS, DEGREES) for x in moves]
    columns = grid_stage(got, tab, back, rows)
    spectra = exchange(columns.reshape(4 * NBAND, 16, LANES), SEND_NODE)
    *mixed, sums = analysis(ids, quadrature, spectra, leg4, moves, st6, damp)
    mixed = [mixed[0]] + [shift(mixed[s], "node", -s) for s in (1, 2, 3)]
    sums = exchange(sums.reshape(4 * NBAND, 1, 128), SEND_NODE)
    out = update(ids, mixed, settled)
    sums, out = lax.optimization_barrier((sums, out))
    total = jnp.sum(sums, axis=(0, 1))
    ratio = jnp.sqrt(total[:3] / (4.0 * total[3:6] + 1e-06))
    out = out.reshape(2, 32, 3, 4, DEGREES).transpose(0, 1, 3, 2, 4)
    return (out[None], ratio)


def solution(mesh):
    torus = Mesh(
        mesh.devices.reshape(mesh.shape["node"], 4, 4, 2), ("node", "band_0", "band_1", "band_2")
    )
    return jax.shard_map(
        body,
        mesh=torus,
        in_specs=(
            P(None, BAND, None, None, None),
            P("node", None, BAND, None, None, None),
            P(BAND, None, None),
            P(),
            P(),
            P(BAND, None, None),
            P(),
        ),
        out_specs=(P("node", None, BAND, None, None, None), P()),
        check_vma=False,
    )
```
